512 devices in a mesh: mask: 4 (over z_hi), rows: 128 (over z_lo, x, y, core).
Axes of the slice: x: 4, y: 8, z: 8 (z_hi: 4, z_lo: 2; z = z_hi * 2 + z_lo), core: 2. Of those that a mesh axis runs over, the one named last changes fastest.
Arguments:
- object_field: float32 [2, 4096, 4096], P(None, 'rows'), may hold values from -6 to 6
- phases: int32 [4, 4096, 4096], P('mask', 'rows'), may hold values from 0 to 3
- intensity: float32 [4, 4096, 4096], P('mask', 'rows'), may hold values from 0.5 to 4
Outputs:
- updated: float32 [2, 4096, 4096], P(None, 'rows')
- gradient: float32 [2, 4096, 4096], P(None, 'rows')
The draws below stay inside these ranges and needn't reach their ends.
Inputs may be any that keep to these rules, and one draw needn't show every extreme that they name: `phases`: index k stands for the mask entry i^k.
All inputs are finite; a program needn't handle non-finite values.
Results may differ from the reference program's by a relative error of at most 0.00011.
Values sent between devices are 32-bit elements; how exact they have to be, the bound alone decides.
No kernel may reach another device: no remote copies, remote signals or barrier semaphores. Data moves between devices by JAX's collectives and lax.ppermute only.
A program may use at most 64 MiB of HBM per device.

```python
import math
import jax
import jax.numpy as jnp
from jax import lax

N = 4096
L = 4


def set_ends(entries, stream_key, least, largest):
    longest = entries.shape.index(max(entries.shape))
    spots = []
    for shift in (0, 1):
        where = [jax.random.randint(jax.random.fold_in(stream_key, axis), (), 0, length) for axis, length in enumerate(entries.shape)]
        where[longest] = (where[longest] + shift) % entries.shape[longest]
        spots.append(tuple(where))
    return entries.at[spots[0]].set(least).at[spots[1]].set(largest)


def levels(key, extent, pieces, smallest, largest):
    loudness = 1.0
    for dim, shards_of in pieces:
        heights = jax.random.uniform(jax.random.fold_in(jax.random.fold_in(key, 6), dim), (shards_of,), jnp.float32, smallest / len(pieces), largest / len(pieces))
        loudness = loudness * jnp.repeat(jnp.exp(heights), extent[dim] // shards_of).reshape((-1,) + (1,) * (len(extent) - 1 - dim))
    return loudness


def gaussian(own_key, extent, spread, bound, shards=(), kind=jnp.bfloat16):
    values = spread * jax.random.normal(own_key, extent, jnp.float32)
    if shards:
        values = values * levels(own_key, extent, shards, -0.22, 0.18)
    return jnp.clip(values, -bound, bound).astype(kind)


def setup_inputs(seed: int = 0) -> dict:
    keys = jax.random.split(jax.random.key(seed), 4)
    return {
        "object_field": gaussian(keys[0], (2, N, N), 1.0, 6.0, ((1, 128),), jnp.float32),
        "phases": set_ends(jax.random.randint(keys[1], (L, N, N), 0, 4), jax.random.fold_in(keys[1], 1), 0, 3).astype(jnp.int32),
        "intensity": jnp.clip(jnp.exp(math.log(4.0) - 2.0794415 * jax.random.uniform(keys[2], (L, N, N), jnp.float32) ** levels(keys[2], (L, N, N), ((0, 4), (1, 128)), -0.2, 0.2)), 0.5, 4.0),
    }


def reference(object_field, phases, intensity):
    zc = lax.complex(object_field[0], object_field[1])
    grad = jnp.zeros_like(zc)
    for index in range(L):
        code = phases[index]
        d_real = (jnp.where(code == 0, 1.0, 0.0) - jnp.where(code == 2, 1.0, 0.0)).astype(object_field.dtype)
        d_imag = (jnp.where(code == 1, 1.0, 0.0) - jnp.where(code == 3, 1.0, 0.0)).astype(object_field.dtype)
        mask_val = lax.complex(d_real, d_imag)
        wave = jnp.fft.fft2(mask_val * zc, norm="ortho")
        weight = jnp.abs(wave) ** 2 - intensity[index].T
        back = jnp.fft.ifft2(weight * wave, norm="ortho")
        grad = grad + jnp.conj(mask_val) * back
    direction = (1.0 / L) * grad
    updated = zc - 0.2 * direction
    updated_out = jnp.stack([jnp.real(updated), jnp.imag(updated)]).astype(object_field.dtype)
    gradient_out = jnp.stack([jnp.real(direction), jnp.imag(direction)]).astype(object_field.dtype)
    return (updated_out, gradient_out)
```

```python
import functools
import math

import jax
import jax.numpy as jnp
import ml_dtypes
import numpy as np
from jax import lax
from jax.experimental import pallas as pl
from jax.experimental.pallas import tpu as pltpu
from jax.sharding import PartitionSpec as P

N = 4096
LANES = 128
SHORT = 32
OCT = 8
MASKS = 4
step_size = 0.2


def _split(table):
    high = table.astype(np.float32).astype(ml_dtypes.bfloat16)
    low = (table - high.astype(np.float64)).astype(np.float32).astype(ml_dtypes.bfloat16)
    return high, low


@functools.lru_cache(maxsize=None)
def tables():
    i128 = np.arange(LANES)
    w = np.exp(-2j * math.pi * (np.outer(i128, i128) % LANES) / LANES) / 64.0
    left = np.block([[w.real, -w.imag], [w.imag, w.real]])
    t = np.exp(-2j * math.pi * np.outer(np.arange(SHORT), i128) / N)
    t = np.broadcast_to(t[:, None, :], (SHORT, OCT, LANES))
    row_tw = np.stack([t.real, t.imag]).astype(np.float32)
    rho = i128 % OCT
    row = np.arange(MASKS)[:, None] * OCT + rho[None, :]
    t = np.exp(-2j * math.pi * (i128[None, :, None] * row[:, None, :]) / N)
    col_tw = np.stack([t.real, t.imag]).astype(np.float32)
    blocks = []
    for e in range(4):
        r8 = np.arange(OCT)
        small = np.exp(-2j * math.pi * np.outer(r8, r8) / 8 - 2j * math.pi * r8[:, None] * e / 32)
        big = np.kron(np.eye(16), small)
        blocks.append(np.block([[big.real, big.imag], [-big.imag, big.real]]))
    lh, ll = _split(left)
    ih, il = _split(left.T)
    mh, ml = _split(np.stack(blocks))
    return dict(lh=lh, ll=ll, ih=ih, il=il, mh=mh, ml=ml, row_tw=row_tw, col_tw=col_tw)


def split(x):
    high = x.astype(jnp.bfloat16)
    return high, (x - high.astype(jnp.float32)).astype(jnp.bfloat16)


def dot3(a, b, dims):
    dot = functools.partial(
        lax.dot_general, dimension_numbers=(dims, ((), ())), preferred_element_type=jnp.float32
    )
    return dot(a[0], b[0]) + (dot(a[0], b[1]) + dot(a[1], b[0]))


NN = ((1,), (0,))
NT = ((1,), (1,))


def cmul(a, b):
    return a[0] * b[0] - a[1] * b[1], a[0] * b[1] + a[1] * b[0]


def cadd(a, b):
    return a[0] + b[0], a[1] + b[1]


def csub(a, b):
    return a[0] - b[0], a[1] - b[1]


def times_i(a, sign):
    return (-a[1], a[0]) if sign > 0 else (a[1], -a[0])


def rotate(a, turns, length, sign):
    turns = turns % length
    if turns == 0:
        return a
    eighths = turns * 8 % (length * 8) / length
    if eighths == 4:
        return -a[0], -a[1]
    if eighths == 2:
        return times_i(a, sign)
    if eighths == 6:
        return times_i(a, -sign)
    angle = sign * 2 * math.pi * turns / length
    c, s = float(np.float32(math.cos(angle))), float(np.float32(math.sin(angle)))
    if eighths in (1, 3, 5, 7):
        h = float(np.float32(math.sqrt(0.5)))
        cs, ss = (1 if c > 0 else -1), (1 if s > 0 else -1)
        re = (a[0] if cs > 0 else -a[0]) - (a[1] if ss > 0 else -a[1])
        im = (a[1] if cs > 0 else -a[1]) + (a[0] if ss > 0 else -a[0])
        return re * h, im * h
    return a[0] * c - a[1] * s, a[0] * s + a[1] * c


def fft4(x, sign):
    a, b = cadd(x[0], x[2]), csub(x[0], x[2])
    c, d = cadd(x[1], x[3]), times_i(csub(x[1], x[3]), sign)
    return [cadd(a, c), cadd(b, d), csub(a, c), csub(b, d)]


def fft8(x, sign):
    even, odd = fft4(x[0::2], sign), fft4(x[1::2], sign)
    odd = [rotate(o, j, 8, sign) for j, o in enumerate(odd)]
    return [cadd(u, v) for u, v in zip(even, odd)] + [csub(u, v) for u, v in zip(even, odd)]


def fft32(load, store, mid, sign):
    for p0 in range(8):
        y = fft4([load(8 * p1 + p0) for p1 in range(4)], sign)
        for k0 in range(4):
            v = rotate(y[k0], p0 * k0, 32, sign)
            mid[0, k0 * 8 + p0] = v[0]
            mid[1, k0 * 8 + p0] = v[1]
    for k0 in range(4):
        y = fft8([(mid[0, k0 * 8 + p0], mid[1, k0 * 8 + p0]) for p0 in range(8)], sign)
        for k1 in range(8):
            store(k0 + 4 * k1, y[k1])


def code_times(code, z):
    odd = (code & 1) == 1
    a = jnp.where(odd, z[1], z[0])
    b = jnp.where(odd, z[0], z[1])
    return jnp.where((code == 1) | (code == 2), -a, a), jnp.where(code >= 2, -b, b)


def conj_code_times(code, z):
    odd = (code & 1) == 1
    a = jnp.where(odd, z[1], z[0])
    b = jnp.where(odd, z[0], z[1])
    return jnp.where(code >= 2, -a, a), jnp.where((code == 1) | (code == 2), -b, b)


def rows_forward(obj, code, lh, ll, tw, out, mid, xs):
    for m in range(MASKS):
        rows = slice(OCT * m, OCT * m + OCT)

        def load(p):
            cols = slice(LANES * p, LANES * p + LANES)
            return code_times(code[0, rows, cols], (obj[0, rows, cols], obj[1, rows, cols]))

        def store(k, v):
            v = cmul(v, (tw[0, k], tw[1, k]))
            xs[OCT * k : OCT * k + OCT, :LANES] = v[0]
            xs[OCT * k : OCT * k + OCT, LANES:] = v[1]

        fft32(load, store, mid, -1)
        y = dot3((lh[...], ll[...]), split(xs[...]), NT)
        for ri in range(2):
            for h in range(2):
                out[pl.ds(ri * 8 + 2 * m + h, LANES, stride=16), :] = y[
                    LANES * ri : LANES * ri + LANES, LANES * h : LANES * h + LANES
                ]


def columns(rec, inten, lh, ll, ih, il, mh, ml, tw, out, s):
    for m in range(MASKS):
        x = jnp.concatenate(
            [
                jnp.concatenate(
                    [rec[pl.ds(ri * 8 + 2 * m + h, LANES, stride=16), :] for h in range(2)], axis=1
                )
                for ri in range(2)
            ],
            axis=0,
        )
        y = dot3((lh[...], ll[...]), split(x), NN)
        t = (tw[0, m], tw[1, m])
        for h in range(2):
            cols = slice(LANES * h, LANES * h + LANES)
            v = cmul((y[:LANES, cols], y[LANES:, cols]), t)
            s[m, 0, h] = v[0]
            s[m, 1, h] = v[1]

    for h in range(2):
        def turn(i, _):
            rows = pl.ds(pl.multiple_of(i * OCT, OCT), OCT)
            y = fft4([(s[m, 0, h, rows, :], s[m, 1, h, rows, :]) for m in range(4)], -1)
            for e in range(4):
                s[e, 0, h, rows, :] = y[e][0]
                s[e, 1, h, rows, :] = y[e][1]
            return 0

        lax.fori_loop(0, LANES // OCT, turn, 0, unroll=True)

    for e in range(4):
        x = jnp.concatenate(
            [jnp.concatenate([s[e, 0, h], s[e, 1, h]], axis=1) for h in range(2)], axis=0
        )
        table = (mh[e], ml[e])
        y = dot3(split(x), table, NN)
        wr, wi = y[:, :LANES], y[:, LANES:]
        weight = wr * wr + wi * wi - inten[e]
        v = jnp.concatenate([wr * weight, wi * weight], axis=1)
        y = dot3(split(v), table, NT)
        for h in range(2):
            rows = slice(LANES * h, LANES * h + LANES)
            s[e, 0, h] = y[rows, :LANES]
            s[e, 1, h] = y[rows, LANES:]

    for h in range(2):
        def turn_back(i, _):
            rows = pl.ds(pl.multiple_of(i * OCT, OCT), OCT)
            y = fft4([(s[e, 0, h, rows, :], s[e, 1, h, rows, :]) for e in range(4)], 1)
            for m in range(4):
                v = cmul(y[m], (tw[0, m, rows, :], -tw[1, m, rows, :]))
                s[m, 0, h, rows, :] = v[0]
                s[m, 1, h, rows, :] = v[1]
            return 0

        lax.fori_loop(0, LANES // OCT, turn_back, 0, unroll=True)

    for m in range(MASKS):
        x = jnp.concatenate(
            [jnp.concatenate([s[m, ri, 0], s[m, ri, 1]], axis=1) for ri in range(2)], axis=0
        )
        y = dot3((ih[...], il[...]), split(x), NN)
        for ri in range(2):
            for h in range(2):
                out[pl.ds(m * 512 + ri * 2 + h, LANES, stride=4), :] = y[
                    LANES * ri : LANES * ri + LANES, LANES * h : LANES * h + LANES
                ]


def rows_back(rec, code, lh, ll, tw, out, mid, ys):
    for l in range(MASKS):
        x = jnp.concatenate(
            [
                jnp.concatenate(
                    [
                        rec[pl.ds(l * 512 + ri * 2 + h, LANES, stride=4), :].T
                        for ri in range(2)
                    ],
                    axis=1,
                )
                for h in range(2)
            ],
            axis=0,
        )
        ys[...] = dot3(split(x), (lh[...], ll[...]), NN)

        def load(k):
            rows = slice(OCT * k, OCT * k + OCT)
            return cmul((ys[rows, :LANES], ys[rows, LANES:]), (tw[0, k], -tw[1, k]))

        def store(p, v):
            cols = slice(LANES * p, LANES * p + LANES)
            v = conj_code_times(code[l, :, cols], v)
            for ri in range(2):
                if l == 0:
                    out[ri, :, cols] = v[ri]
                elif l < MASKS - 1:
                    out[ri, :, cols] += v[ri]
                else:
                    out[ri, :, cols] = (out[ri, :, cols] + v[ri]) * (1.0 / MASKS)

        fft32(load, store, mid, 1)


def finish(index, own, before, after, far_re, far_im, obj, updated, direction):
    me = index[0]

    def put(shift, ri, value):
        rows = pl.ds(pl.multiple_of(lax.rem(me + shift, MASKS) * OCT, OCT), OCT)
        direction[ri, rows, :] = value
        updated[ri, rows, :] = obj[ri, rows, :] - step_size * value

    for ri in range(2):
        put(0, ri, own[ri])
        put(3, ri, before[ri])
        put(1, ri, after[ri])
    put(2, 0, far_re[0])
    put(2, 1, far_im[0])


VM = pl.BlockSpec(memory_space=pltpu.VMEM)
F32 = jnp.float32


def call(kernel, name, out_shape, n_in, scratch, flops, vmem=24, smem_first=False):
    specs = [VM] * n_in
    if smem_first:
        specs[0] = pl.BlockSpec(memory_space=pltpu.SMEM)
    outs = jax.tree.map(lambda _: VM, out_shape)
    return pl.pallas_call(
        kernel,
        name=name,
        out_shape=out_shape,
        in_specs=specs,
        out_specs=outs,
        scratch_shapes=scratch,
        compiler_params=pltpu.CompilerParams(vmem_limit_bytes=vmem << 20),
        cost_estimate=pl.CostEstimate(flops=flops, bytes_accessed=3 << 20, transcendentals=0),
    )


def body(object_field, phases, intensity):
    t = {k: jnp.asarray(v) for k, v in tables().items()}
    sds = jax.ShapeDtypeStruct
    codes = lax.all_to_all(phases.reshape(MASKS, OCT, N), "mask", 0, 0, tiled=True)
    sent = call(
        rows_forward, "rows_forward", sds((2048, LANES), F32), 5,
        [pltpu.VMEM((2, SHORT, OCT, LANES), F32), pltpu.VMEM((256, 256), F32)], 1 << 29,
    )(object_field, phases, t["lh"], t["ll"], t["row_tw"])
    inten = intensity.reshape(2, 16, 8, 4, LANES).transpose(3, 0, 4, 1, 2).reshape(4, 256, LANES)
    rec = lax.all_to_all(sent.reshape(LANES, 16, LANES), "rows", 0, 0, tiled=True)
    back = call(
        columns, "columns", sds((2048, LANES), F32), 9,
        [pltpu.VMEM((4, 2, 2, LANES, LANES), F32)], 3 << 29,
    )(rec.reshape(2048, LANES), inten, t["lh"], t["ll"], t["ih"], t["il"], t["mh"], t["ml"], t["col_tw"])
    rec = lax.all_to_all(back.reshape(512, 4, LANES), ("mask", "rows"), 0, 0, tiled=True)
    part = call(
        rows_back, "rows_back", sds((2, OCT, N), F32), 5,
        [pltpu.VMEM((2, SHORT, OCT, LANES), F32), pltpu.VMEM((256, 256), F32)], 1 << 29,
    )(rec.reshape(2048, LANES), codes, t["lh"], t["ll"], t["row_tw"])
    up = [(i, (i + 1) % MASKS) for i in range(MASKS)]
    down = [((i + 1) % MASKS, i) for i in range(MASKS)]
    before = lax.ppermute(part, "mask", up)
    after = lax.ppermute(part, "mask", down)
    far_re = lax.ppermute(before[:1], "mask", up)
    far_im = lax.ppermute(after[1:], "mask", down)
    index = lax.axis_index("mask").astype(jnp.int32).reshape(1)
    whole = sds((2, SHORT, N), F32)
    return call(finish, "finish", (whole, whole), 7, [], 1 << 20, smem_first=True)(
        index, part, before, after, far_re, far_im, object_field
    )


def solution(mesh):
    return jax.shard_map(
        body,
        mesh=mesh,
        in_specs=(P(None, "rows", None), P("mask", "rows", None), P("mask", "rows", None)),
        out_specs=(P(None, "rows", None), P(None, "rows", None)),
        check_vma=False,
    )
```

```python
import functools
import math

import jax
import jax.numpy as jnp
import ml_dtypes
import numpy as np
from jax import lax
from jax.experimental import pallas as pl
from jax.experimental.pallas import tpu as pltpu
from jax.sharding import PartitionSpec as P

N = 4096
LANES = 128
SHORT = 32
OCT = 8
MASKS = 4
step_size = 0.2


def _split(table):
    high = table.astype(np.float32).astype(ml_dtypes.bfloat16)
    low = (table - high.astype(np.float64)).astype(np.float32).astype(ml_dtypes.bfloat16)
    return high, low


@functools.lru_cache(maxsize=None)
def tables():
    i128 = np.arange(LANES)
    w = np.exp(-2j * math.pi * (np.outer(i128, i128) % LANES) / LANES) / 64.0
    left = np.block([[w.real, -w.imag], [w.imag, w.real]])
    t = np.exp(-2j * math.pi * np.outer(np.arange(SHORT), i128) / N)
    row_tw = np.stack([t.real, t.imag]).astype(np.float32)
    rho = i128 % OCT
    row = np.arange(MASKS)[:, None] * OCT + rho[None, :]
    t = np.exp(-2j * math.pi * (i128[None, :, None] * row[:, None, :]) / N)
    col_tw = np.stack([t.real, t.imag]).astype(np.float32)
    blocks = []
    for e in range(4):
        r8 = np.arange(OCT)
        small = np.exp(-2j * math.pi * np.outer(r8, r8) / 8 - 2j * math.pi * r8[:, None] * e / 32)
        big = np.kron(np.eye(16), small)
        blocks.append(np.block([[big.real, big.imag], [-big.imag, big.real]]))
    lh, ll = _split(left)
    ih, il = _split(left.T)
    mh, ml = _split(np.stack(blocks))
    return dict(lh=lh, ll=ll, ih=ih, il=il, mh=mh, ml=ml, row_tw=row_tw, col_tw=col_tw)


def split(x):
    high = x.astype(jnp.bfloat16)
    return high, (x - high.astype(jnp.float32)).astype(jnp.bfloat16)


def dot3(a, b, dims):
    dot = functools.partial(
        lax.dot_general, dimension_numbers=(dims, ((), ())), preferred_element_type=jnp.float32
    )
    return dot(a[0], b[0]) + (dot(a[0], b[1]) + dot(a[1], b[0]))


NN = ((1,), (0,))
NT = ((1,), (1,))


def cmul(a, b):
    return a[0] * b[0] - a[1] * b[1], a[0] * b[1] + a[1] * b[0]


def cadd(a, b):
    return a[0] + b[0], a[1] + b[1]


def csub(a, b):
    return a[0] - b[0], a[1] - b[1]


def times_i(a, sign):
    return (-a[1], a[0]) if sign > 0 else (a[1], -a[0])


def rotate(a, turns, length, sign):
    turns = turns % length
    if turns == 0:
        return a
    eighths = turns * 8 % (length * 8) / length
    if eighths == 4:
        return -a[0], -a[1]
    if eighths == 2:
        return times_i(a, sign)
    if eighths == 6:
        return times_i(a, -sign)
    angle = sign * 2 * math.pi * turns / length
    c, s = float(np.float32(math.cos(angle))), float(np.float32(math.sin(angle)))
    if eighths in (1, 3, 5, 7):
        h = float(np.float32(math.sqrt(0.5)))
        cs, ss = (1 if c > 0 else -1), (1 if s > 0 else -1)
        re = (a[0] if cs > 0 else -a[0]) - (a[1] if ss > 0 else -a[1])
        im = (a[1] if cs > 0 else -a[1]) + (a[0] if ss > 0 else -a[0])
        return re * h, im * h
    return a[0] * c - a[1] * s, a[0] * s + a[1] * c


def fft4(x, sign):
    a, b = cadd(x[0], x[2]), csub(x[0], x[2])
    c, d = cadd(x[1], x[3]), times_i(csub(x[1], x[3]), sign)
    return [cadd(a, c), cadd(b, d), csub(a, c), csub(b, d)]


def fft8(x, sign):
    even, odd = fft4(x[0::2], sign), fft4(x[1::2], sign)
    odd = [rotate(o, j, 8, sign) for j, o in enumerate(odd)]
    return [cadd(u, v) for u, v in zip(even, odd)] + [csub(u, v) for u, v in zip(even, odd)]


def fft32(load, store, mid, sign):
    for p0 in range(8):
        y = fft4([load(8 * p1 + p0) for p1 in range(4)], sign)
        for k0 in range(4):
            v = rotate(y[k0], p0 * k0, 32, sign)
            mid[0, k0 * 8 + p0] = v[0]
            mid[1, k0 * 8 + p0] = v[1]
    for k0 in range(4):
        y = fft8([(mid[0, k0 * 8 + p0], mid[1, k0 * 8 + p0]) for p0 in range(8)], sign)
        for k1 in range(8):
            store(k0 + 4 * k1, y[k1])


def code_times(code, z):
    odd = (code & 1) == 1
    a = jnp.where(odd, z[1], z[0])
    b = jnp.where(odd, z[0], z[1])
    return jnp.where((code == 1) | (code == 2), -a, a), jnp.where(code >= 2, -b, b)


def conj_code_times(code, z):
    odd = (code & 1) == 1
    a = jnp.where(odd, z[1], z[0])
    b = jnp.where(odd, z[0], z[1])
    return jnp.where(code >= 2, -a, a), jnp.where((code == 1) | (code == 2), -b, b)


def rows_forward(obj, code, lh, ll, tw, out, mid, xs):
    m = pl.program_id(0)

    def load(p):
        cols = slice(LANES * p, LANES * p + LANES)
        return code_times(code[0, :, cols], (obj[0, :, cols], obj[1, :, cols]))

    def store(k, v):
        v = cmul(v, (tw[0, k : k + 1], tw[1, k : k + 1]))
        xs[OCT * k : OCT * k + OCT, :LANES] = v[0]
        xs[OCT * k : OCT * k + OCT, LANES:] = v[1]

    fft32(load, store, mid, -1)
    y = dot3((lh[...], ll[...]), split(xs[...]), NT)
    for ri in range(2):
        for h in range(2):
            out[pl.ds(ri * 8 + 2 * m + h, LANES, stride=16), :] = y[
                LANES * ri : LANES * ri + LANES, LANES * h : LANES * h + LANES
            ]


def columns(rec, inten, lh, ll, ih, il, mh, ml, tw, out, s):
    for m in range(MASKS):
        x = jnp.concatenate(
            [
                jnp.concatenate(
                    [rec[pl.ds(ri * 8 + 2 * m + h, LANES, stride=16), :] for h in range(2)], axis=1
                )
                for ri in range(2)
            ],
            axis=0,
        )
        y = dot3((lh[...], ll[...]), split(x), NN)
        t = (tw[0, m], tw[1, m])
        for h in range(2):
            cols = slice(LANES * h, LANES * h + LANES)
            v = cmul((y[:LANES, cols], y[LANES:, cols]), t)
            s[m, 0, h] = v[0]
            s[m, 1, h] = v[1]

    for h in range(2):
        def turn(i, _):
            rows = pl.ds(pl.multiple_of(i * OCT, OCT), OCT)
            y = fft4([(s[m, 0, h, rows, :], s[m, 1, h, rows, :]) for m in range(4)], -1)
            for e in range(4):
                s[e, 0, h, rows, :] = y[e][0]
                s[e, 1, h, rows, :] = y[e][1]
            return 0

        lax.fori_loop(0, LANES // OCT, turn, 0, unroll=True)

    for e in range(4):
        x = jnp.concatenate(
            [jnp.concatenate([s[e, 0, h], s[e, 1, h]], axis=1) for h in range(2)], axis=0
        )
        table = (mh[e], ml[e])
        y = dot3(split(x), table, NN)
        wr, wi = y[:, :LANES], y[:, LANES:]
        weight = wr * wr + wi * wi - inten[e]
        v = jnp.concatenate([wr * weight, wi * weight], axis=1)
        y = dot3(split(v), table, NT)
        for h in range(2):
            rows = slice(LANES * h, LANES * h + LANES)
            s[e, 0, h] = y[rows, :LANES]
            s[e, 1, h] = y[rows, LANES:]

    for h in range(2):
        def turn_back(i, _):
            rows = pl.ds(pl.multiple_of(i * OCT, OCT), OCT)
            y = fft4([(s[e, 0, h, rows, :], s[e, 1, h, rows, :]) for e in range(4)], 1)
            for m in range(4):
                v = cmul(y[m], (tw[0, m, rows, :], -tw[1, m, rows, :]))
                s[m, 0, h, rows, :] = v[0]
                s[m, 1, h, rows, :] = v[1]
            return 0

        lax.fori_loop(0, LANES // OCT, turn_back, 0, unroll=True)

    for m in range(MASKS):
        x = jnp.concatenate(
            [jnp.concatenate([s[m, ri, 0], s[m, ri, 1]], axis=1) for ri in range(2)], axis=0
        )
        y = dot3((ih[...], il[...]), split(x), NN)
        for ri in range(2):
            for h in range(2):
                out[pl.ds(m * 512 + ri * 2 + h, LANES, stride=4), :] = y[
                    LANES * ri : LANES * ri + LANES, LANES * h : LANES * h + LANES
                ]


def rows_back(rec, code, lh, ll, tw, out, mid, ys):
    for l in range(MASKS):
        x = jnp.concatenate(
            [
                jnp.concatenate(
                    [
                        rec[pl.ds(l * 512 + ri * 2 + h, LANES, stride=4), :].T
                        for ri in range(2)
                    ],
                    axis=1,
                )
                for h in range(2)
            ],
            axis=0,
        )
        ys[...] = dot3(split(x), (lh[...], ll[...]), NN)

        def load(k):
            rows = slice(OCT * k, OCT * k + OCT)
            return cmul((ys[rows, :LANES], ys[rows, LANES:]), (tw[0, k : k + 1], -tw[1, k : k + 1]))

        def store(p, v):
            cols = slice(LANES * p, LANES * p + LANES)
            v = conj_code_times(code[l, :, cols], v)
            for ri in range(2):
                if l == 0:
                    out[ri, :, cols] = v[ri]
                elif l < MASKS - 1:
                    out[ri, :, cols] += v[ri]
                else:
                    out[ri, :, cols] = (out[ri, :, cols] + v[ri]) * (1.0 / MASKS)

        fft32(load, store, mid, 1)


def finish(index, own, before, after, far_re, far_im, obj, updated, direction):
    me = index[0]

    def put(shift, ri, value):
        rows = pl.ds(pl.multiple_of(lax.rem(me + shift, MASKS) * OCT, OCT), OCT)
        direction[ri, rows, :] = value
        updated[ri, rows, :] = obj[ri, rows, :] - step_size * value

    for ri in range(2):
        put(0, ri, own[ri])
        put(3, ri, before[ri])
        put(1, ri, after[ri])
    put(2, 0, far_re[0])
    put(2, 1, far_im[0])


VM = pl.BlockSpec(memory_space=pltpu.VMEM)
F32 = jnp.float32


def call(kernel, name, out_shape, n_in, scratch, flops, vmem=24, smem=()):
    specs = [VM] * n_in
    for i in smem:
        specs[i] = pl.BlockSpec(memory_space=pltpu.SMEM)
    outs = jax.tree.map(lambda _: VM, out_shape)
    return pl.pallas_call(
        kernel,
        name=name,
        out_shape=out_shape,
        in_specs=specs,
        out_specs=outs,
        scratch_shapes=scratch,
        compiler_params=pltpu.CompilerParams(vmem_limit_bytes=vmem << 20),
        cost_estimate=pl.CostEstimate(flops=flops, bytes_accessed=3 << 20, transcendentals=0),
    )


def body(object_field, phases, intensity):
    t = {k: jnp.asarray(v) for k, v in tables().items()}
    sds = jax.ShapeDtypeStruct
    index = lax.axis_index("mask").astype(jnp.int32).reshape(1)
    every = lax.all_gather(phases, "mask", axis=0, tiled=True)
    codes = lax.dynamic_slice_in_dim(every, index[0] * OCT, OCT, axis=1)
    octet = lambda m: (0, m, 0)
    sent = pl.pallas_call(
        rows_forward,
        name="rows_forward",
        out_shape=sds((2048, LANES), F32),
        grid=(MASKS,),
        in_specs=[
            pl.BlockSpec((2, OCT, N), octet),
            pl.BlockSpec((1, OCT, N), octet),
            pl.BlockSpec((256, 256), lambda m: (0, 0)),
            pl.BlockSpec((256, 256), lambda m: (0, 0)),
            pl.BlockSpec((2, SHORT, LANES), lambda m: (0, 0, 0)),
        ],
        out_specs=pl.BlockSpec((2048, LANES), lambda m: (0, 0)),
        scratch_shapes=[
            pltpu.VMEM((2, SHORT, OCT, LANES), F32),
            pltpu.VMEM((256, 256), F32),
        ],
        compiler_params=pltpu.CompilerParams(vmem_limit_bytes=60 << 20),
        cost_estimate=pl.CostEstimate(flops=1 << 29, bytes_accessed=3 << 20, transcendentals=0),
    )(object_field, phases, t["lh"], t["ll"], t["row_tw"])
    inten = intensity.reshape(2, 16, 8, 4, LANES).transpose(3, 0, 4, 1, 2).reshape(4, 256, LANES)
    rec = lax.all_to_all(sent.reshape(LANES, 16, LANES), "rows", 0, 0, tiled=True)
    back = call(
        columns, "columns", sds((2048, LANES), F32), 9,
        [pltpu.VMEM((4, 2, 2, LANES, LANES), F32)], 3 << 29,
    )(rec.reshape(2048, LANES), inten, t["lh"], t["ll"], t["ih"], t["il"], t["mh"], t["ml"], t["col_tw"])
    rec = lax.all_to_all(back.reshape(512, 4, LANES), ("mask", "rows"), 0, 0, tiled=True)
    part = call(
        rows_back, "rows_back", sds((2, OCT, N), F32), 5,
        [pltpu.VMEM((2, SHORT, OCT, LANES), F32), pltpu.VMEM((256, 256), F32)], 1 << 29,
    )(rec.reshape(2048, LANES), codes, t["lh"], t["ll"], t["row_tw"])
    up = [(i, (i + 1) % MASKS) for i in range(MASKS)]
    down = [((i + 1) % MASKS, i) for i in range(MASKS)]
    before = lax.ppermute(part, "mask", up)
    after = lax.ppermute(part, "mask", down)
    far_re = lax.ppermute(before[:1], "mask", up)
    far_im = lax.ppermute(after[1:], "mask", down)
    whole = sds((2, SHORT, N), F32)
    return call(finish, "finish", (whole, whole), 7, [], 1 << 20, smem=(0,))(
        index, part, before, after, far_re, far_im, object_field
    )


def solution(mesh):
    return jax.shard_map(
        body,
        mesh=mesh,
        in_specs=(P(None, "rows", None), P("mask", "rows", None), P("mask", "rows", None)),
        out_specs=(P(None, "rows", None), P(None, "rows", None)),
        check_vma=False,
    )
```

```python
import functools
import math

import jax
import jax.numpy as jnp
import ml_dtypes
import numpy as np
from jax import lax
from jax.experimental import pallas as pl
from jax.experimental.pallas import tpu as pltpu
from jax.sharding import PartitionSpec as P

N = 4096
LANES = 128
SHORT = 32
OCT = 8
MASKS = 4
step_size = 0.2


def _split(table):
    high = table.astype(np.float32).astype(ml_dtypes.bfloat16)
    low = (table - high.astype(np.float64)).astype(np.float32).astype(ml_dtypes.bfloat16)
    return high, low


@functools.lru_cache(maxsize=None)
def tables():
    i128 = np.arange(LANES)
    w = np.exp(-2j * math.pi * (np.outer(i128, i128) % LANES) / LANES) / 64.0
    left = np.block([[w.real, -w.imag], [w.imag, w.real]])
    t = np.exp(-2j * math.pi * np.outer(np.arange(SHORT), i128) / N)
    row_tw = np.stack([t.real, t.imag]).astype(np.float32)
    rho = i128 % OCT
    row = np.arange(MASKS)[:, None] * OCT + rho[None, :]
    t = np.exp(-2j * math.pi * (i128[None, :, None] * row[:, None, :]) / N)
    col_tw = np.stack([t.real, t.imag]).astype(np.float32)
    blocks = []
    for e in range(4):
        r8 = np.arange(OCT)
        small = np.exp(-2j * math.pi * np.outer(r8, r8) / 8 - 2j * math.pi * r8[:, None] * e / 32)
        big = np.kron(np.eye(16), small)
        blocks.append(np.block([[big.real, big.imag], [-big.imag, big.real]]))
    lh, ll = _split(left)
    ih, il = _split(left.T)
    mh, ml = _split(np.stack(blocks))
    return dict(lh=lh, ll=ll, ih=ih, il=il, mh=mh, ml=ml, row_tw=row_tw, col_tw=col_tw)


def split(x):
    high = x.astype(jnp.bfloat16)
    return high, (x - high.astype(jnp.float32)).astype(jnp.bfloat16)


def dot3(a, b, dims):
    dot = functools.partial(
        lax.dot_general, dimension_numbers=(dims, ((), ())), preferred_element_type=jnp.float32
    )
    return dot(a[0], b[0]) + (dot(a[0], b[1]) + dot(a[1], b[0]))


NN = ((1,), (0,))
NT = ((1,), (1,))


def cmul(a, b):
    return a[0] * b[0] - a[1] * b[1], a[0] * b[1] + a[1] * b[0]


def cadd(a, b):
    return a[0] + b[0], a[1] + b[1]


def csub(a, b):
    return a[0] - b[0], a[1] - b[1]


def times_i(a, sign):
    return (-a[1], a[0]) if sign > 0 else (a[1], -a[0])


def rotate(a, turns, length, sign):
    turns = turns % length
    if turns == 0:
        return a
    eighths = turns * 8 % (length * 8) / length
    if eighths == 4:
        return -a[0], -a[1]
    if eighths == 2:
        return times_i(a, sign)
    if eighths == 6:
        return times_i(a, -sign)
    angle = sign * 2 * math.pi * turns / length
    c, s = float(np.float32(math.cos(angle))), float(np.float32(math.sin(angle)))
    if eighths in (1, 3, 5, 7):
        h = float(np.float32(math.sqrt(0.5)))
        cs, ss = (1 if c > 0 else -1), (1 if s > 0 else -1)
        re = (a[0] if cs > 0 else -a[0]) - (a[1] if ss > 0 else -a[1])
        im = (a[1] if cs > 0 else -a[1]) + (a[0] if ss > 0 else -a[0])
        return re * h, im * h
    return a[0] * c - a[1] * s, a[0] * s + a[1] * c


def fft4(x, sign):
    a, b = cadd(x[0], x[2]), csub(x[0], x[2])
    c, d = cadd(x[1], x[3]), times_i(csub(x[1], x[3]), sign)
    return [cadd(a, c), cadd(b, d), csub(a, c), csub(b, d)]


def fft8(x, sign):
    even, odd = fft4(x[0::2], sign), fft4(x[1::2], sign)
    odd = [rotate(o, j, 8, sign) for j, o in enumerate(odd)]
    return [cadd(u, v) for u, v in zip(even, odd)] + [csub(u, v) for u, v in zip(even, odd)]


def fft32(load, store, mid, sign):
    for p0 in range(8):
        y = fft4([load(8 * p1 + p0) for p1 in range(4)], sign)
        for k0 in range(4):
            v = rotate(y[k0], p0 * k0, 32, sign)
            mid[0, k0 * 8 + p0] = v[0]
            mid[1, k0 * 8 + p0] = v[1]
    for k0 in range(4):
        y = fft8([(mid[0, k0 * 8 + p0], mid[1, k0 * 8 + p0]) for p0 in range(8)], sign)
        for k1 in range(8):
            store(k0 + 4 * k1, y[k1])


def code_times(code, z):
    odd = (code & 1) == 1
    a = jnp.where(odd, z[1], z[0])
    b = jnp.where(odd, z[0], z[1])
    return jnp.where((code == 1) | (code == 2), -a, a), jnp.where(code >= 2, -b, b)


def conj_code_times(code, z):
    odd = (code & 1) == 1
    a = jnp.where(odd, z[1], z[0])
    b = jnp.where(odd, z[0], z[1])
    return jnp.where(code >= 2, -a, a), jnp.where((code == 1) | (code == 2), -b, b)


def rows_forward(index, obj, code, lh, ll, tw, out, c0, c1, c2, c3, mid, xs):
    m = pl.program_id(0)
    shift = lax.rem(m + MASKS - index[0], MASKS)
    for s, c in enumerate((c0, c1, c2, c3)):

        @pl.when(shift == s)
        def _():
            c[...] = code[0]

    def load(p):
        cols = slice(LANES * p, LANES * p + LANES)
        return code_times(code[0, :, cols], (obj[0, :, cols], obj[1, :, cols]))

    def store(k, v):
        v = cmul(v, (tw[0, k : k + 1], tw[1, k : k + 1]))
        xs[OCT * k : OCT * k + OCT, :LANES] = v[0]
        xs[OCT * k : OCT * k + OCT, LANES:] = v[1]

    fft32(load, store, mid, -1)
    y = dot3((lh[...], ll[...]), split(xs[...]), NT)
    for ri in range(2):
        for h in range(2):
            out[pl.ds(ri * 8 + 2 * m + h, LANES, stride=16), :] = y[
                LANES * ri : LANES * ri + LANES, LANES * h : LANES * h + LANES
            ]


def columns(rec, inten, lh, ll, ih, il, mh, ml, tw, out, s):
    for m in range(MASKS):
        x = jnp.concatenate(
            [
                jnp.concatenate(
                    [rec[pl.ds(ri * 8 + 2 * m + h, LANES, stride=16), :] for h in range(2)], axis=1
                )
                for ri in range(2)
            ],
            axis=0,
        )
        y = dot3((lh[...], ll[...]), split(x), NN)
        t = (tw[0, m], tw[1, m])
        for h in range(2):
            cols = slice(LANES * h, LANES * h + LANES)
            v = cmul((y[:LANES, cols], y[LANES:, cols]), t)
            s[m, 0, h] = v[0]
            s[m, 1, h] = v[1]

    for h in range(2):
        def turn(i, _):
            rows = pl.ds(pl.multiple_of(i * OCT, OCT), OCT)
            y = fft4([(s[m, 0, h, rows, :], s[m, 1, h, rows, :]) for m in range(4)], -1)
            for e in range(4):
                s[e, 0, h, rows, :] = y[e][0]
                s[e, 1, h, rows, :] = y[e][1]
            return 0

        lax.fori_loop(0, LANES // OCT, turn, 0, unroll=True)

    for e in range(4):
        x = jnp.concatenate(
            [jnp.concatenate([s[e, 0, h], s[e, 1, h]], axis=1) for h in range(2)], axis=0
        )
        table = (mh[e], ml[e])
        y = dot3(split(x), table, NN)
        wr, wi = y[:, :LANES], y[:, LANES:]
        weight = wr * wr + wi * wi - inten[e]
        v = jnp.concatenate([wr * weight, wi * weight], axis=1)
        y = dot3(split(v), table, NT)
        for h in range(2):
            rows = slice(LANES * h, LANES * h + LANES)
            s[e, 0, h] = y[rows, :LANES]
            s[e, 1, h] = y[rows, LANES:]

    for h in range(2):
        def turn_back(i, _):
            rows = pl.ds(pl.multiple_of(i * OCT, OCT), OCT)
            y = fft4([(s[e, 0, h, rows, :], s[e, 1, h, rows, :]) for e in range(4)], 1)
            for m in range(4):
                v = cmul(y[m], (tw[0, m, rows, :], -tw[1, m, rows, :]))
                s[m, 0, h, rows, :] = v[0]
                s[m, 1, h, rows, :] = v[1]
            return 0

        lax.fori_loop(0, LANES // OCT, turn_back, 0, unroll=True)

    for m in range(MASKS):
        x = jnp.concatenate(
            [jnp.concatenate([s[m, ri, 0], s[m, ri, 1]], axis=1) for ri in range(2)], axis=0
        )
        y = dot3((ih[...], il[...]), split(x), NN)
        for ri in range(2):
            for h in range(2):
                out[pl.ds(m * 512 + ri * 2 + h, LANES, stride=4), :] = y[
                    LANES * ri : LANES * ri + LANES, LANES * h : LANES * h + LANES
                ]


def rows_back(index, rec, c0, c1, c2, c3, lh, ll, tw, out_re, out_im, mid, ys):
    out = (out_re, out_im)
    for s, code in enumerate((c0, c1, c2, c3)):
        l = lax.rem(index[0] + MASKS - s, MASKS)
        x = jnp.concatenate(
            [
                jnp.concatenate(
                    [
                        rec[pl.ds(l * 512 + ri * 2 + h, LANES, stride=4), :].T
                        for ri in range(2)
                    ],
                    axis=1,
                )
                for h in range(2)
            ],
            axis=0,
        )
        ys[...] = dot3(split(x), (lh[...], ll[...]), NN)

        def load(k):
            rows = slice(OCT * k, OCT * k + OCT)
            return cmul((ys[rows, :LANES], ys[rows, LANES:]), (tw[0, k : k + 1], -tw[1, k : k + 1]))

        def store(p, v):
            cols = slice(LANES * p, LANES * p + LANES)
            v = conj_code_times(code[:, cols], v)
            for ri in range(2):
                if s == 0:
                    out[ri][:, cols] = v[ri]
                elif s < MASKS - 1:
                    out[ri][:, cols] += v[ri]
                else:
                    out[ri][:, cols] = (out[ri][:, cols] + v[ri]) * (1.0 / MASKS)

        fft32(load, store, mid, 1)


def finish(index, own_re, own_im, b_re, b_im, a_re, a_im, far_re, far_im, obj, updated, direction):
    me = index[0]

    def put(shift, ri, value):
        rows = pl.ds(pl.multiple_of(lax.rem(me + shift, MASKS) * OCT, OCT), OCT)
        direction[ri, rows, :] = value
        updated[ri, rows, :] = obj[ri, rows, :] - step_size * value

    put(0, 0, own_re[...])
    put(0, 1, own_im[...])
    put(3, 0, b_re[...])
    put(3, 1, b_im[...])
    put(1, 0, a_re[...])
    put(1, 1, a_im[...])
    put(2, 0, far_re[...])
    put(2, 1, far_im[...])


VM = pl.BlockSpec(memory_space=pltpu.VMEM)
F32 = jnp.float32


def call(kernel, name, out_shape, n_in, scratch, flops, vmem=24, smem=()):
    specs = [VM] * n_in
    for i in smem:
        specs[i] = pl.BlockSpec(memory_space=pltpu.SMEM)
    outs = jax.tree.map(lambda _: VM, out_shape)
    return pl.pallas_call(
        kernel,
        name=name,
        out_shape=out_shape,
        in_specs=specs,
        out_specs=outs,
        scratch_shapes=scratch,
        compiler_params=pltpu.CompilerParams(vmem_limit_bytes=vmem << 20),
        cost_estimate=pl.CostEstimate(flops=flops, bytes_accessed=3 << 20, transcendentals=0),
    )


def body(object_field, phases, intensity):
    t = {k: jnp.asarray(v) for k, v in tables().items()}
    sds = jax.ShapeDtypeStruct
    index = lax.axis_index("mask").astype(jnp.int32).reshape(1)
    octet = lambda m: (0, m, 0)
    flat = lambda m: (0, 0)
    rows8 = sds((OCT, N), jnp.int32)
    sent, c0, c1, c2, c3 = pl.pallas_call(
        rows_forward,
        name="rows_forward",
        out_shape=(sds((2048, LANES), F32),) + (rows8,) * MASKS,
        grid=(MASKS,),
        in_specs=[
            pl.BlockSpec(memory_space=pltpu.SMEM),
            pl.BlockSpec((2, OCT, N), octet),
            pl.BlockSpec((1, OCT, N), octet),
            pl.BlockSpec((256, 256), flat),
            pl.BlockSpec((256, 256), flat),
            pl.BlockSpec((2, SHORT, LANES), lambda m: (0, 0, 0)),
        ],
        out_specs=(pl.BlockSpec((2048, LANES), flat),) + (pl.BlockSpec((OCT, N), flat),) * MASKS,
        scratch_shapes=[
            pltpu.VMEM((2, SHORT, OCT, LANES), F32),
            pltpu.VMEM((256, 256), F32),
        ],
        compiler_params=pltpu.CompilerParams(vmem_limit_bytes=60 << 20),
        cost_estimate=pl.CostEstimate(flops=1 << 29, bytes_accessed=3 << 20, transcendentals=0),
    )(index, object_field, phases, t["lh"], t["ll"], t["row_tw"])
    inten = intensity.reshape(2, 16, 8, 4, LANES).transpose(3, 0, 4, 1, 2).reshape(4, 256, LANES)
    rec = lax.all_to_all(sent.reshape(LANES, 16, LANES), "rows", 0, 0, tiled=True)
    back = call(
        columns, "columns", sds((2048, LANES), F32), 9,
        [pltpu.VMEM((4, 2, 2, LANES, LANES), F32)], 3 << 29,
    )(rec.reshape(2048, LANES), inten, t["lh"], t["ll"], t["ih"], t["il"], t["mh"], t["ml"], t["col_tw"])
    rec = lax.all_to_all(back.reshape(512, 4, LANES), ("mask", "rows"), 0, 0, tiled=True)
    up = [(i, (i + 1) % MASKS) for i in range(MASKS)]
    down = [((i + 1) % MASKS, i) for i in range(MASKS)]
    across = [(i, (i + 2) % MASKS) for i in range(MASKS)]
    g1 = lax.ppermute(c1, "mask", up)
    g2 = lax.ppermute(c2, "mask", across)
    g3 = lax.ppermute(c3, "mask", down)
    own_re, own_im = call(
        rows_back, "rows_back", (sds((OCT, N), F32),) * 2, 9,
        [pltpu.VMEM((2, SHORT, OCT, LANES), F32), pltpu.VMEM((256, 256), F32)], 1 << 29, smem=(0,),
    )(index, rec.reshape(2048, LANES), c0, g1, g2, g3, t["lh"], t["ll"], t["row_tw"])
    b_re = lax.ppermute(own_re, "mask", up)
    a_im = lax.ppermute(own_im, "mask", down)
    b_im = lax.ppermute(own_im, "mask", up)
    a_re = lax.ppermute(own_re, "mask", down)
    far_re = lax.ppermute(b_re, "mask", up)
    far_im = lax.ppermute(a_im, "mask", down)
    whole = sds((2, SHORT, N), F32)
    return call(finish, "finish", (whole, whole), 10, [], 1 << 20, smem=(0,))(
        index, own_re, own_im, b_re, b_im, a_re, a_im, far_re, far_im, object_field
    )


def solution(mesh):
    return jax.shard_map(
        body,
        mesh=mesh,
        in_specs=(P(None, "rows", None), P("mask", "rows", None), P("mask", "rows", None)),
        out_specs=(P(None, "rows", None), P(None, "rows", None)),
        check_vma=False,
    )
```

```python
import functools
import math

import jax
import jax.numpy as jnp
import ml_dtypes
import numpy as np
from jax import lax
from jax.experimental import pallas as pl
from jax.experimental.pallas import tpu as pltpu
from jax.sharding import PartitionSpec as P

N = 4096
LANES = 128
SHORT = 32
OCT = 8
MASKS = 4
step_size = 0.2


def _split(table):
    high = table.astype(np.float32).astype(ml_dtypes.bfloat16)
    low = (table - high.astype(np.float64)).astype(np.float32).astype(ml_dtypes.bfloat16)
    return np.stack([high, low])


@functools.lru_cache(maxsize=None)
def tables():
    i128 = np.arange(LANES)
    w = np.exp(-2j * math.pi * (np.outer(i128, i128) % LANES) / LANES) / 64.0
    left = np.block([[w.real, -w.imag], [w.imag, w.real]])
    t = np.exp(-2j * math.pi * np.outer(np.arange(SHORT), i128) / N)
    row_tw = np.stack([t.real, t.imag]).astype(np.float32)
    rho = i128 % OCT
    row = np.arange(MASKS)[:, None] * OCT + rho[None, :]
    t = np.exp(-2j * math.pi * (i128[None, :, None] * row[:, None, :]) / N)
    col_tw = np.stack([t.real, t.imag]).astype(np.float32)
    blocks = []
    for e in range(4):
        r8 = np.arange(OCT)
        small = np.exp(-2j * math.pi * np.outer(r8, r8) / 8 - 2j * math.pi * r8[:, None] * e / 32)
        big = np.kron(np.eye(16), small)
        blocks.append(np.block([[big.real, big.imag], [-big.imag, big.real]]))
    both = np.concatenate([_split(left), _split(left.T)])
    return dict(left=_split(left), both=both, block=_split(np.stack(blocks)), row_tw=row_tw, col_tw=col_tw)


def split(x):
    high = x.astype(jnp.bfloat16)
    return high, (x - high.astype(jnp.float32)).astype(jnp.bfloat16)


def dot3(a, b, dims):
    dot = functools.partial(
        lax.dot_general, dimension_numbers=(dims, ((), ())), preferred_element_type=jnp.float32
    )
    return dot(a[0], b[0]) + (dot(a[0], b[1]) + dot(a[1], b[0]))


NN = ((1,), (0,))
NT = ((1,), (1,))


def cmul(a, b):
    return a[0] * b[0] - a[1] * b[1], a[0] * b[1] + a[1] * b[0]


def cadd(a, b):
    return a[0] + b[0], a[1] + b[1]


def csub(a, b):
    return a[0] - b[0], a[1] - b[1]


def times_i(a, sign):
    return (-a[1], a[0]) if sign > 0 else (a[1], -a[0])


def rotate(a, turns, length, sign):
    turns = turns % length
    if turns == 0:
        return a
    eighths = turns * 8 % (length * 8) / length
    if eighths == 4:
        return -a[0], -a[1]
    if eighths == 2:
        return times_i(a, sign)
    if eighths == 6:
        return times_i(a, -sign)
    angle = sign * 2 * math.pi * turns / length
    c, s = float(np.float32(math.cos(angle))), float(np.float32(math.sin(angle)))
    if eighths in (1, 3, 5, 7):
        h = float(np.float32(math.sqrt(0.5)))
        cs, ss = (1 if c > 0 else -1), (1 if s > 0 else -1)
        re = (a[0] if cs > 0 else -a[0]) - (a[1] if ss > 0 else -a[1])
        im = (a[1] if cs > 0 else -a[1]) + (a[0] if ss > 0 else -a[0])
        return re * h, im * h
    return a[0] * c - a[1] * s, a[0] * s + a[1] * c


def fft4(x, sign):
    a, b = cadd(x[0], x[2]), csub(x[0], x[2])
    c, d = cadd(x[1], x[3]), times_i(csub(x[1], x[3]), sign)
    return [cadd(a, c), cadd(b, d), csub(a, c), csub(b, d)]


def fft8(x, sign):
    even, odd = fft4(x[0::2], sign), fft4(x[1::2], sign)
    odd = [rotate(o, j, 8, sign) for j, o in enumerate(odd)]
    return [cadd(u, v) for u, v in zip(even, odd)] + [csub(u, v) for u, v in zip(even, odd)]


def fft32(load, store, mid, sign):
    for p0 in range(8):
        y = fft4([load(8 * p1 + p0) for p1 in range(4)], sign)
        for k0 in range(4):
            v = rotate(y[k0], p0 * k0, 32, sign)
            mid[0, k0 * 8 + p0] = v[0]
            mid[1, k0 * 8 + p0] = v[1]
    for k0 in range(4):
        y = fft8([(mid[0, k0 * 8 + p0], mid[1, k0 * 8 + p0]) for p0 in range(8)], sign)
        for k1 in range(8):
            store(k0 + 4 * k1, y[k1])


def code_times(code, z):
    odd = (code & 1) == 1
    a = jnp.where(odd, z[1], z[0])
    b = jnp.where(odd, z[0], z[1])
    return jnp.where((code == 1) | (code == 2), -a, a), jnp.where(code >= 2, -b, b)


def conj_code_times(code, z):
    odd = (code & 1) == 1
    a = jnp.where(odd, z[1], z[0])
    b = jnp.where(odd, z[0], z[1])
    return jnp.where(code >= 2, -a, a), jnp.where((code == 1) | (code == 2), -b, b)


def rows_forward(index, obj, code, left, tw, out, c0, c1, c2, c3, mid, xs):
    m = pl.program_id(0)
    shift = lax.rem(m + MASKS - index[0], MASKS)
    for s, c in enumerate((c0, c1, c2, c3)):

        @pl.when(shift == s)
        def _():
            c[...] = code[0]

    def load(p):
        cols = slice(LANES * p, LANES * p + LANES)
        return code_times(code[0, :, cols], (obj[0, :, cols], obj[1, :, cols]))

    def store(k, v):
        v = cmul(v, (tw[0, k : k + 1], tw[1, k : k + 1]))
        xs[OCT * k : OCT * k + OCT, :LANES] = v[0]
        xs[OCT * k : OCT * k + OCT, LANES:] = v[1]

    fft32(load, store, mid, -1)
    y = dot3((left[0], left[1]), split(xs[...]), NT)
    for ri in range(2):
        for h in range(2):
            out[pl.ds(ri * 8 + 2 * m + h, LANES, stride=16), :] = y[
                LANES * ri : LANES * ri + LANES, LANES * h : LANES * h + LANES
            ]


def columns(rec, inten, both, block, tw, out, s):
    for m in range(MASKS):
        x = jnp.concatenate(
            [
                jnp.concatenate(
                    [rec[pl.ds(ri * 8 + 2 * m + h, LANES, stride=16), :] for h in range(2)], axis=1
                )
                for ri in range(2)
            ],
            axis=0,
        )
        y = dot3((both[0], both[1]), split(x), NN)
        t = (tw[0, m], tw[1, m])
        for h in range(2):
            cols = slice(LANES * h, LANES * h + LANES)
            v = cmul((y[:LANES, cols], y[LANES:, cols]), t)
            s[m, 0, h] = v[0]
            s[m, 1, h] = v[1]

    for h in range(2):
        def turn(i, _):
            rows = pl.ds(pl.multiple_of(i * OCT, OCT), OCT)
            y = fft4([(s[m, 0, h, rows, :], s[m, 1, h, rows, :]) for m in range(4)], -1)
            for e in range(4):
                s[e, 0, h, rows, :] = y[e][0]
                s[e, 1, h, rows, :] = y[e][1]
            return 0

        lax.fori_loop(0, LANES // OCT, turn, 0, unroll=True)

    for e in range(4):
        x = jnp.concatenate(
            [jnp.concatenate([s[e, 0, h], s[e, 1, h]], axis=1) for h in range(2)], axis=0
        )
        table = (block[0, e], block[1, e])
        y = dot3(split(x), table, NN)
        wr, wi = y[:, :LANES], y[:, LANES:]
        weight = wr * wr + wi * wi - inten[e]
        v = jnp.concatenate([wr * weight, wi * weight], axis=1)
        y = dot3(split(v), table, NT)
        for h in range(2):
            rows = slice(LANES * h, LANES * h + LANES)
            s[e, 0, h] = y[rows, :LANES]
            s[e, 1, h] = y[rows, LANES:]

    for h in range(2):
        def turn_back(i, _):
            rows = pl.ds(pl.multiple_of(i * OCT, OCT), OCT)
            y = fft4([(s[e, 0, h, rows, :], s[e, 1, h, rows, :]) for e in range(4)], 1)
            for m in range(4):
                v = cmul(y[m], (tw[0, m, rows, :], -tw[1, m, rows, :]))
                s[m, 0, h, rows, :] = v[0]
                s[m, 1, h, rows, :] = v[1]
            return 0

        lax.fori_loop(0, LANES // OCT, turn_back, 0, unroll=True)

    for m in range(MASKS):
        x = jnp.concatenate(
            [jnp.concatenate([s[m, ri, 0], s[m, ri, 1]], axis=1) for ri in range(2)], axis=0
        )
        y = dot3((both[2], both[3]), split(x), NN)
        for ri in range(2):
            for h in range(2):
                out[pl.ds(m * 512 + ri * 2 + h, LANES, stride=4), :] = y[
                    LANES * ri : LANES * ri + LANES, LANES * h : LANES * h + LANES
                ]


def rows_back(index, rec, c0, c1, c2, c3, left, tw, out_re, out_im, mid, ys):
    out = (out_re, out_im)
    for s, code in enumerate((c0, c1, c2, c3)):
        l = lax.rem(index[0] + MASKS - s, MASKS)
        x = jnp.concatenate(
            [
                jnp.concatenate(
                    [
                        rec[pl.ds(l * 512 + ri * 2 + h, LANES, stride=4), :].T
                        for ri in range(2)
                    ],
                    axis=1,
                )
                for h in range(2)
            ],
            axis=0,
        )
        ys[...] = dot3(split(x), (left[0], left[1]), NN)

        def load(k):
            rows = slice(OCT * k, OCT * k + OCT)
            return cmul((ys[rows, :LANES], ys[rows, LANES:]), (tw[0, k : k + 1], -tw[1, k : k + 1]))

        def store(p, v):
            cols = slice(LANES * p, LANES * p + LANES)
            v = conj_code_times(code[:, cols], v)
            for ri in range(2):
                if s == 0:
                    out[ri][:, cols] = v[ri]
                elif s < MASKS - 1:
                    out[ri][:, cols] += v[ri]
                else:
                    out[ri][:, cols] = (out[ri][:, cols] + v[ri]) * (1.0 / MASKS)

        fft32(load, store, mid, 1)


def finish(index, own_re, own_im, b_re, b_im, a_re, a_im, far_re, far_im, obj, updated, direction):
    me = index[0]

    def put(shift, ri, value):
        rows = pl.ds(pl.multiple_of(lax.rem(me + shift, MASKS) * OCT, OCT), OCT)
        direction[ri, rows, :] = value
        updated[ri, rows, :] = obj[ri, rows, :] - step_size * value

    put(0, 0, own_re[...])
    put(0, 1, own_im[...])
    put(3, 0, b_re[...])
    put(3, 1, b_im[...])
    put(1, 0, a_re[...])
    put(1, 1, a_im[...])
    put(2, 0, far_re[...])
    put(2, 1, far_im[...])


VM = pl.BlockSpec(memory_space=pltpu.VMEM)
F32 = jnp.float32


def call(kernel, name, out_shape, n_in, scratch, flops, vmem=24, smem=()):
    specs = [VM] * n_in
    for i in smem:
        specs[i] = pl.BlockSpec(memory_space=pltpu.SMEM)
    outs = jax.tree.map(lambda _: VM, out_shape)
    return pl.pallas_call(
        kernel,
        name=name,
        out_shape=out_shape,
        in_specs=specs,
        out_specs=outs,
        scratch_shapes=scratch,
        compiler_params=pltpu.CompilerParams(vmem_limit_bytes=vmem << 20),
        cost_estimate=pl.CostEstimate(flops=flops, bytes_accessed=3 << 20, transcendentals=0),
    )


def body(object_field, phases, intensity):
    t = {k: jnp.asarray(v) for k, v in tables().items()}
    sds = jax.ShapeDtypeStruct
    index = lax.axis_index("mask").astype(jnp.int32).reshape(1)
    octet = lambda m: (0, m, 0)
    flat = lambda m: (0, 0)
    rows8 = sds((OCT, N), jnp.int32)
    sent, c0, c1, c2, c3 = pl.pallas_call(
        rows_forward,
        name="rows_forward",
        out_shape=(sds((2048, LANES), F32),) + (rows8,) * MASKS,
        grid=(MASKS,),
        in_specs=[
            pl.BlockSpec(memory_space=pltpu.SMEM),
            pl.BlockSpec((2, OCT, N), octet),
            pl.BlockSpec((1, OCT, N), octet),
            pl.BlockSpec((2, 256, 256), lambda m: (0, 0, 0)),
            pl.BlockSpec((2, SHORT, LANES), lambda m: (0, 0, 0)),
        ],
        out_specs=(pl.BlockSpec((2048, LANES), flat),) + (pl.BlockSpec((OCT, N), flat),) * MASKS,
        scratch_shapes=[
            pltpu.VMEM((2, SHORT, OCT, LANES), F32),
            pltpu.VMEM((256, 256), F32),
        ],
        compiler_params=pltpu.CompilerParams(vmem_limit_bytes=60 << 20),
        cost_estimate=pl.CostEstimate(flops=1 << 29, bytes_accessed=3 << 20, transcendentals=0),
    )(index, object_field, phases, t["left"], t["row_tw"])
    inten = intensity.reshape(2, 16, 8, 4, LANES).transpose(3, 0, 4, 1, 2).reshape(4, 256, LANES)
    up = [(i, (i + 1) % MASKS) for i in range(MASKS)]
    down = [((i + 1) % MASKS, i) for i in range(MASKS)]
    across = [(i, (i + 2) % MASKS) for i in range(MASKS)]
    rec = lax.all_to_all(sent.reshape(LANES, 16, LANES), "rows", 0, 0, tiled=True)
    g1 = lax.ppermute(c1, "mask", up)
    g2 = lax.ppermute(c2, "mask", across)
    g3 = lax.ppermute(c3, "mask", down)
    rec, g1, g2, g3 = lax.optimization_barrier((rec, g1, g2, g3))
    back = call(
        columns, "columns", sds((2048, LANES), F32), 5,
        [pltpu.VMEM((4, 2, 2, LANES, LANES), F32)], 3 << 29,
    )(rec.reshape(2048, LANES), inten, t["both"], t["block"], t["col_tw"])
    rec = lax.all_to_all(back.reshape(512, 4, LANES), ("mask", "rows"), 0, 0, tiled=True)
    own_re, own_im = call(
        rows_back, "rows_back", (sds((OCT, N), F32),) * 2, 8,
        [pltpu.VMEM((2, SHORT, OCT, LANES), F32), pltpu.VMEM((256, 256), F32)], 1 << 29, smem=(0,),
    )(index, rec.reshape(2048, LANES), c0, g1, g2, g3, t["left"], t["row_tw"])
    b_re = lax.ppermute(own_re, "mask", up)
    a_im = lax.ppermute(own_im, "mask", down)
    b_im = lax.ppermute(own_im, "mask", up)
    a_re = lax.ppermute(own_re, "mask", down)
    far_re = lax.ppermute(b_re, "mask", up)
    far_im = lax.ppermute(a_im, "mask", down)
    whole = sds((2, SHORT, N), F32)
    return call(finish, "finish", (whole, whole), 10, [], 1 << 20, smem=(0,))(
        index, own_re, own_im, b_re, b_im, a_re, a_im, far_re, far_im, object_field
    )


def solution(mesh):
    return jax.shard_map(
        body,
        mesh=mesh,
        in_specs=(P(None, "rows", None), P("mask", "rows", None), P("mask", "rows", None)),
        out_specs=(P(None, "rows", None), P(None, "rows", None)),
        check_vma=False,
    )
```

```python
import functools
import math

import jax
import jax.numpy as jnp
import ml_dtypes
import numpy as np
from jax import lax
from jax.experimental import pallas as pl
from jax.experimental.pallas import tpu as pltpu
from jax.sharding import PartitionSpec as P

N = 4096
LANES = 128
SHORT = 32
OCT = 8
MASKS = 4
step_size = 0.2


def _split(table):
    high = table.astype(np.float32).astype(ml_dtypes.bfloat16)
    low = (table - high.astype(np.float64)).astype(np.float32).astype(ml_dtypes.bfloat16)
    return np.stack([high, low])


def exchange_order():
    index = np.arange(LANES).reshape(2, 4, 8, 2)
    return index.transpose(3, 0, 1, 2).reshape(LANES)


@functools.lru_cache(maxsize=None)
def tables():
    i128 = np.arange(LANES)
    w = np.exp(-2j * math.pi * (np.outer(i128, i128) % LANES) / LANES) / 64.0
    w = w[exchange_order()]
    left = np.block([[w.real, -w.imag], [w.imag, w.real]])
    inner = np.block([[w.real.T, -w.imag.T], [w.imag.T, w.real.T]])
    t = np.exp(-2j * math.pi * np.outer(np.arange(SHORT), i128) / N)
    row_tw = np.stack([t.real, t.imag]).astype(np.float32)
    rho = i128 % OCT
    row = np.arange(MASKS)[:, None] * OCT + rho[None, :]
    t = np.exp(-2j * math.pi * (i128[None, :, None] * row[:, None, :]) / N)
    col_tw = np.stack([t.real, t.imag]).astype(np.float32)
    blocks = []
    for e in range(4):
        r8 = np.arange(OCT)
        small = np.exp(-2j * math.pi * np.outer(r8, r8) / 8 - 2j * math.pi * r8[:, None] * e / 32)
        big = np.kron(np.eye(16), small)
        blocks.append(np.block([[big.real, big.imag], [-big.imag, big.real]]))
    both = np.concatenate([_split(inner), _split(inner.T)])
    return dict(left=_split(left), both=both, block=_split(np.stack(blocks)), row_tw=row_tw, col_tw=col_tw)


def split(x):
    high = x.astype(jnp.bfloat16)
    return high, (x - high.astype(jnp.float32)).astype(jnp.bfloat16)


def dot3(a, b, dims):
    dot = functools.partial(
        lax.dot_general, dimension_numbers=(dims, ((), ())), preferred_element_type=jnp.float32
    )
    return dot(a[0], b[0]) + (dot(a[0], b[1]) + dot(a[1], b[0]))


NN = ((1,), (0,))
NT = ((1,), (1,))


def cmul(a, b):
    return a[0] * b[0] - a[1] * b[1], a[0] * b[1] + a[1] * b[0]


def cadd(a, b):
    return a[0] + b[0], a[1] + b[1]


def csub(a, b):
    return a[0] - b[0], a[1] - b[1]


def times_i(a, sign):
    return (-a[1], a[0]) if sign > 0 else (a[1], -a[0])


def rotate(a, turns, length, sign):
    turns = turns % length
    if turns == 0:
        return a
    eighths = turns * 8 % (length * 8) / length
    if eighths == 4:
        return -a[0], -a[1]
    if eighths == 2:
        return times_i(a, sign)
    if eighths == 6:
        return times_i(a, -sign)
    angle = sign * 2 * math.pi * turns / length
    c, s = float(np.float32(math.cos(angle))), float(np.float32(math.sin(angle)))
    if eighths in (1, 3, 5, 7):
        h = float(np.float32(math.sqrt(0.5)))
        cs, ss = (1 if c > 0 else -1), (1 if s > 0 else -1)
        re = (a[0] if cs > 0 else -a[0]) - (a[1] if ss > 0 else -a[1])
        im = (a[1] if cs > 0 else -a[1]) + (a[0] if ss > 0 else -a[0])
        return re * h, im * h
    return a[0] * c - a[1] * s, a[0] * s + a[1] * c


def fft4(x, sign):
    a, b = cadd(x[0], x[2]), csub(x[0], x[2])
    c, d = cadd(x[1], x[3]), times_i(csub(x[1], x[3]), sign)
    return [cadd(a, c), cadd(b, d), csub(a, c), csub(b, d)]


def fft8(x, sign):
    even, odd = fft4(x[0::2], sign), fft4(x[1::2], sign)
    odd = [rotate(o, j, 8, sign) for j, o in enumerate(odd)]
    return [cadd(u, v) for u, v in zip(even, odd)] + [csub(u, v) for u, v in zip(even, odd)]


def fft32(load, store, mid, sign):
    for p0 in range(8):
        y = fft4([load(8 * p1 + p0) for p1 in range(4)], sign)
        for k0 in range(4):
            v = rotate(y[k0], p0 * k0, 32, sign)
            mid[0, k0 * 8 + p0] = v[0]
            mid[1, k0 * 8 + p0] = v[1]
    for k0 in range(4):
        y = fft8([(mid[0, k0 * 8 + p0], mid[1, k0 * 8 + p0]) for p0 in range(8)], sign)
        for k1 in range(8):
            store(k0 + 4 * k1, y[k1])


def code_times(code, z):
    odd = (code & 1) == 1
    a = jnp.where(odd, z[1], z[0])
    b = jnp.where(odd, z[0], z[1])
    return jnp.where((code == 1) | (code == 2), -a, a), jnp.where(code >= 2, -b, b)


def conj_code_times(code, z):
    odd = (code & 1) == 1
    a = jnp.where(odd, z[1], z[0])
    b = jnp.where(odd, z[0], z[1])
    return jnp.where(code >= 2, -a, a), jnp.where((code == 1) | (code == 2), -b, b)


def rows_forward(index, obj, code, left, tw, out, c0, c1, c2, c3, mid, xs):
    m = pl.program_id(0)
    shift = lax.rem(m + MASKS - index[0], MASKS)
    for s, c in enumerate((c0, c1, c2, c3)):

        @pl.when(shift == s)
        def _():
            c[...] = code[0]

    def load(p):
        cols = slice(LANES * p, LANES * p + LANES)
        return code_times(code[0, :, cols], (obj[0, :, cols], obj[1, :, cols]))

    def store(k, v):
        v = cmul(v, (tw[0, k : k + 1], tw[1, k : k + 1]))
        xs[OCT * k : OCT * k + OCT, :LANES] = v[0]
        xs[OCT * k : OCT * k + OCT, LANES:] = v[1]

    fft32(load, store, mid, -1)
    y = dot3((left[0], left[1]), split(xs[...]), NT)
    for ri in range(2):
        for h in range(2):
            out[pl.ds(ri * 8 + 2 * m + h, LANES, stride=16), :] = y[
                LANES * ri : LANES * ri + LANES, LANES * h : LANES * h + LANES
            ]


def columns(rec, inten, both, block, tw, out, s):
    for m in range(MASKS):
        x = jnp.concatenate(
            [
                jnp.concatenate(
                    [rec[pl.ds(ri * 8 + 2 * m + h, LANES, stride=16), :] for h in range(2)], axis=1
                )
                for ri in range(2)
            ],
            axis=0,
        )
        y = dot3((both[0], both[1]), split(x), NN)
        t = (tw[0, m], tw[1, m])
        for h in range(2):
            cols = slice(LANES * h, LANES * h + LANES)
            v = cmul((y[:LANES, cols], y[LANES:, cols]), t)
            s[m, 0, h] = v[0]
            s[m, 1, h] = v[1]

    for h in range(2):
        def turn(i, _):
            rows = pl.ds(pl.multiple_of(i * OCT, OCT), OCT)
            y = fft4([(s[m, 0, h, rows, :], s[m, 1, h, rows, :]) for m in range(4)], -1)
            for e in range(4):
                s[e, 0, h, rows, :] = y[e][0]
                s[e, 1, h, rows, :] = y[e][1]
            return 0

        lax.fori_loop(0, LANES // OCT, turn, 0, unroll=True)

    for e in range(4):
        x = jnp.concatenate(
            [jnp.concatenate([s[e, 0, h], s[e, 1, h]], axis=1) for h in range(2)], axis=0
        )
        table = (block[0, e], block[1, e])
        y = dot3(split(x), table, NN)
        wr, wi = y[:, :LANES], y[:, LANES:]
        weight = wr * wr + wi * wi - inten[e]
        v = jnp.concatenate([wr * weight, wi * weight], axis=1)
        y = dot3(split(v), table, NT)
        for h in range(2):
            rows = slice(LANES * h, LANES * h + LANES)
            s[e, 0, h] = y[rows, :LANES]
            s[e, 1, h] = y[rows, LANES:]

    for h in range(2):
        def turn_back(i, _):
            rows = pl.ds(pl.multiple_of(i * OCT, OCT), OCT)
            y = fft4([(s[e, 0, h, rows, :], s[e, 1, h, rows, :]) for e in range(4)], 1)
            for m in range(4):
                v = cmul(y[m], (tw[0, m, rows, :], -tw[1, m, rows, :]))
                s[m, 0, h, rows, :] = v[0]
                s[m, 1, h, rows, :] = v[1]
            return 0

        lax.fori_loop(0, LANES // OCT, turn_back, 0, unroll=True)

    for m in range(MASKS):
        x = jnp.concatenate(
            [jnp.concatenate([s[m, ri, 0], s[m, ri, 1]], axis=1) for ri in range(2)], axis=0
        )
        y = dot3((both[2], both[3]), split(x), NN)
        for ri in range(2):
            for h in range(2):
                out[pl.ds(m * 4 + ri * 2 + h, LANES, stride=16), :] = y[
                    LANES * ri : LANES * ri + LANES, LANES * h : LANES * h + LANES
                ]


def rows_back(index, rec, c0, c1, c2, c3, left, tw, out, mid, ys):
    for s, code in enumerate((c0, c1, c2, c3)):
        l = lax.rem(index[0] + MASKS - s, MASKS)
        x = jnp.concatenate(
            [
                jnp.concatenate(
                    [
                        rec[pl.ds(l * 4 + ri * 2 + h, LANES, stride=16), :].T
                        for ri in range(2)
                    ],
                    axis=1,
                )
                for h in range(2)
            ],
            axis=0,
        )
        ys[...] = dot3(split(x), (left[0], left[1]), NN)

        def load(k):
            rows = slice(OCT * k, OCT * k + OCT)
            return cmul((ys[rows, :LANES], ys[rows, LANES:]), (tw[0, k : k + 1], -tw[1, k : k + 1]))

        def store(p, v):
            cols = slice(LANES * p, LANES * p + LANES)
            v = conj_code_times(code[:, cols], v)
            for ri in range(2):
                if s == 0:
                    out[0, ri, :, cols] = v[ri]
                elif s < MASKS - 1:
                    out[0, ri, :, cols] += v[ri]
                else:
                    total = (out[0, ri, :, cols] + v[ri]) * (1.0 / MASKS)
                    for copy in range(MASKS):
                        out[copy, ri, :, cols] = total

        fft32(load, store, mid, 1)


def finish(parts, obj, updated, direction):
    for m in range(MASKS):
        rows = slice(OCT * m, OCT * m + OCT)
        for ri in range(2):
            value = parts[m, ri]
            direction[ri, rows, :] = value
            updated[ri, rows, :] = obj[ri, rows, :] - step_size * value


VM = pl.BlockSpec(memory_space=pltpu.VMEM)
F32 = jnp.float32


def call(kernel, name, out_shape, n_in, scratch, flops, vmem=24, smem=()):
    specs = [VM] * n_in
    for i in smem:
        specs[i] = pl.BlockSpec(memory_space=pltpu.SMEM)
    outs = jax.tree.map(lambda _: VM, out_shape)
    return pl.pallas_call(
        kernel,
        name=name,
        out_shape=out_shape,
        in_specs=specs,
        out_specs=outs,
        scratch_shapes=scratch,
        compiler_params=pltpu.CompilerParams(vmem_limit_bytes=vmem << 20),
        cost_estimate=pl.CostEstimate(flops=flops, bytes_accessed=3 << 20, transcendentals=0),
    )


def body(object_field, phases, intensity):
    t = {k: jnp.asarray(v) for k, v in tables().items()}
    sds = jax.ShapeDtypeStruct
    index = lax.axis_index("mask").astype(jnp.int32).reshape(1)
    octet = lambda m: (0, m, 0)
    flat = lambda m: (0, 0)
    rows8 = sds((OCT, N), jnp.int32)
    sent, c0, c1, c2, c3 = pl.pallas_call(
        rows_forward,
        name="rows_forward",
        out_shape=(sds((2048, LANES), F32),) + (rows8,) * MASKS,
        grid=(MASKS,),
        in_specs=[
            pl.BlockSpec(memory_space=pltpu.SMEM),
            pl.BlockSpec((2, OCT, N), octet),
            pl.BlockSpec((1, OCT, N), octet),
            pl.BlockSpec((2, 256, 256), lambda m: (0, 0, 0)),
            pl.BlockSpec((2, SHORT, LANES), lambda m: (0, 0, 0)),
        ],
        out_specs=(pl.BlockSpec((2048, LANES), flat),) + (pl.BlockSpec((OCT, N), flat),) * MASKS,
        scratch_shapes=[
            pltpu.VMEM((2, SHORT, OCT, LANES), F32),
            pltpu.VMEM((256, 256), F32),
        ],
        compiler_params=pltpu.CompilerParams(vmem_limit_bytes=60 << 20),
        cost_estimate=pl.CostEstimate(flops=1 << 29, bytes_accessed=3 << 20, transcendentals=0),
    )(index, object_field, phases, t["left"], t["row_tw"])
    inten = intensity.reshape(2, 16, 8, 4, LANES).transpose(3, 0, 4, 1, 2).reshape(4, 256, LANES)
    up = [(i, (i + 1) % MASKS) for i in range(MASKS)]
    down = [((i + 1) % MASKS, i) for i in range(MASKS)]
    across = [(i, (i + 2) % MASKS) for i in range(MASKS)]
    order = [int(i) for i in exchange_order()]
    every = [m * LANES + i for i in order for m in range(MASKS)]
    exchange = functools.partial(lax.all_to_all, split_axis=0, concat_axis=0, tiled=True)
    rec = exchange(sent.reshape(LANES, 16, LANES), "rows", axis_index_groups=[order])
    g1 = lax.ppermute(c1, "mask", up)
    g2 = lax.ppermute(c2, "mask", across)
    g3 = lax.ppermute(c3, "mask", down)
    back = call(
        columns, "columns", sds((2048, LANES), F32), 5,
        [pltpu.VMEM((4, 2, 2, LANES, LANES), F32)], 3 << 29,
    )(rec.reshape(2048, LANES), inten, t["both"], t["block"], t["col_tw"])
    back, g1, g2, g3 = lax.optimization_barrier((back, g1, g2, g3))
    rec = exchange(back.reshape(512, 4, LANES), ("mask", "rows"), axis_index_groups=[every])
    part = call(
        rows_back, "rows_back", sds((MASKS, 2, OCT, N), F32), 8,
        [pltpu.VMEM((2, SHORT, OCT, LANES), F32), pltpu.VMEM((256, 256), F32)], 1 << 29, smem=(0,),
    )(index, rec.reshape(2048, LANES), c0, g1, g2, g3, t["left"], t["row_tw"])
    parts = exchange(part, "mask")
    whole = sds((2, SHORT, N), F32)
    return call(finish, "finish", (whole, whole), 2, [], 1 << 20)(parts, object_field)


def solution(mesh):
    return jax.shard_map(
        body,
        mesh=mesh,
        in_specs=(P(None, "rows", None), P("mask", "rows", None), P("mask", "rows", None)),
        out_specs=(P(None, "rows", None), P(None, "rows", None)),
        check_vma=False,
    )
```

```python
import functools
import math

import jax
import jax.numpy as jnp
import ml_dtypes
import numpy as np
from jax import lax
from jax.experimental import pallas as pl
from jax.experimental.pallas import tpu as pltpu
from jax.sharding import PartitionSpec as P

N = 4096
LANES = 128
SHORT = 32
OCT = 8
MASKS = 4
step_size = 0.2


def _split(table):
    high = table.astype(np.float32).astype(ml_dtypes.bfloat16)
    low = (table - high.astype(np.float64)).astype(np.float32).astype(ml_dtypes.bfloat16)
    return np.stack([high, low])


def exchange_order():
    index = np.arange(LANES).reshape(2, 4, 8, 2)
    return index.transpose(3, 0, 1, 2).reshape(LANES)


@functools.lru_cache(maxsize=None)
def tables():
    i128 = np.arange(LANES)
    w = np.exp(-2j * math.pi * (np.outer(i128, i128) % LANES) / LANES) / 64.0
    w = w[exchange_order()]
    left = np.block([[w.real, -w.imag], [w.imag, w.real]])
    inner = np.block([[w.real.T, -w.imag.T], [w.imag.T, w.real.T]])
    t = np.exp(-2j * math.pi * np.outer(np.arange(SHORT), i128) / N)
    row_tw = np.stack([t.real, t.imag]).astype(np.float32)
    rho = i128 % OCT
    row = np.arange(MASKS)[:, None] * OCT + rho[None, :]
    t = np.exp(-2j * math.pi * (i128[None, :, None] * row[:, None, :]) / N)
    col_tw = np.stack([t.real, t.imag])
    r8 = np.arange(OCT)
    big = np.kron(np.eye(16), np.exp(-2j * math.pi * np.outer(r8, r8) / 8))
    block = np.block([[big.real, big.imag], [-big.imag, big.real]])
    t = np.exp(-2j * math.pi * np.outer(np.arange(OCT), rho) / SHORT)
    col_tw = np.concatenate([col_tw.reshape(2, 4 * LANES, LANES), np.stack([t.real, t.imag])], axis=1)
    return dict(left=_split(left), inner=_split(inner), block=_split(block), row_tw=row_tw, col_tw=col_tw.astype(np.float32))


def split(x):
    high = x.astype(jnp.bfloat16)
    return high, (x - high.astype(jnp.float32)).astype(jnp.bfloat16)


def dot3(a, b, dims):
    dot = functools.partial(
        lax.dot_general, dimension_numbers=(dims, ((), ())), preferred_element_type=jnp.float32
    )
    return dot(a[0], b[0]) + (dot(a[0], b[1]) + dot(a[1], b[0]))


NN = ((1,), (0,))
NT = ((1,), (1,))
TN = ((0,), (0,))


def cmul(a, b):
    return a[0] * b[0] - a[1] * b[1], a[0] * b[1] + a[1] * b[0]


def cadd(a, b):
    return a[0] + b[0], a[1] + b[1]


def csub(a, b):
    return a[0] - b[0], a[1] - b[1]


def times_i(a, sign):
    return (-a[1], a[0]) if sign > 0 else (a[1], -a[0])


def rotate(a, turns, length, sign):
    turns = turns % length
    if turns == 0:
        return a
    eighths = turns * 8 % (length * 8) / length
    if eighths == 4:
        return -a[0], -a[1]
    if eighths == 2:
        return times_i(a, sign)
    if eighths == 6:
        return times_i(a, -sign)
    angle = sign * 2 * math.pi * turns / length
    c, s = float(np.float32(math.cos(angle))), float(np.float32(math.sin(angle)))
    if eighths in (1, 3, 5, 7):
        h = float(np.float32(math.sqrt(0.5)))
        cs, ss = (1 if c > 0 else -1), (1 if s > 0 else -1)
        re = (a[0] if cs > 0 else -a[0]) - (a[1] if ss > 0 else -a[1])
        im = (a[1] if cs > 0 else -a[1]) + (a[0] if ss > 0 else -a[0])
        return re * h, im * h
    return a[0] * c - a[1] * s, a[0] * s + a[1] * c


def fft4(x, sign):
    a, b = cadd(x[0], x[2]), csub(x[0], x[2])
    c, d = cadd(x[1], x[3]), times_i(csub(x[1], x[3]), sign)
    return [cadd(a, c), cadd(b, d), csub(a, c), csub(b, d)]


def fft8(x, sign):
    even, odd = fft4(x[0::2], sign), fft4(x[1::2], sign)
    odd = [rotate(o, j, 8, sign) for j, o in enumerate(odd)]
    return [cadd(u, v) for u, v in zip(even, odd)] + [csub(u, v) for u, v in zip(even, odd)]


def fft32(load, store, mid, sign):
    for p0 in range(8):
        y = fft4([load(8 * p1 + p0) for p1 in range(4)], sign)
        for k0 in range(4):
            v = rotate(y[k0], p0 * k0, 32, sign)
            mid[0, k0 * 8 + p0] = v[0]
            mid[1, k0 * 8 + p0] = v[1]
    for k0 in range(4):
        y = fft8([(mid[0, k0 * 8 + p0], mid[1, k0 * 8 + p0]) for p0 in range(8)], sign)
        for k1 in range(8):
            store(k0 + 4 * k1, y[k1])


def code_times(code, z):
    odd = (code & 1) == 1
    a = jnp.where(odd, z[1], z[0])
    b = jnp.where(odd, z[0], z[1])
    return jnp.where((code == 1) | (code == 2), -a, a), jnp.where(code >= 2, -b, b)


def conj_code_times(code, z):
    odd = (code & 1) == 1
    a = jnp.where(odd, z[1], z[0])
    b = jnp.where(odd, z[0], z[1])
    return jnp.where(code >= 2, -a, a), jnp.where((code == 1) | (code == 2), -b, b)


def rows_forward(index, obj, code, left, tw, out, c0, c2, c1, c3, mid, xs):
    m = pl.program_id(0)
    shift = lax.rem(m + MASKS - index[0], MASKS)
    for s, c in enumerate((c0, c1, c2, c3)):

        @pl.when(shift == s)
        def _():
            c[...] = code[0]

    def load(p):
        cols = slice(LANES * p, LANES * p + LANES)
        return code_times(code[0, :, cols], (obj[0, :, cols], obj[1, :, cols]))

    def store(k, v):
        v = cmul(v, (tw[0, k : k + 1], tw[1, k : k + 1]))
        xs[OCT * k : OCT * k + OCT, :LANES] = v[0]
        xs[OCT * k : OCT * k + OCT, LANES:] = v[1]

    fft32(load, store, mid, -1)
    y = dot3((left[0], left[1]), split(xs[...]), NT)
    for ri in range(2):
        for h in range(2):
            out[pl.ds(ri * 8 + 2 * m + h, LANES, stride=16), :] = y[
                LANES * ri : LANES * ri + LANES, LANES * h : LANES * h + LANES
            ]


def columns(rec, inten, inner, block, tw, out, s):
    def turned(e, sign):
        row = slice(4 * LANES + e, 4 * LANES + e + 1)
        return tw[0, row, :], sign * tw[1, row, :]

    for m in range(MASKS):
        x = jnp.concatenate(
            [
                jnp.concatenate(
                    [rec[pl.ds(ri * 8 + 2 * m + h, LANES, stride=16), :] for h in range(2)], axis=1
                )
                for ri in range(2)
            ],
            axis=0,
        )
        y = dot3((inner[0], inner[1]), split(x), NN)
        rows = slice(LANES * m, LANES * m + LANES)
        t = (tw[0, rows], tw[1, rows])
        for h in range(2):
            cols = slice(LANES * h, LANES * h + LANES)
            v = cmul((y[:LANES, cols], y[LANES:, cols]), t)
            s[m, 0, h] = v[0]
            s[m, 1, h] = v[1]

    for h in range(2):
        def turn(i, _):
            rows = pl.ds(pl.multiple_of(i * OCT, OCT), OCT)
            y = fft4([(s[m, 0, h, rows, :], s[m, 1, h, rows, :]) for m in range(4)], -1)
            for e in range(4):
                v = cmul(y[e], turned(e, 1)) if e else y[e]
                s[e, 0, h, rows, :] = v[0]
                s[e, 1, h, rows, :] = v[1]
            return 0

        lax.fori_loop(0, LANES // OCT, turn, 0, unroll=True)

    for e in range(4):
        x = jnp.concatenate(
            [jnp.concatenate([s[e, 0, h], s[e, 1, h]], axis=1) for h in range(2)], axis=0
        )
        y = dot3(split(x), (block[0], block[1]), NN)
        wr, wi = y[:, :LANES], y[:, LANES:]
        weight = wr * wr + wi * wi - inten[e]
        v = jnp.concatenate([wr * weight, wi * weight], axis=1)
        y = dot3(split(v), (block[0], block[1]), NT)
        for h in range(2):
            rows = slice(LANES * h, LANES * h + LANES)
            s[e, 0, h] = y[rows, :LANES]
            s[e, 1, h] = y[rows, LANES:]

    for h in range(2):
        def turn_back(i, _):
            rows = pl.ds(pl.multiple_of(i * OCT, OCT), OCT)
            x = [(s[e, 0, h, rows, :], s[e, 1, h, rows, :]) for e in range(4)]
            y = fft4([cmul(v, turned(e, -1)) if e else v for e, v in enumerate(x)], 1)
            for m in range(4):
                near = pl.ds(pl.multiple_of(LANES * m + i * OCT, OCT), OCT)
                v = cmul(y[m], (tw[0, near, :], -tw[1, near, :]))
                s[m, 0, h, rows, :] = v[0]
                s[m, 1, h, rows, :] = v[1]
            return 0

        lax.fori_loop(0, LANES // OCT, turn_back, 0, unroll=True)

    for m in range(MASKS):
        x = jnp.concatenate(
            [jnp.concatenate([s[m, ri, 0], s[m, ri, 1]], axis=1) for ri in range(2)], axis=0
        )
        y = dot3((inner[0], inner[1]), split(x), TN)
        for ri in range(2):
            for h in range(2):
                out[pl.ds(m * 4 + ri * 2 + h, LANES, stride=16), :] = y[
                    LANES * ri : LANES * ri + LANES, LANES * h : LANES * h + LANES
                ]


def rows_back(index, rec, c0, c1, c2, c3, left, tw, out, mid, ys):
    for s, code in enumerate((c0, c1, c2, c3)):
        l = lax.rem(index[0] + MASKS - s, MASKS)
        x = jnp.concatenate(
            [
                jnp.concatenate(
                    [
                        rec[pl.ds(l * 4 + ri * 2 + h, LANES, stride=16), :].T
                        for ri in range(2)
                    ],
                    axis=1,
                )
                for h in range(2)
            ],
            axis=0,
        )
        ys[...] = dot3(split(x), (left[0], left[1]), NN)

        def load(k):
            rows = slice(OCT * k, OCT * k + OCT)
            return cmul((ys[rows, :LANES], ys[rows, LANES:]), (tw[0, k : k + 1], -tw[1, k : k + 1]))

        def store(p, v):
            cols = slice(LANES * p, LANES * p + LANES)
            v = conj_code_times(code[:, cols], v)
            for ri in range(2):
                if s == 0:
                    out[0, ri, :, cols] = v[ri]
                elif s < MASKS - 1:
                    out[0, ri, :, cols] += v[ri]
                else:
                    total = (out[0, ri, :, cols] + v[ri]) * (1.0 / MASKS)
                    for copy in range(MASKS):
                        out[copy, ri, :, cols] = total

        fft32(load, store, mid, 1)


def finish(parts, obj, updated, direction):
    for m in range(MASKS):
        rows = slice(OCT * m, OCT * m + OCT)
        for ri in range(2):
            value = parts[m, ri]
            direction[ri, rows, :] = value
            updated[ri, rows, :] = obj[ri, rows, :] - step_size * value


VM = pl.BlockSpec(memory_space=pltpu.VMEM)
F32 = jnp.float32


def call(kernel, name, out_shape, n_in, scratch, flops, vmem=24, smem=()):
    specs = [VM] * n_in
    for i in smem:
        specs[i] = pl.BlockSpec(memory_space=pltpu.SMEM)
    outs = jax.tree.map(lambda _: VM, out_shape)
    return pl.pallas_call(
        kernel,
        name=name,
        out_shape=out_shape,
        in_specs=specs,
        out_specs=outs,
        scratch_shapes=scratch,
        compiler_params=pltpu.CompilerParams(vmem_limit_bytes=vmem << 20),
        cost_estimate=pl.CostEstimate(flops=flops, bytes_accessed=3 << 20, transcendentals=0),
    )


def body(object_field, phases, intensity):
    t = {k: jnp.asarray(v) for k, v in tables().items()}
    sds = jax.ShapeDtypeStruct
    index = lax.axis_index("mask").astype(jnp.int32).reshape(1)
    octet = lambda m: (0, m, 0)
    flat = lambda m: (0, 0)
    rows8 = sds((OCT, N), jnp.int32)
    sent, c0, c2, c1, c3 = pl.pallas_call(
        rows_forward,
        name="rows_forward",
        out_shape=(sds((2048, LANES), F32),) + (rows8,) * MASKS,
        grid=(MASKS,),
        in_specs=[
            pl.BlockSpec(memory_space=pltpu.SMEM),
            pl.BlockSpec((2, OCT, N), octet),
            pl.BlockSpec((1, OCT, N), octet),
            pl.BlockSpec((2, 256, 256), lambda m: (0, 0, 0)),
            pl.BlockSpec((2, SHORT, LANES), lambda m: (0, 0, 0)),
        ],
        out_specs=(pl.BlockSpec((2048, LANES), flat),) + (pl.BlockSpec((OCT, N), flat),) * MASKS,
        scratch_shapes=[
            pltpu.VMEM((2, SHORT, OCT, LANES), F32),
            pltpu.VMEM((256, 256), F32),
        ],
        compiler_params=pltpu.CompilerParams(vmem_limit_bytes=60 << 20),
        cost_estimate=pl.CostEstimate(flops=1 << 29, bytes_accessed=3 << 20, transcendentals=0),
    )(index, object_field, phases, t["left"], t["row_tw"])
    inten = intensity.reshape(2, 16, 8, 4, LANES).transpose(3, 0, 4, 1, 2).reshape(4, 256, LANES)
    up = [(i, (i + 1) % MASKS) for i in range(MASKS)]
    down = [((i + 1) % MASKS, i) for i in range(MASKS)]
    across = [(i, (i + 2) % MASKS) for i in range(MASKS)]
    order = [int(i) for i in exchange_order()]
    every = [m * LANES + i for i in order for m in range(MASKS)]
    exchange = functools.partial(lax.all_to_all, split_axis=0, concat_axis=0, tiled=True)
    rec = exchange(sent.reshape(LANES, 16, LANES), "rows", axis_index_groups=[order])
    g1 = lax.ppermute(c1, "mask", up)
    g2 = lax.ppermute(c2, "mask", across)
    g3 = lax.ppermute(c3, "mask", down)
    back = call(
        columns, "columns", sds((2048, LANES), F32), 5,
        [pltpu.VMEM((4, 2, 2, LANES, LANES), F32)], 3 << 29,
    )(rec.reshape(2048, LANES), inten, t["inner"], t["block"], t["col_tw"])
    back, g2, g1, g3 = lax.optimization_barrier((back, g2, g1, g3))
    rec = exchange(back.reshape(512, 4, LANES), ("mask", "rows"), axis_index_groups=[every])
    part = call(
        rows_back, "rows_back", sds((MASKS, 2, OCT, N), F32), 8,
        [pltpu.VMEM((2, SHORT, OCT, LANES), F32), pltpu.VMEM((256, 256), F32)], 1 << 29, smem=(0,),
    )(index, rec.reshape(2048, LANES), c0, g1, g2, g3, t["left"], t["row_tw"])
    parts = exchange(part, "mask")
    whole = sds((2, SHORT, N), F32)
    return call(finish, "finish", (whole, whole), 2, [], 1 << 20)(parts, object_field)


def solution(mesh):
    return jax.shard_map(
        body,
        mesh=mesh,
        in_specs=(P(None, "rows", None), P("mask", "rows", None), P("mask", "rows", None)),
        out_specs=(P(None, "rows", None), P(None, "rows", None)),
        check_vma=False,
    )
```

```python
import functools
import math

import jax
import jax.numpy as jnp
import ml_dtypes
import numpy as np
from jax import lax
from jax.experimental import pallas as pl
from jax.experimental.pallas import tpu as pltpu
from jax.sharding import PartitionSpec as P

N = 4096
LANES = 128
SHORT = 32
OCT = 8
MASKS = 4
step_size = 0.2


def _split(table):
    high = table.astype(np.float32).astype(ml_dtypes.bfloat16)
    low = (table - high.astype(np.float64)).astype(np.float32).astype(ml_dtypes.bfloat16)
    return np.stack([high, low])


def exchange_order():
    index = np.arange(LANES).reshape(2, 4, 8, 2)
    return index.transpose(0, 1, 3, 2).reshape(LANES)


@functools.lru_cache(maxsize=None)
def tables():
    i128 = np.arange(LANES)
    w = np.exp(-2j * math.pi * (np.outer(i128, i128) % LANES) / LANES) / 64.0
    w = w[exchange_order()]
    left = np.block([[w.real, -w.imag], [w.imag, w.real]])
    inner = np.block([[w.real.T, -w.imag.T], [w.imag.T, w.real.T]])
    t = np.exp(-2j * math.pi * np.outer(np.arange(SHORT), i128) / N)
    row_tw = np.stack([t.real, t.imag]).astype(np.float32)
    rho = i128 % OCT
    row = np.arange(MASKS)[:, None] * OCT + rho[None, :]
    t = np.exp(-2j * math.pi * (i128[None, :, None] * row[:, None, :]) / N)
    col_tw = np.stack([t.real, t.imag])
    r8 = np.arange(OCT)
    big = np.kron(np.eye(16), np.exp(-2j * math.pi * np.outer(r8, r8) / 8))
    block = np.block([[big.real, big.imag], [-big.imag, big.real]])
    t = np.exp(-2j * math.pi * np.outer(np.arange(OCT), rho) / SHORT)
    col_tw = np.concatenate([col_tw.reshape(2, 4 * LANES, LANES), np.stack([t.real, t.imag])], axis=1)
    return dict(left=_split(left), inner=_split(inner), block=_split(block), row_tw=row_tw, col_tw=col_tw.astype(np.float32))


def split(x):
    high = x.astype(jnp.bfloat16)
    return high, (x - high.astype(jnp.float32)).astype(jnp.bfloat16)


def dot3(a, b, dims):
    dot = functools.partial(
        lax.dot_general, dimension_numbers=(dims, ((), ())), preferred_element_type=jnp.float32
    )
    return dot(a[0], b[0]) + (dot(a[0], b[1]) + dot(a[1], b[0]))


NN = ((1,), (0,))
NT = ((1,), (1,))
TN = ((0,), (0,))


def cmul(a, b):
    return a[0] * b[0] - a[1] * b[1], a[0] * b[1] + a[1] * b[0]


def cadd(a, b):
    return a[0] + b[0], a[1] + b[1]


def csub(a, b):
    return a[0] - b[0], a[1] - b[1]


def times_i(a, sign):
    return (-a[1], a[0]) if sign > 0 else (a[1], -a[0])


def rotate(a, turns, length, sign):
    turns = turns % length
    if turns == 0:
        return a
    eighths = turns * 8 % (length * 8) / length
    if eighths == 4:
        return -a[0], -a[1]
    if eighths == 2:
        return times_i(a, sign)
    if eighths == 6:
        return times_i(a, -sign)
    angle = sign * 2 * math.pi * turns / length
    c, s = float(np.float32(math.cos(angle))), float(np.float32(math.sin(angle)))
    if eighths in (1, 3, 5, 7):
        h = float(np.float32(math.sqrt(0.5)))
        cs, ss = (1 if c > 0 else -1), (1 if s > 0 else -1)
        re = (a[0] if cs > 0 else -a[0]) - (a[1] if ss > 0 else -a[1])
        im = (a[1] if cs > 0 else -a[1]) + (a[0] if ss > 0 else -a[0])
        return re * h, im * h
    return a[0] * c - a[1] * s, a[0] * s + a[1] * c


def fft4(x, sign):
    a, b = cadd(x[0], x[2]), csub(x[0], x[2])
    c, d = cadd(x[1], x[3]), times_i(csub(x[1], x[3]), sign)
    return [cadd(a, c), cadd(b, d), csub(a, c), csub(b, d)]


def fft8(x, sign):
    even, odd = fft4(x[0::2], sign), fft4(x[1::2], sign)
    odd = [rotate(o, j, 8, sign) for j, o in enumerate(odd)]
    return [cadd(u, v) for u, v in zip(even, odd)] + [csub(u, v) for u, v in zip(even, odd)]


def fft32(load, store, mid, sign):
    for p0 in range(8):
        y = fft4([load(8 * p1 + p0) for p1 in range(4)], sign)
        for k0 in range(4):
            v = rotate(y[k0], p0 * k0, 32, sign)
            mid[0, k0 * 8 + p0] = v[0]
            mid[1, k0 * 8 + p0] = v[1]
    for k0 in range(4):
        y = fft8([(mid[0, k0 * 8 + p0], mid[1, k0 * 8 + p0]) for p0 in range(8)], sign)
        for k1 in range(8):
            store(k0 + 4 * k1, y[k1])


def code_times(code, z):
    odd = (code & 1) == 1
    a = jnp.where(odd, z[1], z[0])
    b = jnp.where(odd, z[0], z[1])
    return jnp.where((code == 1) | (code == 2), -a, a), jnp.where(code >= 2, -b, b)


def conj_code_times(code, z):
    odd = (code & 1) == 1
    a = jnp.where(odd, z[1], z[0])
    b = jnp.where(odd, z[0], z[1])
    return jnp.where(code >= 2, -a, a), jnp.where((code == 1) | (code == 2), -b, b)


def rows_forward(index, obj, code, left, tw, out, c0, c2, c1, c3, mid, xs):
    m = pl.program_id(0)
    shift = lax.rem(m + MASKS - index[0], MASKS)
    for s, c in enumerate((c0, c1, c2, c3)):

        @pl.when(shift == s)
        def _():
            c[...] = code[0]

    def load(p):
        cols = slice(LANES * p, LANES * p + LANES)
        return code_times(code[0, :, cols], (obj[0, :, cols], obj[1, :, cols]))

    def store(k, v):
        v = cmul(v, (tw[0, k : k + 1], tw[1, k : k + 1]))
        xs[OCT * k : OCT * k + OCT, :LANES] = v[0]
        xs[OCT * k : OCT * k + OCT, LANES:] = v[1]

    fft32(load, store, mid, -1)
    y = dot3((left[0], left[1]), split(xs[...]), NT)
    for ri in range(2):
        for h in range(2):
            out[pl.ds(ri * 8 + 2 * m + h, LANES, stride=16), :] = y[
                LANES * ri : LANES * ri + LANES, LANES * h : LANES * h + LANES
            ]


def columns(rec, inten, inner, block, tw, out, s):
    def turned(e, sign):
        row = slice(4 * LANES + e, 4 * LANES + e + 1)
        return tw[0, row, :], sign * tw[1, row, :]

    for m in range(MASKS):
        x = jnp.concatenate(
            [
                jnp.concatenate(
                    [rec[pl.ds(ri * 8 + 2 * m + h, LANES, stride=16), :] for h in range(2)], axis=1
                )
                for ri in range(2)
            ],
            axis=0,
        )
        y = dot3((inner[0], inner[1]), split(x), NN)
        rows = slice(LANES * m, LANES * m + LANES)
        t = (tw[0, rows], tw[1, rows])
        for h in range(2):
            cols = slice(LANES * h, LANES * h + LANES)
            v = cmul((y[:LANES, cols], y[LANES:, cols]), t)
            s[m, 0, h] = v[0]
            s[m, 1, h] = v[1]

    for h in range(2):
        def turn(i, _):
            rows = pl.ds(pl.multiple_of(i * OCT, OCT), OCT)
            y = fft4([(s[m, 0, h, rows, :], s[m, 1, h, rows, :]) for m in range(4)], -1)
            for e in range(4):
                v = cmul(y[e], turned(e, 1)) if e else y[e]
                s[e, 0, h, rows, :] = v[0]
                s[e, 1, h, rows, :] = v[1]
            return 0

        lax.fori_loop(0, LANES // OCT, turn, 0, unroll=True)

    for e in range(4):
        x = jnp.concatenate(
            [jnp.concatenate([s[e, 0, h], s[e, 1, h]], axis=1) for h in range(2)], axis=0
        )
        y = dot3(split(x), (block[0], block[1]), NN)
        wr, wi = y[:, :LANES], y[:, LANES:]
        weight = wr * wr + wi * wi - inten[e]
        v = jnp.concatenate([wr * weight, wi * weight], axis=1)
        y = dot3(split(v), (block[0], block[1]), NT)
        for h in range(2):
            rows = slice(LANES * h, LANES * h + LANES)
            s[e, 0, h] = y[rows, :LANES]
            s[e, 1, h] = y[rows, LANES:]

    for h in range(2):
        def turn_back(i, _):
            rows = pl.ds(pl.multiple_of(i * OCT, OCT), OCT)
            x = [(s[e, 0, h, rows, :], s[e, 1, h, rows, :]) for e in range(4)]
            y = fft4([cmul(v, turned(e, -1)) if e else v for e, v in enumerate(x)], 1)
            for m in range(4):
                near = pl.ds(pl.multiple_of(LANES * m + i * OCT, OCT), OCT)
                v = cmul(y[m], (tw[0, near, :], -tw[1, near, :]))
                s[m, 0, h, rows, :] = v[0]
                s[m, 1, h, rows, :] = v[1]
            return 0

        lax.fori_loop(0, LANES // OCT, turn_back, 0, unroll=True)

    for m in range(MASKS):
        x = jnp.concatenate(
            [jnp.concatenate([s[m, ri, 0], s[m, ri, 1]], axis=1) for ri in range(2)], axis=0
        )
        y = dot3((inner[0], inner[1]), split(x), TN)
        for ri in range(2):
            for h in range(2):
                out[pl.ds(m * 4 + ri * 2 + h, LANES, stride=16), :] = y[
                    LANES * ri : LANES * ri + LANES, LANES * h : LANES * h + LANES
                ]


def rows_back(index, rec, c0, c1, c2, c3, left, tw, out, mid, ys):
    for s, code in enumerate((c0, c1, c2, c3)):
        l = lax.rem(index[0] + MASKS - s, MASKS)
        x = jnp.concatenate(
            [
                jnp.concatenate(
                    [
                        rec[pl.ds(l * 4 + ri * 2 + h, LANES, stride=16), :].T
                        for ri in range(2)
                    ],
                    axis=1,
                )
                for h in range(2)
            ],
            axis=0,
        )
        ys[...] = dot3(split(x), (left[0], left[1]), NN)

        def load(k):
            rows = slice(OCT * k, OCT * k + OCT)
            return cmul((ys[rows, :LANES], ys[rows, LANES:]), (tw[0, k : k + 1], -tw[1, k : k + 1]))

        def store(p, v):
            cols = slice(LANES * p, LANES * p + LANES)
            v = conj_code_times(code[:, cols], v)
            for ri in range(2):
                if s == 0:
                    out[ri, :, cols] = v[ri]
                elif s < MASKS - 1:
                    out[ri, :, cols] += v[ri]
                else:
                    out[ri, :, cols] = (out[ri, :, cols] + v[ri]) * (1.0 / MASKS)

        fft32(load, store, mid, 1)


def finish(masks, own, near, far, other, obj, updated, direction):
    for i, part in enumerate((own, near, far, other)):
        rows = pl.ds(pl.multiple_of(masks[i] * OCT, OCT), OCT)
        for ri in range(2):
            value = part[ri]
            direction[ri, rows, :] = value
            updated[ri, rows, :] = obj[ri, rows, :] - step_size * value


VM = pl.BlockSpec(memory_space=pltpu.VMEM)
F32 = jnp.float32


def call(kernel, name, out_shape, n_in, scratch, flops, vmem=24, smem=()):
    specs = [VM] * n_in
    for i in smem:
        specs[i] = pl.BlockSpec(memory_space=pltpu.SMEM)
    outs = jax.tree.map(lambda _: VM, out_shape)
    return pl.pallas_call(
        kernel,
        name=name,
        out_shape=out_shape,
        in_specs=specs,
        out_specs=outs,
        scratch_shapes=scratch,
        compiler_params=pltpu.CompilerParams(vmem_limit_bytes=vmem << 20),
        cost_estimate=pl.CostEstimate(flops=flops, bytes_accessed=3 << 20, transcendentals=0),
    )


def body(object_field, phases, intensity):
    t = {k: jnp.asarray(v) for k, v in tables().items()}
    sds = jax.ShapeDtypeStruct
    index = lax.axis_index("mask").astype(jnp.int32).reshape(1)
    octet = lambda m: (0, m, 0)
    flat = lambda m: (0, 0)
    rows8 = sds((OCT, N), jnp.int32)
    sent, c0, c2, c1, c3 = pl.pallas_call(
        rows_forward,
        name="rows_forward",
        out_shape=(sds((2048, LANES), F32),) + (rows8,) * MASKS,
        grid=(MASKS,),
        in_specs=[
            pl.BlockSpec(memory_space=pltpu.SMEM),
            pl.BlockSpec((2, OCT, N), octet),
            pl.BlockSpec((1, OCT, N), octet),
            pl.BlockSpec((2, 256, 256), lambda m: (0, 0, 0)),
            pl.BlockSpec((2, SHORT, LANES), lambda m: (0, 0, 0)),
        ],
        out_specs=(pl.BlockSpec((2048, LANES), flat),) + (pl.BlockSpec((OCT, N), flat),) * MASKS,
        scratch_shapes=[
            pltpu.VMEM((2, SHORT, OCT, LANES), F32),
            pltpu.VMEM((256, 256), F32),
        ],
        compiler_params=pltpu.CompilerParams(vmem_limit_bytes=60 << 20),
        cost_estimate=pl.CostEstimate(flops=1 << 29, bytes_accessed=3 << 20, transcendentals=0),
    )(index, object_field, phases, t["left"], t["row_tw"])
    inten = intensity.reshape(2, 16, 8, 4, LANES).transpose(3, 0, 4, 1, 2).reshape(4, 256, LANES)
    up = [(i, (i + 1) % MASKS) for i in range(MASKS)]
    down = [((i + 1) % MASKS, i) for i in range(MASKS)]
    across = [(i, (i + 2) % MASKS) for i in range(MASKS)]
    order = [int(i) for i in exchange_order()]
    every = [m * LANES + i for i in order for m in range(MASKS)]
    exchange = functools.partial(lax.all_to_all, split_axis=0, concat_axis=0, tiled=True)
    rec = exchange(sent.reshape(LANES, 16, LANES), "rows", axis_index_groups=[order])
    g1 = lax.ppermute(c1, "mask", up)
    g2 = lax.ppermute(c2, "mask", across)
    g3 = lax.ppermute(c3, "mask", down)
    back = call(
        columns, "columns", sds((2048, LANES), F32), 5,
        [pltpu.VMEM((4, 2, 2, LANES, LANES), F32)], 3 << 29,
    )(rec.reshape(2048, LANES), inten, t["inner"], t["block"], t["col_tw"])
    back, g2, g1, g3 = lax.optimization_barrier((back, g2, g1, g3))
    rec = exchange(back.reshape(512, 4, LANES), ("mask", "rows"), axis_index_groups=[every])
    part = call(
        rows_back, "rows_back", sds((2, OCT, N), F32), 8,
        [pltpu.VMEM((2, SHORT, OCT, LANES), F32), pltpu.VMEM((256, 256), F32)], 1 << 29, smem=(0,),
    )(index, rec.reshape(2048, LANES), c0, g1, g2, g3, t["left"], t["row_tw"])
    ring = [
        (m * LANES + r, (m + 1 - 2 * (r % 2)) % MASKS * LANES + r)
        for m in range(MASKS)
        for r in range(LANES)
    ]
    swap = [(r, r ^ 1) for r in range(LANES)]
    near = lax.ppermute(part, ("mask", "rows"), ring)
    partner = lax.ppermute(part, "rows", swap)
    passed = lax.ppermute(partner, ("mask", "rows"), ring)
    far = lax.ppermute(near, ("mask", "rows"), ring)
    other = lax.ppermute(passed, "rows", swap)
    side = 2 * (lax.axis_index("rows").astype(jnp.int32) % 2) - 1
    me = index[0] + MASKS
    masks = jnp.stack([me, me + side, me + 2, me - side]) % MASKS
    whole = sds((2, SHORT, N), F32)
    return call(finish, "finish", (whole, whole), 6, [], 1 << 20, smem=(0,))(
        masks, part, near, far, other, object_field
    )


def solution(mesh):
    return jax.shard_map(
        body,
        mesh=mesh,
        in_specs=(P(None, "rows", None), P("mask", "rows", None), P("mask", "rows", None)),
        out_specs=(P(None, "rows", None), P(None, "rows", None)),
        check_vma=False,
    )
```

```python
import functools
import math

import jax
import jax.numpy as jnp
import ml_dtypes
import numpy as np
from jax import lax
from jax.experimental import pallas as pl
from jax.experimental.pallas import tpu as pltpu
from jax.sharding import PartitionSpec as P

N = 4096
LANES = 128
SHORT = 32
OCT = 8
MASKS = 4
step_size = 0.2


def _split(table):
    high = table.astype(np.float32).astype(ml_dtypes.bfloat16)
    low = (table - high.astype(np.float64)).astype(np.float32).astype(ml_dtypes.bfloat16)
    return np.stack([high, low])


def exchange_order():
    index = np.arange(LANES).reshape(2, 4, 8, 2)
    return index.transpose(0, 1, 3, 2).reshape(LANES)


@functools.lru_cache(maxsize=None)
def tables():
    i128 = np.arange(LANES)
    w = np.exp(-2j * math.pi * (np.outer(i128, i128) % LANES) / LANES) / 64.0
    w = w[exchange_order()]
    left = np.block([[w.real, -w.imag], [w.imag, w.real]])
    inner = np.block([[w.real.T, -w.imag.T], [w.imag.T, w.real.T]])
    t = np.exp(-2j * math.pi * np.outer(np.arange(SHORT), i128) / N)
    row_tw = np.stack([t.real, t.imag]).astype(np.float32)
    rho = i128 % OCT
    row = np.arange(MASKS)[:, None] * OCT + rho[None, :]
    t = np.exp(-2j * math.pi * (i128[None, :, None] * row[:, None, :]) / N)
    col_tw = np.stack([t.real, t.imag])
    r8 = np.arange(OCT)
    big = np.kron(np.eye(16), np.exp(-2j * math.pi * np.outer(r8, r8) / 8))
    block = np.block([[big.real, big.imag], [-big.imag, big.real]])
    t = np.exp(-2j * math.pi * np.outer(np.arange(OCT), rho) / SHORT)
    col_tw = np.concatenate([col_tw.reshape(2, 4 * LANES, LANES), np.stack([t.real, t.imag])], axis=1)
    return dict(left=_split(left), inner=_split(inner), block=_split(block), row_tw=row_tw, col_tw=col_tw.astype(np.float32))


def split(x):
    high = x.astype(jnp.bfloat16)
    return high, (x - high.astype(jnp.float32)).astype(jnp.bfloat16)


def dot3(a, b, dims):
    dot = functools.partial(
        lax.dot_general, dimension_numbers=(dims, ((), ())), preferred_element_type=jnp.float32
    )
    return dot(a[0], b[0]) + (dot(a[0], b[1]) + dot(a[1], b[0]))


NN = ((1,), (0,))
NT = ((1,), (1,))
TN = ((0,), (0,))


def cmul(a, b):
    return a[0] * b[0] - a[1] * b[1], a[0] * b[1] + a[1] * b[0]


def cadd(a, b):
    return a[0] + b[0], a[1] + b[1]


def csub(a, b):
    return a[0] - b[0], a[1] - b[1]


def times_i(a, sign):
    return (-a[1], a[0]) if sign > 0 else (a[1], -a[0])


def rotate(a, turns, length, sign):
    turns = turns % length
    if turns == 0:
        return a
    eighths = turns * 8 % (length * 8) / length
    if eighths == 4:
        return -a[0], -a[1]
    if eighths == 2:
        return times_i(a, sign)
    if eighths == 6:
        return times_i(a, -sign)
    angle = sign * 2 * math.pi * turns / length
    c, s = float(np.float32(math.cos(angle))), float(np.float32(math.sin(angle)))
    if eighths in (1, 3, 5, 7):
        h = float(np.float32(math.sqrt(0.5)))
        cs, ss = (1 if c > 0 else -1), (1 if s > 0 else -1)
        re = (a[0] if cs > 0 else -a[0]) - (a[1] if ss > 0 else -a[1])
        im = (a[1] if cs > 0 else -a[1]) + (a[0] if ss > 0 else -a[0])
        return re * h, im * h
    return a[0] * c - a[1] * s, a[0] * s + a[1] * c


def fft4(x, sign):
    a, b = cadd(x[0], x[2]), csub(x[0], x[2])
    c, d = cadd(x[1], x[3]), times_i(csub(x[1], x[3]), sign)
    return [cadd(a, c), cadd(b, d), csub(a, c), csub(b, d)]


def fft8(x, sign):
    even, odd = fft4(x[0::2], sign), fft4(x[1::2], sign)
    odd = [rotate(o, j, 8, sign) for j, o in enumerate(odd)]
    return [cadd(u, v) for u, v in zip(even, odd)] + [csub(u, v) for u, v in zip(even, odd)]


def fft32(load, store, mid, sign):
    for p0 in range(8):
        y = fft4([load(8 * p1 + p0) for p1 in range(4)], sign)
        for k0 in range(4):
            v = rotate(y[k0], p0 * k0, 32, sign)
            mid[0, k0 * 8 + p0] = v[0]
            mid[1, k0 * 8 + p0] = v[1]
    for k0 in range(4):
        y = fft8([(mid[0, k0 * 8 + p0], mid[1, k0 * 8 + p0]) for p0 in range(8)], sign)
        for k1 in range(8):
            store(k0 + 4 * k1, y[k1])


def code_times(code, z):
    odd = (code & 1) == 1
    a = jnp.where(odd, z[1], z[0])
    b = jnp.where(odd, z[0], z[1])
    return jnp.where((code == 1) | (code == 2), -a, a), jnp.where(code >= 2, -b, b)


def conj_code_times(code, z):
    odd = (code & 1) == 1
    a = jnp.where(odd, z[1], z[0])
    b = jnp.where(odd, z[0], z[1])
    return jnp.where(code >= 2, -a, a), jnp.where((code == 1) | (code == 2), -b, b)


def rows_forward(index, obj, code, left, tw, out, c0, c2, c1, c3, mid, xs):
    m = pl.program_id(0)
    shift = lax.rem(m + MASKS - index[0], MASKS)
    for s, c in enumerate((c0, c1, c2, c3)):

        @pl.when(shift == s)
        def _():
            c[...] = code[0]

    def load(p):
        cols = slice(LANES * p, LANES * p + LANES)
        return code_times(code[0, :, cols], (obj[0, :, cols], obj[1, :, cols]))

    def store(k, v):
        v = cmul(v, (tw[0, k : k + 1], tw[1, k : k + 1]))
        xs[OCT * k : OCT * k + OCT, :LANES] = v[0]
        xs[OCT * k : OCT * k + OCT, LANES:] = v[1]

    fft32(load, store, mid, -1)
    y = dot3((left[0], left[1]), split(xs[...]), NT)
    for ri in range(2):
        for h in range(2):
            out[pl.ds(ri * 8 + 2 * m + h, LANES, stride=16), :] = y[
                LANES * ri : LANES * ri + LANES, LANES * h : LANES * h + LANES
            ]


def columns(rec, inten, inner, block, tw, out, s):
    def turned(e, sign):
        row = slice(4 * LANES + e, 4 * LANES + e + 1)
        return tw[0, row, :], sign * tw[1, row, :]

    for m in range(MASKS):
        x = jnp.concatenate(
            [
                jnp.concatenate(
                    [rec[pl.ds(ri * 8 + 2 * m + h, LANES, stride=16), :] for h in range(2)], axis=1
                )
                for ri in range(2)
            ],
            axis=0,
        )
        y = dot3((inner[0], inner[1]), split(x), NN)
        rows = slice(LANES * m, LANES * m + LANES)
        t = (tw[0, rows], tw[1, rows])
        for h in range(2):
            cols = slice(LANES * h, LANES * h + LANES)
            v = cmul((y[:LANES, cols], y[LANES:, cols]), t)
            s[m, 0, h] = v[0]
            s[m, 1, h] = v[1]

    for h in range(2):
        def turn(i, _):
            rows = pl.ds(pl.multiple_of(i * OCT, OCT), OCT)
            y = fft4([(s[m, 0, h, rows, :], s[m, 1, h, rows, :]) for m in range(4)], -1)
            for e in range(4):
                v = cmul(y[e], turned(e, 1)) if e else y[e]
                s[e, 0, h, rows, :] = v[0]
                s[e, 1, h, rows, :] = v[1]
            return 0

        lax.fori_loop(0, LANES // OCT, turn, 0, unroll=True)

    for e in range(4):
        x = jnp.concatenate(
            [jnp.concatenate([s[e, 0, h], s[e, 1, h]], axis=1) for h in range(2)], axis=0
        )
        y = dot3(split(x), (block[0], block[1]), NN)
        wr, wi = y[:, :LANES], y[:, LANES:]
        weight = wr * wr + wi * wi - inten[e]
        v = jnp.concatenate([wr * weight, wi * weight], axis=1)
        y = dot3(split(v), (block[0], block[1]), NT)
        for h in range(2):
            rows = slice(LANES * h, LANES * h + LANES)
            s[e, 0, h] = y[rows, :LANES]
            s[e, 1, h] = y[rows, LANES:]

    for h in range(2):
        def turn_back(i, _):
            rows = pl.ds(pl.multiple_of(i * OCT, OCT), OCT)
            x = [(s[e, 0, h, rows, :], s[e, 1, h, rows, :]) for e in range(4)]
            y = fft4([cmul(v, turned(e, -1)) if e else v for e, v in enumerate(x)], 1)
            for m in range(4):
                near = pl.ds(pl.multiple_of(LANES * m + i * OCT, OCT), OCT)
                v = cmul(y[m], (tw[0, near, :], -tw[1, near, :]))
                s[m, 0, h, rows, :] = v[0]
                s[m, 1, h, rows, :] = v[1]
            return 0

        lax.fori_loop(0, LANES // OCT, turn_back, 0, unroll=True)

    for m in range(MASKS):
        x = jnp.concatenate(
            [jnp.concatenate([s[m, ri, 0], s[m, ri, 1]], axis=1) for ri in range(2)], axis=0
        )
        y = dot3((inner[0], inner[1]), split(x), TN)
        for ri in range(2):
            for h in range(2):
                out[pl.ds(m * 4 + ri * 2 + h, LANES, stride=16), :] = y[
                    LANES * ri : LANES * ri + LANES, LANES * h : LANES * h + LANES
                ]


def rows_back(index, rec, c0, c1, c2, c3, left, tw, out, out_re, out_im, mid, ys):
    for s, code in enumerate((c0, c1, c2, c3)):
        l = lax.rem(index[0] + MASKS - s, MASKS)
        x = jnp.concatenate(
            [
                jnp.concatenate(
                    [
                        rec[pl.ds(l * 4 + ri * 2 + h, LANES, stride=16), :].T
                        for ri in range(2)
                    ],
                    axis=1,
                )
                for h in range(2)
            ],
            axis=0,
        )
        ys[...] = dot3(split(x), (left[0], left[1]), NN)

        def load(k):
            rows = slice(OCT * k, OCT * k + OCT)
            return cmul((ys[rows, :LANES], ys[rows, LANES:]), (tw[0, k : k + 1], -tw[1, k : k + 1]))

        def store(p, v):
            cols = slice(LANES * p, LANES * p + LANES)
            v = conj_code_times(code[:, cols], v)
            for ri in range(2):
                if s == 0:
                    out[ri, :, cols] = v[ri]
                elif s < MASKS - 1:
                    out[ri, :, cols] += v[ri]
                else:
                    total = (out[ri, :, cols] + v[ri]) * (1.0 / MASKS)
                    out[ri, :, cols] = total
                    (out_re, out_im)[ri][:, cols] = total

        fft32(load, store, mid, 1)


def finish(masks, own_re, own_im, near_re, near_im, far_re, far_im, other, obj, updated, direction):
    parts = ((own_re, own_im), (near_re, near_im), (far_re, far_im), (other.at[0], other.at[1]))
    for i, part in enumerate(parts):
        rows = pl.ds(pl.multiple_of(masks[i] * OCT, OCT), OCT)
        for ri in range(2):
            value = part[ri][...]
            direction[ri, rows, :] = value
            updated[ri, rows, :] = obj[ri, rows, :] - step_size * value


VM = pl.BlockSpec(memory_space=pltpu.VMEM)
F32 = jnp.float32


def call(kernel, name, out_shape, n_in, scratch, flops, vmem=24, smem=()):
    specs = [VM] * n_in
    for i in smem:
        specs[i] = pl.BlockSpec(memory_space=pltpu.SMEM)
    outs = jax.tree.map(lambda _: VM, out_shape)
    return pl.pallas_call(
        kernel,
        name=name,
        out_shape=out_shape,
        in_specs=specs,
        out_specs=outs,
        scratch_shapes=scratch,
        compiler_params=pltpu.CompilerParams(vmem_limit_bytes=vmem << 20),
        cost_estimate=pl.CostEstimate(flops=flops, bytes_accessed=3 << 20, transcendentals=0),
    )


def body(object_field, phases, intensity):
    t = {k: jnp.asarray(v) for k, v in tables().items()}
    sds = jax.ShapeDtypeStruct
    index = lax.axis_index("mask").astype(jnp.int32).reshape(1)
    octet = lambda m: (0, m, 0)
    flat = lambda m: (0, 0)
    rows8 = sds((OCT, N), jnp.int32)
    sent, c0, c2, c1, c3 = pl.pallas_call(
        rows_forward,
        name="rows_forward",
        out_shape=(sds((2048, LANES), F32),) + (rows8,) * MASKS,
        grid=(MASKS,),
        in_specs=[
            pl.BlockSpec(memory_space=pltpu.SMEM),
            pl.BlockSpec((2, OCT, N), octet),
            pl.BlockSpec((1, OCT, N), octet),
            pl.BlockSpec((2, 256, 256), lambda m: (0, 0, 0)),
            pl.BlockSpec((2, SHORT, LANES), lambda m: (0, 0, 0)),
        ],
        out_specs=(pl.BlockSpec((2048, LANES), flat),) + (pl.BlockSpec((OCT, N), flat),) * MASKS,
        scratch_shapes=[
            pltpu.VMEM((2, SHORT, OCT, LANES), F32),
            pltpu.VMEM((256, 256), F32),
        ],
        compiler_params=pltpu.CompilerParams(vmem_limit_bytes=60 << 20),
        cost_estimate=pl.CostEstimate(flops=1 << 29, bytes_accessed=3 << 20, transcendentals=0),
    )(index, object_field, phases, t["left"], t["row_tw"])
    inten = intensity.reshape(2, 16, 8, 4, LANES).transpose(3, 0, 4, 1, 2).reshape(4, 256, LANES)
    up = [(i, (i + 1) % MASKS) for i in range(MASKS)]
    down = [((i + 1) % MASKS, i) for i in range(MASKS)]
    across = [(i, (i + 2) % MASKS) for i in range(MASKS)]
    order = [int(i) for i in exchange_order()]
    every = [m * LANES + i for i in order for m in range(MASKS)]
    exchange = functools.partial(lax.all_to_all, split_axis=0, concat_axis=0, tiled=True)
    rec = exchange(sent.reshape(LANES, 16, LANES), "rows", axis_index_groups=[order])
    g1 = lax.ppermute(c1, "mask", up)
    g2 = lax.ppermute(c2, "mask", across)
    g3 = lax.ppermute(c3, "mask", down)
    back = call(
        columns, "columns", sds((2048, LANES), F32), 5,
        [pltpu.VMEM((4, 2, 2, LANES, LANES), F32)], 3 << 29,
    )(rec.reshape(2048, LANES), inten, t["inner"], t["block"], t["col_tw"])
    back, g2, g1, g3 = lax.optimization_barrier((back, g2, g1, g3))
    rec = exchange(back.reshape(512, 4, LANES), ("mask", "rows"), axis_index_groups=[every])
    half = sds((OCT, N), F32)
    part, own_re, own_im = call(
        rows_back, "rows_back", (sds((2, OCT, N), F32), half, half), 8,
        [pltpu.VMEM((2, SHORT, OCT, LANES), F32), pltpu.VMEM((256, 256), F32)], 1 << 29, smem=(0,),
    )(index, rec.reshape(2048, LANES), c0, g1, g2, g3, t["left"], t["row_tw"])
    ring = [
        (m * LANES + r, (m + 1 - 2 * (r % 2)) % MASKS * LANES + r)
        for m in range(MASKS)
        for r in range(LANES)
    ]
    both = ("mask", "rows")
    near_re = lax.ppermute(own_re, both, ring)
    near_im = lax.ppermute(own_im, both, ring)
    other = lax.ppermute(part, both, [(b, a) for a, b in ring])
    far_re = lax.ppermute(near_re, both, ring)
    far_im = lax.ppermute(near_im, both, ring)
    side = 2 * (lax.axis_index("rows").astype(jnp.int32) % 2) - 1
    me = index[0] + MASKS
    masks = jnp.stack([me, me + side, me + 2, me - side]) % MASKS
    whole = sds((2, SHORT, N), F32)
    return call(finish, "finish", (whole, whole), 9, [], 1 << 20, smem=(0,))(
        masks, own_re, own_im, near_re, near_im, far_re, far_im, other, object_field
    )


def solution(mesh):
    return jax.shard_map(
        body,
        mesh=mesh,
        in_specs=(P(None, "rows", None), P("mask", "rows", None), P("mask", "rows", None)),
        out_specs=(P(None, "rows", None), P(None, "rows", None)),
        check_vma=False,
    )
```

```python
import functools
import math

import jax
import jax.numpy as jnp
import ml_dtypes
import numpy as np
from jax import lax
from jax.experimental import pallas as pl
from jax.experimental.pallas import tpu as pltpu
from jax.sharding import PartitionSpec as P

N = 4096
LANES = 128
SHORT = 32
OCT = 8
MASKS = 4
step_size = 0.2


def _split(table):
    high = table.astype(np.float32).astype(ml_dtypes.bfloat16)
    low = (table - high.astype(np.float64)).astype(np.float32).astype(ml_dtypes.bfloat16)
    return np.stack([high, low])


def exchange_order():
    index = np.arange(LANES).reshape(2, 4, 8, 2)
    return index.transpose(0, 1, 3, 2).reshape(LANES)


@functools.lru_cache(maxsize=None)
def tables():
    i128 = np.arange(LANES)
    w = np.exp(-2j * math.pi * (np.outer(i128, i128) % LANES) / LANES) / 64.0
    w = w[exchange_order()]
    left = np.block([[w.real, -w.imag], [w.imag, w.real]])
    inner = np.block([[w.real.T, -w.imag.T], [w.imag.T, w.real.T]])
    t = np.exp(-2j * math.pi * np.outer(np.arange(SHORT), i128) / N)
    row_tw = np.stack([t.real, t.imag]).astype(np.float32)
    rho = i128 % OCT
    row = np.arange(MASKS)[:, None] * OCT + rho[None, :]
    t = np.exp(-2j * math.pi * (i128[None, :, None] * row[:, None, :]) / N)
    col_tw = np.stack([t.real, t.imag])
    r8 = np.arange(OCT)
    big = np.kron(np.eye(16), np.exp(-2j * math.pi * np.outer(r8, r8) / 8))
    block = np.block([[big.real, big.imag], [-big.imag, big.real]])
    t = np.exp(-2j * math.pi * np.outer(np.arange(OCT), rho) / SHORT)
    col_tw = np.concatenate([col_tw.reshape(2, 4 * LANES, LANES), np.stack([t.real, t.imag])], axis=1)
    return dict(left=_split(left), inner=_split(inner), block=_split(block), row_tw=row_tw, col_tw=col_tw.astype(np.float32))


def split(x):
    high = x.astype(jnp.bfloat16)
    return high, (x - high.astype(jnp.float32)).astype(jnp.bfloat16)


def dot3(a, b, dims):
    dot = functools.partial(
        lax.dot_general, dimension_numbers=(dims, ((), ())), preferred_element_type=jnp.float32
    )
    return dot(a[0], b[0]) + (dot(a[0], b[1]) + dot(a[1], b[0]))


NN = ((1,), (0,))
NT = ((1,), (1,))
TN = ((0,), (0,))


def cmul(a, b):
    return a[0] * b[0] - a[1] * b[1], a[0] * b[1] + a[1] * b[0]


def cadd(a, b):
    return a[0] + b[0], a[1] + b[1]


def csub(a, b):
    return a[0] - b[0], a[1] - b[1]


def times_i(a, sign):
    return (-a[1], a[0]) if sign > 0 else (a[1], -a[0])


def rotate(a, turns, length, sign):
    turns = turns % length
    if turns == 0:
        return a
    eighths = turns * 8 % (length * 8) / length
    if eighths == 4:
        return -a[0], -a[1]
    if eighths == 2:
        return times_i(a, sign)
    if eighths == 6:
        return times_i(a, -sign)
    angle = sign * 2 * math.pi * turns / length
    c, s = float(np.float32(math.cos(angle))), float(np.float32(math.sin(angle)))
    if eighths in (1, 3, 5, 7):
        h = float(np.float32(math.sqrt(0.5)))
        cs, ss = (1 if c > 0 else -1), (1 if s > 0 else -1)
        re = (a[0] if cs > 0 else -a[0]) - (a[1] if ss > 0 else -a[1])
        im = (a[1] if cs > 0 else -a[1]) + (a[0] if ss > 0 else -a[0])
        return re * h, im * h
    return a[0] * c - a[1] * s, a[0] * s + a[1] * c


def fft4(x, sign):
    a, b = cadd(x[0], x[2]), csub(x[0], x[2])
    c, d = cadd(x[1], x[3]), times_i(csub(x[1], x[3]), sign)
    return [cadd(a, c), cadd(b, d), csub(a, c), csub(b, d)]


def fft8(x, sign):
    even, odd = fft4(x[0::2], sign), fft4(x[1::2], sign)
    odd = [rotate(o, j, 8, sign) for j, o in enumerate(odd)]
    return [cadd(u, v) for u, v in zip(even, odd)] + [csub(u, v) for u, v in zip(even, odd)]


def fft32(load, store, mid, sign):
    for p0 in range(8):
        y = fft4([load(8 * p1 + p0) for p1 in range(4)], sign)
        for k0 in range(4):
            v = rotate(y[k0], p0 * k0, 32, sign)
            mid[0, k0 * 8 + p0] = v[0]
            mid[1, k0 * 8 + p0] = v[1]
    for k0 in range(4):
        y = fft8([(mid[0, k0 * 8 + p0], mid[1, k0 * 8 + p0]) for p0 in range(8)], sign)
        for k1 in range(8):
            store(k0 + 4 * k1, y[k1])


def code_times(code, z):
    odd = (code & 1) == 1
    a = jnp.where(odd, z[1], z[0])
    b = jnp.where(odd, z[0], z[1])
    return jnp.where((code == 1) | (code == 2), -a, a), jnp.where(code >= 2, -b, b)


def conj_code_times(code, z):
    odd = (code & 1) == 1
    a = jnp.where(odd, z[1], z[0])
    b = jnp.where(odd, z[0], z[1])
    return jnp.where(code >= 2, -a, a), jnp.where((code == 1) | (code == 2), -b, b)


def rows_forward(index, obj, code, left, tw, out, c0, c2, c1, c3, mid, xs):
    m = pl.program_id(0)
    shift = lax.rem(m + MASKS - index[0], MASKS)
    for s, c in enumerate((c0, c1, c2, c3)):

        @pl.when(shift == s)
        def _():
            c[...] = code[0]

    def load(p):
        cols = slice(LANES * p, LANES * p + LANES)
        return code_times(code[0, :, cols], (obj[0, :, cols], obj[1, :, cols]))

    def store(k, v):
        v = cmul(v, (tw[0, k : k + 1], tw[1, k : k + 1]))
        xs[OCT * k : OCT * k + OCT, :LANES] = v[0]
        xs[OCT * k : OCT * k + OCT, LANES:] = v[1]

    fft32(load, store, mid, -1)
    y = dot3((left[0], left[1]), split(xs[...]), NT)
    for ri in range(2):
        for h in range(2):
            out[pl.ds(ri * 8 + 2 * m + h, LANES, stride=16), :] = y[
                LANES * ri : LANES * ri + LANES, LANES * h : LANES * h + LANES
            ]


def columns(rec, inten, inner, block, tw, out, s):
    def turned(e, sign):
        row = slice(4 * LANES + e, 4 * LANES + e + 1)
        return tw[0, row, :], sign * tw[1, row, :]

    for m in range(MASKS):
        x = jnp.concatenate(
            [
                jnp.concatenate(
                    [rec[pl.ds(ri * 8 + 2 * m + h, LANES, stride=16), :] for h in range(2)], axis=1
                )
                for ri in range(2)
            ],
            axis=0,
        )
        y = dot3((inner[0], inner[1]), split(x), NN)
        rows = slice(LANES * m, LANES * m + LANES)
        t = (tw[0, rows], tw[1, rows])
        for h in range(2):
            cols = slice(LANES * h, LANES * h + LANES)
            v = cmul((y[:LANES, cols], y[LANES:, cols]), t)
            s[m, 0, h] = v[0]
            s[m, 1, h] = v[1]

    for h in range(2):
        def turn(i, _):
            rows = pl.ds(pl.multiple_of(i * OCT, OCT), OCT)
            y = fft4([(s[m, 0, h, rows, :], s[m, 1, h, rows, :]) for m in range(4)], -1)
            for e in range(4):
                v = cmul(y[e], turned(e, 1)) if e else y[e]
                s[e, 0, h, rows, :] = v[0]
                s[e, 1, h, rows, :] = v[1]
            return 0

        lax.fori_loop(0, LANES // OCT, turn, 0, unroll=True)

    for e in range(4):
        x = jnp.concatenate(
            [jnp.concatenate([s[e, 0, h], s[e, 1, h]], axis=1) for h in range(2)], axis=0
        )
        y = dot3(split(x), (block[0], block[1]), NN)
        wr, wi = y[:, :LANES], y[:, LANES:]
        weight = wr * wr + wi * wi - inten[e]
        v = jnp.concatenate([wr * weight, wi * weight], axis=1)
        y = dot3(split(v), (block[0], block[1]), NT)
        for h in range(2):
            rows = slice(LANES * h, LANES * h + LANES)
            s[e, 0, h] = y[rows, :LANES]
            s[e, 1, h] = y[rows, LANES:]

    for h in range(2):
        def turn_back(i, _):
            rows = pl.ds(pl.multiple_of(i * OCT, OCT), OCT)
            x = [(s[e, 0, h, rows, :], s[e, 1, h, rows, :]) for e in range(4)]
            y = fft4([cmul(v, turned(e, -1)) if e else v for e, v in enumerate(x)], 1)
            for m in range(4):
                near = pl.ds(pl.multiple_of(LANES * m + i * OCT, OCT), OCT)
                v = cmul(y[m], (tw[0, near, :], -tw[1, near, :]))
                s[m, 0, h, rows, :] = v[0]
                s[m, 1, h, rows, :] = v[1]
            return 0

        lax.fori_loop(0, LANES // OCT, turn_back, 0, unroll=True)

    for m in range(MASKS):
        x = jnp.concatenate(
            [jnp.concatenate([s[m, ri, 0], s[m, ri, 1]], axis=1) for ri in range(2)], axis=0
        )
        y = dot3((inner[0], inner[1]), split(x), TN)
        for ri in range(2):
            for h in range(2):
                out[pl.ds(m * 4 + ri * 2 + h, LANES, stride=16), :] = y[
                    LANES * ri : LANES * ri + LANES, LANES * h : LANES * h + LANES
                ]


def rows_back(index, rec, c0, c1, c2, c3, left, tw, out, out_re, out_im, mid, ys):
    for s, code in enumerate((c0, c1, c2, c3)):
        l = lax.rem(index[0] + MASKS - s, MASKS)
        x = jnp.concatenate(
            [
                jnp.concatenate(
                    [
                        rec[pl.ds(l * 4 + ri * 2 + h, LANES, stride=16), :].T
                        for ri in range(2)
                    ],
                    axis=1,
                )
                for h in range(2)
            ],
            axis=0,
        )
        ys[...] = dot3(split(x), (left[0], left[1]), NN)

        def load(k):
            rows = slice(OCT * k, OCT * k + OCT)
            return cmul((ys[rows, :LANES], ys[rows, LANES:]), (tw[0, k : k + 1], -tw[1, k : k + 1]))

        def store(p, v):
            cols = slice(LANES * p, LANES * p + LANES)
            v = conj_code_times(code[:, cols], v)
            for ri in range(2):
                if s == 0:
                    out[ri, :, cols] = v[ri]
                elif s < MASKS - 1:
                    out[ri, :, cols] += v[ri]
                else:
                    total = (out[ri, :, cols] + v[ri]) * (1.0 / MASKS)
                    out[ri, :, cols] = total
                    (out_re, out_im)[ri][:, cols] = total

        fft32(load, store, mid, 1)


def finish(index, core, own_re, own_im, near_re, near_im, far_re, far_im, other, obj, updated, direction):
    parts = ((own_re, own_im), (near_re, near_im), (far_re, far_im), (other.at[0], other.at[1]))
    side = 2 * lax.rem(core[0], 2) - 1
    for shift, part in zip((0, side, 2, -side), parts):
        mask = lax.rem(index[0] + MASKS + shift, MASKS)
        rows = pl.ds(pl.multiple_of(mask * OCT, OCT), OCT)
        for ri in range(2):
            value = part[ri][...]
            direction[ri, rows, :] = value
            updated[ri, rows, :] = obj[ri, rows, :] - step_size * value


VM = pl.BlockSpec(memory_space=pltpu.VMEM)
F32 = jnp.float32


def call(kernel, name, out_shape, n_in, scratch, flops, vmem=24, smem=()):
    specs = [VM] * n_in
    for i in smem:
        specs[i] = pl.BlockSpec(memory_space=pltpu.SMEM)
    outs = jax.tree.map(lambda _: VM, out_shape)
    return pl.pallas_call(
        kernel,
        name=name,
        out_shape=out_shape,
        in_specs=specs,
        out_specs=outs,
        scratch_shapes=scratch,
        compiler_params=pltpu.CompilerParams(vmem_limit_bytes=vmem << 20),
        cost_estimate=pl.CostEstimate(flops=flops, bytes_accessed=3 << 20, transcendentals=0),
    )


def body(object_field, phases, intensity):
    t = {k: jnp.asarray(v) for k, v in tables().items()}
    sds = jax.ShapeDtypeStruct
    index = lax.axis_index("mask").astype(jnp.int32).reshape(1)
    octet = lambda m: (0, m, 0)
    flat = lambda m: (0, 0)
    rows8 = sds((OCT, N), jnp.int32)
    sent, c0, c2, c1, c3 = pl.pallas_call(
        rows_forward,
        name="rows_forward",
        out_shape=(sds((2048, LANES), F32),) + (rows8,) * MASKS,
        grid=(MASKS,),
        in_specs=[
            pl.BlockSpec(memory_space=pltpu.SMEM),
            pl.BlockSpec((2, OCT, N), octet),
            pl.BlockSpec((1, OCT, N), octet),
            pl.BlockSpec((2, 256, 256), lambda m: (0, 0, 0)),
            pl.BlockSpec((2, SHORT, LANES), lambda m: (0, 0, 0)),
        ],
        out_specs=(pl.BlockSpec((2048, LANES), flat),) + (pl.BlockSpec((OCT, N), flat),) * MASKS,
        scratch_shapes=[
            pltpu.VMEM((2, SHORT, OCT, LANES), F32),
            pltpu.VMEM((256, 256), F32),
        ],
        compiler_params=pltpu.CompilerParams(vmem_limit_bytes=60 << 20),
        cost_estimate=pl.CostEstimate(flops=1 << 29, bytes_accessed=3 << 20, transcendentals=0),
    )(index, object_field, phases, t["left"], t["row_tw"])
    inten = intensity.reshape(2, 16, 8, 4, LANES).transpose(3, 0, 4, 1, 2).reshape(4, 256, LANES)
    up = [(i, (i + 1) % MASKS) for i in range(MASKS)]
    down = [((i + 1) % MASKS, i) for i in range(MASKS)]
    ring = [
        (m * LANES + r, (m + 1 - 2 * (r % 2)) % MASKS * LANES + r)
        for m in range(MASKS)
        for r in range(LANES)
    ]
    both = ("mask", "rows")
    order = [int(i) for i in exchange_order()]
    every = [m * LANES + i for i in order for m in range(MASKS)]
    exchange = functools.partial(lax.all_to_all, split_axis=0, concat_axis=0, tiled=True)
    rec = exchange(sent.reshape(LANES, 16, LANES), "rows", axis_index_groups=[order])
    g1 = lax.ppermute(c1, "mask", up)
    g2 = lax.ppermute(lax.ppermute(c2, both, ring), both, ring)
    g3 = lax.ppermute(c3, "mask", down)
    back = call(
        columns, "columns", sds((2048, LANES), F32), 5,
        [pltpu.VMEM((4, 2, 2, LANES, LANES), F32)], 3 << 29,
    )(rec.reshape(2048, LANES), inten, t["inner"], t["block"], t["col_tw"])
    back, g2, g1, g3 = lax.optimization_barrier((back, g2, g1, g3))
    rec = exchange(back.reshape(512, 4, LANES), ("mask", "rows"), axis_index_groups=[every])
    half = sds((OCT, N), F32)
    part, own_re, own_im = call(
        rows_back, "rows_back", (sds((2, OCT, N), F32), half, half), 8,
        [pltpu.VMEM((2, SHORT, OCT, LANES), F32), pltpu.VMEM((256, 256), F32)], 1 << 29, smem=(0,),
    )(index, rec.reshape(2048, LANES), c0, g1, g2, g3, t["left"], t["row_tw"])
    near_re = lax.ppermute(own_re, both, ring)
    near_im = lax.ppermute(own_im, both, ring)
    other = lax.ppermute(part, both, [(b, a) for a, b in ring])
    far_re = lax.ppermute(near_re, both, ring)
    far_im = lax.ppermute(near_im, both, ring)
    core = lax.axis_index("rows").astype(jnp.int32).reshape(1)
    whole = sds((2, SHORT, N), F32)
    return call(finish, "finish", (whole, whole), 10, [], 1 << 20, smem=(0, 1))(
        index, core, own_re, own_im, near_re, near_im, far_re, far_im, other, object_field
    )


def solution(mesh):
    return jax.shard_map(
        body,
        mesh=mesh,
        in_specs=(P(None, "rows", None), P("mask", "rows", None), P("mask", "rows", None)),
        out_specs=(P(None, "rows", None), P(None, "rows", None)),
        check_vma=False,
    )
```

```python
import functools
import math

import jax
import jax.numpy as jnp
import ml_dtypes
import numpy as np
from jax import lax
from jax.experimental import pallas as pl
from jax.experimental.pallas import tpu as pltpu
from jax.sharding import PartitionSpec as P

N = 4096
LANES = 128
SHORT = 32
OCT = 8
MASKS = 4
step_size = 0.2


def _split(table):
    high = table.astype(np.float32).astype(ml_dtypes.bfloat16)
    low = (table - high.astype(np.float64)).astype(np.float32).astype(ml_dtypes.bfloat16)
    return np.stack([high, low])


def exchange_order():
    index = np.arange(LANES).reshape(2, 4, 8, 2)
    return index.transpose(0, 1, 3, 2).reshape(LANES)


@functools.lru_cache(maxsize=None)
def tables():
    i128 = np.arange(LANES)
    w = np.exp(-2j * math.pi * (np.outer(i128, i128) % LANES) / LANES) / 64.0
    w = w[exchange_order()]
    left = np.block([[w.real, -w.imag], [w.imag, w.real]])
    inner = np.block([[w.real.T, -w.imag.T], [w.imag.T, w.real.T]])
    t = np.exp(-2j * math.pi * np.outer(np.arange(SHORT), i128) / N)
    row_tw = np.stack([t.real, t.imag]).astype(np.float32)
    rho = i128 % OCT
    row = np.arange(MASKS)[:, None] * OCT + rho[None, :]
    t = np.exp(-2j * math.pi * (i128[None, :, None] * row[:, None, :]) / N)
    col_tw = np.stack([t.real, t.imag])
    r8 = np.arange(OCT)
    big = np.kron(np.eye(16), np.exp(-2j * math.pi * np.outer(r8, r8) / 8))
    block = np.block([[big.real, big.imag], [-big.imag, big.real]])
    t = np.exp(-2j * math.pi * np.outer(np.arange(OCT), rho) / SHORT)
    col_tw = np.concatenate([col_tw.reshape(2, 4 * LANES, LANES), np.stack([t.real, t.imag])], axis=1)
    return dict(left=_split(left), inner=_split(inner), block=_split(block), row_tw=row_tw, col_tw=col_tw.astype(np.float32))


def split(x):
    high = x.astype(jnp.bfloat16)
    return high, (x - high.astype(jnp.float32)).astype(jnp.bfloat16)


def dot3(a, b, dims):
    dot = functools.partial(
        lax.dot_general, dimension_numbers=(dims, ((), ())), preferred_element_type=jnp.float32
    )
    return dot(a[0], b[0]) + (dot(a[0], b[1]) + dot(a[1], b[0]))


NN = ((1,), (0,))
NT = ((1,), (1,))
TN = ((0,), (0,))


def cmul(a, b):
    return a[0] * b[0] - a[1] * b[1], a[0] * b[1] + a[1] * b[0]


def cadd(a, b):
    return a[0] + b[0], a[1] + b[1]


def csub(a, b):
    return a[0] - b[0], a[1] - b[1]


def times_i(a, sign):
    return (-a[1], a[0]) if sign > 0 else (a[1], -a[0])


def rotate(a, turns, length, sign):
    turns = turns % length
    if turns == 0:
        return a
    eighths = turns * 8 % (length * 8) / length
    if eighths == 4:
        return -a[0], -a[1]
    if eighths == 2:
        return times_i(a, sign)
    if eighths == 6:
        return times_i(a, -sign)
    angle = sign * 2 * math.pi * turns / length
    c, s = float(np.float32(math.cos(angle))), float(np.float32(math.sin(angle)))
    if eighths in (1, 3, 5, 7):
        h = float(np.float32(math.sqrt(0.5)))
        cs, ss = (1 if c > 0 else -1), (1 if s > 0 else -1)
        re = (a[0] if cs > 0 else -a[0]) - (a[1] if ss > 0 else -a[1])
        im = (a[1] if cs > 0 else -a[1]) + (a[0] if ss > 0 else -a[0])
        return re * h, im * h
    return a[0] * c - a[1] * s, a[0] * s + a[1] * c


def fft4(x, sign):
    a, b = cadd(x[0], x[2]), csub(x[0], x[2])
    c, d = cadd(x[1], x[3]), times_i(csub(x[1], x[3]), sign)
    return [cadd(a, c), cadd(b, d), csub(a, c), csub(b, d)]


def fft8(x, sign):
    even, odd = fft4(x[0::2], sign), fft4(x[1::2], sign)
    odd = [rotate(o, j, 8, sign) for j, o in enumerate(odd)]
    return [cadd(u, v) for u, v in zip(even, odd)] + [csub(u, v) for u, v in zip(even, odd)]


def fft32(load, store, mid, sign):
    for p0 in range(8):
        y = fft4([load(8 * p1 + p0) for p1 in range(4)], sign)
        for k0 in range(4):
            v = rotate(y[k0], p0 * k0, 32, sign)
            mid[0, k0 * 8 + p0] = v[0]
            mid[1, k0 * 8 + p0] = v[1]
    for k0 in range(4):
        y = fft8([(mid[0, k0 * 8 + p0], mid[1, k0 * 8 + p0]) for p0 in range(8)], sign)
        for k1 in range(8):
            store(k0 + 4 * k1, y[k1])


def code_times(code, z):
    odd = (code & 1) == 1
    a = jnp.where(odd, z[1], z[0])
    b = jnp.where(odd, z[0], z[1])
    return jnp.where((code == 1) | (code == 2), -a, a), jnp.where(code >= 2, -b, b)


def conj_code_times(code, z):
    odd = (code & 1) == 1
    a = jnp.where(odd, z[1], z[0])
    b = jnp.where(odd, z[0], z[1])
    return jnp.where(code >= 2, -a, a), jnp.where((code == 1) | (code == 2), -b, b)


def rows_forward(index, obj, code, every, left, tw, out, c0, c2, c1, c3, mid, xs, buf, sems, code_sems):
    m = pl.program_id(0)

    def code_copy(s, c):
        row = pl.multiple_of(lax.rem(index[0] + s, MASKS) * OCT, OCT)
        return pltpu.make_async_copy(every.at[0, pl.ds(row, OCT), :], c, code_sems.at[s])

    def out_copy(step):
        return pltpu.make_async_copy(buf.at[step], out.at[:, step], sems.at[step])

    @pl.when(m == 0)
    def _():
        for s, c in enumerate((c0, c1, c2, c3)):
            code_copy(s, c).start()

    def load(p):
        cols = slice(LANES * p, LANES * p + LANES)
        return code_times(code[0, :, cols], (obj[0, :, cols], obj[1, :, cols]))

    def store(k, v):
        v = cmul(v, (tw[0, k : k + 1], tw[1, k : k + 1]))
        xs[OCT * k : OCT * k + OCT, :LANES] = v[0]
        xs[OCT * k : OCT * k + OCT, LANES:] = v[1]

    fft32(load, store, mid, -1)
    y = dot3((left[0], left[1]), split(xs[...]), NT)
    for ri in range(2):
        for h in range(2):
            buf[m, :, ri * 2 + h, :] = y[
                LANES * ri : LANES * ri + LANES, LANES * h : LANES * h + LANES
            ]
    out_copy(m).start()

    @pl.when(m == MASKS - 1)
    def _():
        for s, c in enumerate((c0, c1, c2, c3)):
            code_copy(s, c).wait()
        for step in range(MASKS):
            out_copy(step).wait()


def columns(rec, inten, inner, block, tw, out, s):
    def turned(e, sign):
        row = slice(4 * LANES + e, 4 * LANES + e + 1)
        return tw[0, row, :], sign * tw[1, row, :]

    for m in range(MASKS):
        x = jnp.concatenate(
            [
                jnp.concatenate(
                    [rec[pl.ds(m * 4 + ri * 2 + h, LANES, stride=16), :] for h in range(2)], axis=1
                )
                for ri in range(2)
            ],
            axis=0,
        )
        y = dot3((inner[0], inner[1]), split(x), NN)
        rows = slice(LANES * m, LANES * m + LANES)
        t = (tw[0, rows], tw[1, rows])
        for h in range(2):
            cols = slice(LANES * h, LANES * h + LANES)
            v = cmul((y[:LANES, cols], y[LANES:, cols]), t)
            s[m, 0, h] = v[0]
            s[m, 1, h] = v[1]

    for h in range(2):
        def turn(i, _):
            rows = pl.ds(pl.multiple_of(i * OCT, OCT), OCT)
            y = fft4([(s[m, 0, h, rows, :], s[m, 1, h, rows, :]) for m in range(4)], -1)
            for e in range(4):
                v = cmul(y[e], turned(e, 1)) if e else y[e]
                s[e, 0, h, rows, :] = v[0]
                s[e, 1, h, rows, :] = v[1]
            return 0

        lax.fori_loop(0, LANES // OCT, turn, 0, unroll=True)

    for e in range(4):
        x = jnp.concatenate(
            [jnp.concatenate([s[e, 0, h], s[e, 1, h]], axis=1) for h in range(2)], axis=0
        )
        y = dot3(split(x), (block[0], block[1]), NN)
        wr, wi = y[:, :LANES], y[:, LANES:]
        weight = wr * wr + wi * wi - inten[e]
        v = jnp.concatenate([wr * weight, wi * weight], axis=1)
        y = dot3(split(v), (block[0], block[1]), NT)
        for h in range(2):
            rows = slice(LANES * h, LANES * h + LANES)
            s[e, 0, h] = y[rows, :LANES]
            s[e, 1, h] = y[rows, LANES:]

    for h in range(2):
        def turn_back(i, _):
            rows = pl.ds(pl.multiple_of(i * OCT, OCT), OCT)
            x = [(s[e, 0, h, rows, :], s[e, 1, h, rows, :]) for e in range(4)]
            y = fft4([cmul(v, turned(e, -1)) if e else v for e, v in enumerate(x)], 1)
            for m in range(4):
                near = pl.ds(pl.multiple_of(LANES * m + i * OCT, OCT), OCT)
                v = cmul(y[m], (tw[0, near, :], -tw[1, near, :]))
                s[m, 0, h, rows, :] = v[0]
                s[m, 1, h, rows, :] = v[1]
            return 0

        lax.fori_loop(0, LANES // OCT, turn_back, 0, unroll=True)

    for m in range(MASKS):
        x = jnp.concatenate(
            [jnp.concatenate([s[m, ri, 0], s[m, ri, 1]], axis=1) for ri in range(2)], axis=0
        )
        y = dot3((inner[0], inner[1]), split(x), TN)
        for ri in range(2):
            for h in range(2):
                out[pl.ds(m * 4 + ri * 2 + h, LANES, stride=16), :] = y[
                    LANES * ri : LANES * ri + LANES, LANES * h : LANES * h + LANES
                ]


def rows_back(index, rec, c0, c1, c2, c3, left, tw, out, out_re, out_im, mid, ys):
    for s, code in enumerate((c0, c1, c2, c3)):
        l = lax.rem(index[0] + MASKS - s, MASKS)
        x = jnp.concatenate(
            [
                jnp.concatenate(
                    [
                        rec[pl.ds(l * 4 + ri * 2 + h, LANES, stride=16), :].T
                        for ri in range(2)
                    ],
                    axis=1,
                )
                for h in range(2)
            ],
            axis=0,
        )
        ys[...] = dot3(split(x), (left[0], left[1]), NN)

        def load(k):
            rows = slice(OCT * k, OCT * k + OCT)
            return cmul((ys[rows, :LANES], ys[rows, LANES:]), (tw[0, k : k + 1], -tw[1, k : k + 1]))

        def store(p, v):
            cols = slice(LANES * p, LANES * p + LANES)
            v = conj_code_times(code[:, cols], v)
            for ri in range(2):
                if s == 0:
                    out[ri, :, cols] = v[ri]
                elif s < MASKS - 1:
                    out[ri, :, cols] += v[ri]
                else:
                    total = (out[ri, :, cols] + v[ri]) * (1.0 / MASKS)
                    out[ri, :, cols] = total
                    (out_re, out_im)[ri][:, cols] = total

        fft32(load, store, mid, 1)


def write_rows(masks, parts, obj, updated, direction, bufs, sems):
    copies = []
    for i, (mask, part) in enumerate(zip(masks, parts)):
        rows = pl.ds(pl.multiple_of(mask * OCT, OCT), OCT)
        for ri in range(2):
            value = part[ri][...]
            bufs[i, 0, ri] = obj[ri, rows, :] - step_size * value
            bufs[i, 1, ri] = value
        for j, out in enumerate((updated, direction)):
            copy = pltpu.make_async_copy(bufs.at[i, j], out.at[:, rows, :], sems.at[i, j])
            copy.start()
            copies.append(copy)
    for copy in copies:
        copy.wait()


def side_of(core):
    return 2 * lax.rem(core[0], 2) - 1


def finish_first(index, core, own_re, own_im, near_re, near_im, obj, updated, direction, bufs, sems):
    masks = [lax.rem(index[0] + MASKS + shift, MASKS) for shift in (0, side_of(core))]
    parts = ((own_re, own_im), (near_re, near_im))
    write_rows(masks, parts, obj, updated, direction, bufs, sems)


def finish_last(index, core, far_re, far_im, other, obj, _u, _d, updated, direction, bufs, sems):
    masks = [lax.rem(index[0] + MASKS + shift, MASKS) for shift in (-side_of(core), 2)]
    parts = ((other.at[0], other.at[1]), (far_re, far_im))
    write_rows(masks, parts, obj, updated, direction, bufs, sems)


VM = pl.BlockSpec(memory_space=pltpu.VMEM)
F32 = jnp.float32


def call(kernel, name, out_shape, n_in, scratch, flops, vmem=24, smem=()):
    specs = [VM] * n_in
    for i in smem:
        specs[i] = pl.BlockSpec(memory_space=pltpu.SMEM)
    outs = jax.tree.map(lambda _: VM, out_shape)
    return pl.pallas_call(
        kernel,
        name=name,
        out_shape=out_shape,
        in_specs=specs,
        out_specs=outs,
        scratch_shapes=scratch,
        compiler_params=pltpu.CompilerParams(vmem_limit_bytes=vmem << 20),
        cost_estimate=pl.CostEstimate(flops=flops, bytes_accessed=3 << 20, transcendentals=0),
    )


def body(object_field, phases, intensity):
    t = {k: jnp.asarray(v) for k, v in tables().items()}
    sds = jax.ShapeDtypeStruct
    index = lax.axis_index("mask").astype(jnp.int32).reshape(1)
    octet = lambda m: (0, m, 0)
    flat = lambda m: (0, 0)
    rows8 = sds((OCT, N), jnp.int32)
    sent, c0, c2, c1, c3 = pl.pallas_call(
        rows_forward,
        name="rows_forward",
        out_shape=(sds((LANES, MASKS, 4, LANES), F32),) + (rows8,) * MASKS,
        grid=(MASKS,),
        in_specs=[
            pl.BlockSpec(memory_space=pltpu.SMEM),
            pl.BlockSpec((2, OCT, N), octet),
            pl.BlockSpec((1, OCT, N), octet),
            pl.BlockSpec(memory_space=pl.ANY),
            pl.BlockSpec((2, 256, 256), lambda m: (0, 0, 0)),
            pl.BlockSpec((2, SHORT, LANES), lambda m: (0, 0, 0)),
        ],
        out_specs=(pl.BlockSpec(memory_space=pl.ANY),) * (1 + MASKS),
        scratch_shapes=[
            pltpu.VMEM((2, SHORT, OCT, LANES), F32),
            pltpu.VMEM((256, 256), F32),
            pltpu.VMEM((MASKS, LANES, 4, LANES), F32),
            pltpu.SemaphoreType.DMA((MASKS,)),
            pltpu.SemaphoreType.DMA((MASKS,)),
        ],
        compiler_params=pltpu.CompilerParams(vmem_limit_bytes=60 << 20),
        cost_estimate=pl.CostEstimate(flops=1 << 29, bytes_accessed=3 << 20, transcendentals=0),
    )(index, object_field, phases, phases, t["left"], t["row_tw"])
    inten = intensity.reshape(2, 16, 8, 4, LANES).transpose(3, 0, 4, 1, 2).reshape(4, 256, LANES)
    up = [(i, (i + 1) % MASKS) for i in range(MASKS)]
    down = [((i + 1) % MASKS, i) for i in range(MASKS)]
    ring = [
        (m * LANES + r, (m + 1 - 2 * (r % 2)) % MASKS * LANES + r)
        for m in range(MASKS)
        for r in range(LANES)
    ]
    both = ("mask", "rows")
    order = [int(i) for i in exchange_order()]
    every = [m * LANES + i for i in order for m in range(MASKS)]
    exchange = functools.partial(lax.all_to_all, split_axis=0, concat_axis=0, tiled=True)
    rec = exchange(sent.reshape(LANES, 16, LANES), "rows", axis_index_groups=[order])
    g1 = lax.ppermute(c1, "mask", up)
    g2 = lax.ppermute(lax.ppermute(c2, both, ring), both, ring)
    g3 = lax.ppermute(c3, "mask", down)
    back = call(
        columns, "columns", sds((2048, LANES), F32), 5,
        [pltpu.VMEM((4, 2, 2, LANES, LANES), F32)], 3 << 29,
    )(rec.reshape(2048, LANES), inten, t["inner"], t["block"], t["col_tw"])
    back, g2, g1, g3 = lax.optimization_barrier((back, g2, g1, g3))
    rec = exchange(back.reshape(512, 4, LANES), ("mask", "rows"), axis_index_groups=[every])
    half = sds((OCT, N), F32)
    part, own_re, own_im = call(
        rows_back, "rows_back", (sds((2, OCT, N), F32), half, half), 8,
        [pltpu.VMEM((2, SHORT, OCT, LANES), F32), pltpu.VMEM((256, 256), F32)], 1 << 29, smem=(0,),
    )(index, rec.reshape(2048, LANES), c0, g1, g2, g3, t["left"], t["row_tw"])
    near_re = lax.ppermute(own_re, both, ring)
    near_im = lax.ppermute(own_im, both, ring)
    other = lax.ppermute(part, both, [(b, a) for a, b in ring])
    far_re = lax.ppermute(near_re, both, ring)
    far_im = lax.ppermute(near_im, both, ring)
    core = lax.axis_index("rows").astype(jnp.int32).reshape(1)
    whole = sds((2, SHORT, N), F32)
    scalars = [pl.BlockSpec(memory_space=pltpu.SMEM)] * 2
    anywhere = [pl.BlockSpec(memory_space=pl.ANY)] * 2
    scratch = [pltpu.VMEM((2, 2, 2, OCT, N), F32), pltpu.SemaphoreType.DMA((2, 2))]
    cost = pl.CostEstimate(flops=1 << 19, bytes_accessed=2 << 20, transcendentals=0)
    options = dict(
        out_shape=(whole, whole),
        out_specs=anywhere,
        scratch_shapes=scratch,
        compiler_params=pltpu.CompilerParams(vmem_limit_bytes=24 << 20),
        cost_estimate=cost,
    )
    first = pl.pallas_call(
        finish_first, name="finish_first", in_specs=scalars + [VM] * 5, **options
    )(index, core, own_re, own_im, near_re, near_im, object_field)
    return pl.pallas_call(
        finish_last,
        name="finish_last",
        in_specs=scalars + [VM] * 4 + anywhere,
        input_output_aliases={6: 0, 7: 1},
        **options,
    )(index, core, far_re, far_im, other, object_field, *first)


def solution(mesh):
    return jax.shard_map(
        body,
        mesh=mesh,
        in_specs=(P(None, "rows", None), P("mask", "rows", None), P("mask", "rows", None)),
        out_specs=(P(None, "rows", None), P(None, "rows", None)),
        check_vma=False,
    )
```

```python
import functools
import math

import jax
import jax.numpy as jnp
import ml_dtypes
import numpy as np
from jax import lax
from jax.experimental import pallas as pl
from jax.experimental.pallas import tpu as pltpu
from jax.sharding import PartitionSpec as P

N = 4096
LANES = 128
SHORT = 32
OCT = 8
MASKS = 4
step_size = 0.2


def _split(table):
    high = table.astype(np.float32).astype(ml_dtypes.bfloat16)
    low = (table - high.astype(np.float64)).astype(np.float32).astype(ml_dtypes.bfloat16)
    return np.stack([high, low])


def exchange_order():
    index = np.arange(LANES).reshape(2, 4, 8, 2)
    return index.transpose(0, 1, 3, 2).reshape(LANES)


@functools.lru_cache(maxsize=None)
def tables():
    i128 = np.arange(LANES)
    w = np.exp(-2j * math.pi * (np.outer(i128, i128) % LANES) / LANES) / 64.0
    w = w[exchange_order()]
    left = np.block([[w.real, -w.imag], [w.imag, w.real]])
    inner = np.block([[w.real.T, -w.imag.T], [w.imag.T, w.real.T]])
    t = np.exp(-2j * math.pi * np.outer(np.arange(SHORT), i128) / N)
    row_tw = np.stack([t.real, t.imag]).astype(np.float32)
    rho = i128 % OCT
    row = np.arange(MASKS)[:, None] * OCT + rho[None, :]
    t = np.exp(-2j * math.pi * (i128[None, :, None] * row[:, None, :]) / N)
    col_tw = np.stack([t.real, t.imag])
    r8 = np.arange(OCT)
    big = np.kron(np.eye(16), np.exp(-2j * math.pi * np.outer(r8, r8) / 8))
    block = np.block([[big.real, big.imag], [-big.imag, big.real]])
    t = np.exp(-2j * math.pi * np.outer(np.arange(OCT), rho) / SHORT)
    col_tw = np.concatenate([col_tw.reshape(2, 4 * LANES, LANES), np.stack([t.real, t.imag])], axis=1)
    return dict(left=_split(left), inner=_split(inner), block=_split(block), row_tw=row_tw, col_tw=col_tw.astype(np.float32))


def split(x):
    high = x.astype(jnp.bfloat16)
    return high, (x - high.astype(jnp.float32)).astype(jnp.bfloat16)


def dot3(a, b, dims):
    dot = functools.partial(
        lax.dot_general, dimension_numbers=(dims, ((), ())), preferred_element_type=jnp.float32
    )
    return dot(a[0], b[0]) + (dot(a[0], b[1]) + dot(a[1], b[0]))


NN = ((1,), (0,))
NT = ((1,), (1,))
TN = ((0,), (0,))


def cmul(a, b):
    return a[0] * b[0] - a[1] * b[1], a[0] * b[1] + a[1] * b[0]


def cadd(a, b):
    return a[0] + b[0], a[1] + b[1]


def csub(a, b):
    return a[0] - b[0], a[1] - b[1]


def times_i(a, sign):
    return (-a[1], a[0]) if sign > 0 else (a[1], -a[0])


def rotate(a, turns, length, sign):
    turns = turns % length
    if turns == 0:
        return a
    eighths = turns * 8 % (length * 8) / length
    if eighths == 4:
        return -a[0], -a[1]
    if eighths == 2:
        return times_i(a, sign)
    if eighths == 6:
        return times_i(a, -sign)
    angle = sign * 2 * math.pi * turns / length
    c, s = float(np.float32(math.cos(angle))), float(np.float32(math.sin(angle)))
    if eighths in (1, 3, 5, 7):
        h = float(np.float32(math.sqrt(0.5)))
        cs, ss = (1 if c > 0 else -1), (1 if s > 0 else -1)
        re = (a[0] if cs > 0 else -a[0]) - (a[1] if ss > 0 else -a[1])
        im = (a[1] if cs > 0 else -a[1]) + (a[0] if ss > 0 else -a[0])
        return re * h, im * h
    return a[0] * c - a[1] * s, a[0] * s + a[1] * c


def fft4(x, sign):
    a, b = cadd(x[0], x[2]), csub(x[0], x[2])
    c, d = cadd(x[1], x[3]), times_i(csub(x[1], x[3]), sign)
    return [cadd(a, c), cadd(b, d), csub(a, c), csub(b, d)]


def fft8(x, sign):
    even, odd = fft4(x[0::2], sign), fft4(x[1::2], sign)
    odd = [rotate(o, j, 8, sign) for j, o in enumerate(odd)]
    return [cadd(u, v) for u, v in zip(even, odd)] + [csub(u, v) for u, v in zip(even, odd)]


def fft32(load, store, mid, sign):
    for p0 in range(8):
        y = fft4([load(8 * p1 + p0) for p1 in range(4)], sign)
        for k0 in range(4):
            v = rotate(y[k0], p0 * k0, 32, sign)
            mid[0, k0 * 8 + p0] = v[0]
            mid[1, k0 * 8 + p0] = v[1]
    for k0 in range(4):
        y = fft8([(mid[0, k0 * 8 + p0], mid[1, k0 * 8 + p0]) for p0 in range(8)], sign)
        for k1 in range(8):
            store(k0 + 4 * k1, y[k1])


def code_times(code, z):
    odd = (code & 1) == 1
    a = jnp.where(odd, z[1], z[0])
    b = jnp.where(odd, z[0], z[1])
    return jnp.where((code == 1) | (code == 2), -a, a), jnp.where(code >= 2, -b, b)


def conj_code_times(code, z):
    odd = (code & 1) == 1
    a = jnp.where(odd, z[1], z[0])
    b = jnp.where(odd, z[0], z[1])
    return jnp.where(code >= 2, -a, a), jnp.where((code == 1) | (code == 2), -b, b)


def rows_forward(index, obj, code, left, tw, out, c0, c2, c1, c3, mid, xs):
    m = pl.program_id(0)
    shift = lax.rem(m + MASKS - index[0], MASKS)
    for s, c in enumerate((c0, c1, c2, c3)):

        @pl.when(shift == s)
        def _():
            c[...] = code[0]

    def load(p):
        cols = slice(LANES * p, LANES * p + LANES)
        return code_times(code[0, :, cols], (obj[0, :, cols], obj[1, :, cols]))

    def store(k, v):
        v = cmul(v, (tw[0, k : k + 1], tw[1, k : k + 1]))
        xs[OCT * k : OCT * k + OCT, :LANES] = v[0]
        xs[OCT * k : OCT * k + OCT, LANES:] = v[1]

    fft32(load, store, mid, -1)
    y = dot3((left[0], left[1]), split(xs[...]), NT)
    for ri in range(2):
        for h in range(2):
            out[pl.ds(ri * 8 + 2 * m + h, LANES, stride=16), :] = y[
                LANES * ri : LANES * ri + LANES, LANES * h : LANES * h + LANES
            ]


def columns(rec, inten, inner, block, tw, out, s):
    def turned(e, sign):
        row = slice(4 * LANES + e, 4 * LANES + e + 1)
        return tw[0, row, :], sign * tw[1, row, :]

    for m in range(MASKS):
        x = jnp.concatenate(
            [
                jnp.concatenate(
                    [rec[pl.ds(ri * 8 + 2 * m + h, LANES, stride=16), :] for h in range(2)], axis=1
                )
                for ri in range(2)
            ],
            axis=0,
        )
        y = dot3((inner[0], inner[1]), split(x), NN)
        rows = slice(LANES * m, LANES * m + LANES)
        t = (tw[0, rows], tw[1, rows])
        for h in range(2):
            cols = slice(LANES * h, LANES * h + LANES)
            v = cmul((y[:LANES, cols], y[LANES:, cols]), t)
            s[m, 0, h] = v[0]
            s[m, 1, h] = v[1]

    for h in range(2):
        def turn(i, _):
            rows = pl.ds(pl.multiple_of(i * OCT, OCT), OCT)
            y = fft4([(s[m, 0, h, rows, :], s[m, 1, h, rows, :]) for m in range(4)], -1)
            for e in range(4):
                v = cmul(y[e], turned(e, 1)) if e else y[e]
                s[e, 0, h, rows, :] = v[0]
                s[e, 1, h, rows, :] = v[1]
            return 0

        lax.fori_loop(0, LANES // OCT, turn, 0, unroll=True)

    for e in range(4):
        x = jnp.concatenate(
            [jnp.concatenate([s[e, 0, h], s[e, 1, h]], axis=1) for h in range(2)], axis=0
        )
        y = dot3(split(x), (block[0], block[1]), NN)
        wr, wi = y[:, :LANES], y[:, LANES:]
        weight = wr * wr + wi * wi - inten[e]
        v = jnp.concatenate([wr * weight, wi * weight], axis=1)
        y = dot3(split(v), (block[0], block[1]), NT)
        for h in range(2):
            rows = slice(LANES * h, LANES * h + LANES)
            s[e, 0, h] = y[rows, :LANES]
            s[e, 1, h] = y[rows, LANES:]

    for h in range(2):
        def turn_back(i, _):
            rows = pl.ds(pl.multiple_of(i * OCT, OCT), OCT)
            x = [(s[e, 0, h, rows, :], s[e, 1, h, rows, :]) for e in range(4)]
            y = fft4([cmul(v, turned(e, -1)) if e else v for e, v in enumerate(x)], 1)
            for m in range(4):
                near = pl.ds(pl.multiple_of(LANES * m + i * OCT, OCT), OCT)
                v = cmul(y[m], (tw[0, near, :], -tw[1, near, :]))
                s[m, 0, h, rows, :] = v[0]
                s[m, 1, h, rows, :] = v[1]
            return 0

        lax.fori_loop(0, LANES // OCT, turn_back, 0, unroll=True)

    for m in range(MASKS):
        x = jnp.concatenate(
            [jnp.concatenate([s[m, ri, 0], s[m, ri, 1]], axis=1) for ri in range(2)], axis=0
        )
        y = dot3((inner[0], inner[1]), split(x), TN)
        for ri in range(2):
            for h in range(2):
                out[pl.ds(m * 4 + ri * 2 + h, LANES, stride=16), :] = y[
                    LANES * ri : LANES * ri + LANES, LANES * h : LANES * h + LANES
                ]


def rows_back(index, rec, c0, c1, c2, c3, left, tw, out, out_re, out_im, mid, ys):
    for s, code in enumerate((c0, c1, c2, c3)):
        l = lax.rem(index[0] + MASKS - s, MASKS)
        x = jnp.concatenate(
            [
                jnp.concatenate(
                    [
                        rec[pl.ds(l * 4 + ri * 2 + h, LANES, stride=16), :].T
                        for ri in range(2)
                    ],
                    axis=1,
                )
                for h in range(2)
            ],
            axis=0,
        )
        ys[...] = dot3(split(x), (left[0], left[1]), NN)

        def load(k):
            rows = slice(OCT * k, OCT * k + OCT)
            return cmul((ys[rows, :LANES], ys[rows, LANES:]), (tw[0, k : k + 1], -tw[1, k : k + 1]))

        def store(p, v):
            cols = slice(LANES * p, LANES * p + LANES)
            v = conj_code_times(code[:, cols], v)
            for ri in range(2):
                if s == 0:
                    out[ri, :, cols] = v[ri]
                elif s < MASKS - 1:
                    out[ri, :, cols] += v[ri]
                else:
                    total = (out[ri, :, cols] + v[ri]) * (1.0 / MASKS)
                    out[ri, :, cols] = total
                    (out_re, out_im)[ri][:, cols] = total

        fft32(load, store, mid, 1)


def write_rows(masks, parts, obj, updated, direction, bufs, sems):
    copies = []
    for i, (mask, part) in enumerate(zip(masks, parts)):
        rows = pl.ds(pl.multiple_of(mask * OCT, OCT), OCT)
        for ri in range(2):
            value = part[ri][...]
            bufs[i, 0, ri] = obj[ri, rows, :] - step_size * value
            bufs[i, 1, ri] = value
        for j, out in enumerate((updated, direction)):
            copy = pltpu.make_async_copy(bufs.at[i, j], out.at[:, rows, :], sems.at[i, j])
            copy.start()
            copies.append(copy)
    for copy in copies:
        copy.wait()


def side_of(core):
    return 2 * lax.rem(core[0], 2) - 1


def finish_first(index, core, own_re, own_im, near_re, near_im, obj, updated, direction, bufs, sems):
    masks = [lax.rem(index[0] + MASKS + shift, MASKS) for shift in (0, side_of(core))]
    parts = ((own_re, own_im), (near_re, near_im))
    write_rows(masks, parts, obj, updated, direction, bufs, sems)


def finish_last(index, core, far_re, far_im, other, obj, _u, _d, updated, direction, bufs, sems):
    masks = [lax.rem(index[0] + MASKS + shift, MASKS) for shift in (-side_of(core), 2)]
    parts = ((other.at[0], other.at[1]), (far_re, far_im))
    write_rows(masks, parts, obj, updated, direction, bufs, sems)


VM = pl.BlockSpec(memory_space=pltpu.VMEM)
F32 = jnp.float32


def call(kernel, name, out_shape, n_in, scratch, flops, vmem=24, smem=()):
    specs = [VM] * n_in
    for i in smem:
        specs[i] = pl.BlockSpec(memory_space=pltpu.SMEM)
    outs = jax.tree.map(lambda _: VM, out_shape)
    return pl.pallas_call(
        kernel,
        name=name,
        out_shape=out_shape,
        in_specs=specs,
        out_specs=outs,
        scratch_shapes=scratch,
        compiler_params=pltpu.CompilerParams(vmem_limit_bytes=vmem << 20),
        cost_estimate=pl.CostEstimate(flops=flops, bytes_accessed=3 << 20, transcendentals=0),
    )


def body(object_field, phases, intensity):
    t = {k: jnp.asarray(v) for k, v in tables().items()}
    sds = jax.ShapeDtypeStruct
    index = lax.axis_index("mask").astype(jnp.int32).reshape(1)
    octet = lambda m: (0, m, 0)
    flat = lambda m: (0, 0)
    rows8 = sds((OCT, N), jnp.int32)
    sent, c0, c2, c1, c3 = pl.pallas_call(
        rows_forward,
        name="rows_forward",
        out_shape=(sds((2048, LANES), F32),) + (rows8,) * MASKS,
        grid=(MASKS,),
        in_specs=[
            pl.BlockSpec(memory_space=pltpu.SMEM),
            pl.BlockSpec((2, OCT, N), octet),
            pl.BlockSpec((1, OCT, N), octet),
            pl.BlockSpec((2, 256, 256), lambda m: (0, 0, 0)),
            pl.BlockSpec((2, SHORT, LANES), lambda m: (0, 0, 0)),
        ],
        out_specs=(pl.BlockSpec((2048, LANES), flat),) + (pl.BlockSpec((OCT, N), flat),) * MASKS,
        scratch_shapes=[
            pltpu.VMEM((2, SHORT, OCT, LANES), F32),
            pltpu.VMEM((256, 256), F32),
        ],
        compiler_params=pltpu.CompilerParams(vmem_limit_bytes=60 << 20),
        cost_estimate=pl.CostEstimate(flops=1 << 29, bytes_accessed=3 << 20, transcendentals=0),
    )(index, object_field, phases, t["left"], t["row_tw"])
    inten = intensity.reshape(2, 16, 8, 4, LANES).transpose(3, 0, 4, 1, 2).reshape(4, 256, LANES)
    up = [(i, (i + 1) % MASKS) for i in range(MASKS)]
    down = [((i + 1) % MASKS, i) for i in range(MASKS)]
    ring = [
        (m * LANES + r, (m + 1 - 2 * (r % 2)) % MASKS * LANES + r)
        for m in range(MASKS)
        for r in range(LANES)
    ]
    both = ("mask", "rows")
    order = [int(i) for i in exchange_order()]
    every = [m * LANES + i for i in order for m in range(MASKS)]
    exchange = functools.partial(lax.all_to_all, split_axis=0, concat_axis=0, tiled=True)
    rec = exchange(sent.reshape(LANES, 16, LANES), "rows", axis_index_groups=[order])
    g1 = lax.ppermute(c1, "mask", up)
    g2 = lax.ppermute(lax.ppermute(c2, both, ring), both, ring)
    g3 = lax.ppermute(c3, "mask", down)
    back = call(
        columns, "columns", sds((2048, LANES), F32), 5,
        [pltpu.VMEM((4, 2, 2, LANES, LANES), F32)], 3 << 29,
    )(rec.reshape(2048, LANES), inten, t["inner"], t["block"], t["col_tw"])
    back, g2, g1, g3 = lax.optimization_barrier((back, g2, g1, g3))
    rec = exchange(back.reshape(512, 4, LANES), ("mask", "rows"), axis_index_groups=[every])
    half = sds((OCT, N), F32)
    part, own_re, own_im = call(
        rows_back, "rows_back", (sds((2, OCT, N), F32), half, half), 8,
        [pltpu.VMEM((2, SHORT, OCT, LANES), F32), pltpu.VMEM((256, 256), F32)], 1 << 29, smem=(0,),
    )(index, rec.reshape(2048, LANES), c0, g1, g2, g3, t["left"], t["row_tw"])
    near_re = lax.ppermute(own_re, both, ring)
    near_im = lax.ppermute(own_im, both, ring)
    other = lax.ppermute(part, both, [(b, a) for a, b in ring])
    far_re = lax.ppermute(near_re, both, ring)
    far_im = lax.ppermute(near_im, both, ring)
    core = lax.axis_index("rows").astype(jnp.int32).reshape(1)
    whole = sds((2, SHORT, N), F32)
    scalars = [pl.BlockSpec(memory_space=pltpu.SMEM)] * 2
    anywhere = [pl.BlockSpec(memory_space=pl.ANY)] * 2
    scratch = [pltpu.VMEM((2, 2, 2, OCT, N), F32), pltpu.SemaphoreType.DMA((2, 2))]
    cost = pl.CostEstimate(flops=1 << 19, bytes_accessed=2 << 20, transcendentals=0)
    options = dict(
        out_shape=(whole, whole),
        out_specs=anywhere,
        scratch_shapes=scratch,
        compiler_params=pltpu.CompilerParams(vmem_limit_bytes=24 << 20),
        cost_estimate=cost,
    )
    first = pl.pallas_call(
        finish_first, name="finish_first", in_specs=scalars + [VM] * 5, **options
    )(index, core, own_re, own_im, near_re, near_im, object_field)
    return pl.pallas_call(
        finish_last,
        name="finish_last",
        in_specs=scalars + [VM] * 4 + anywhere,
        input_output_aliases={6: 0, 7: 1},
        **options,
    )(index, core, far_re, far_im, other, object_field, *first)


def solution(mesh):
    return jax.shard_map(
        body,
        mesh=mesh,
        in_specs=(P(None, "rows", None), P("mask", "rows", None), P("mask", "rows", None)),
        out_specs=(P(None, "rows", None), P(None, "rows", None)),
        check_vma=False,
    )
```

```python
import functools
import math

import jax
import jax.numpy as jnp
import ml_dtypes
import numpy as np
from jax import lax
from jax.experimental import pallas as pl
from jax.experimental.pallas import tpu as pltpu
from jax.sharding import PartitionSpec as P

N = 4096
LANES = 128
SHORT = 32
OCT = 8
MASKS = 4
step_size = 0.2


def _split(table):
    high = table.astype(np.float32).astype(ml_dtypes.bfloat16)
    low = (table - high.astype(np.float64)).astype(np.float32).astype(ml_dtypes.bfloat16)
    return np.stack([high, low])


def exchange_order():
    index = np.arange(LANES).reshape(2, 4, 8, 2)
    return index.transpose(0, 1, 3, 2).reshape(LANES)


@functools.lru_cache(maxsize=None)
def tables():
    i128 = np.arange(LANES)
    w = np.exp(-2j * math.pi * (np.outer(i128, i128) % LANES) / LANES) / 64.0
    w = w[exchange_order()]
    left = np.block([[w.real, -w.imag], [w.imag, w.real]])
    inner = np.block([[w.real.T, -w.imag.T], [w.imag.T, w.real.T]])
    t = np.exp(-2j * math.pi * np.outer(np.arange(SHORT), i128) / N)
    row_tw = np.stack([t.real, t.imag]).astype(np.float32)
    rho = i128 % OCT
    row = np.arange(MASKS)[:, None] * OCT + rho[None, :]
    t = np.exp(-2j * math.pi * (i128[None, :, None] * row[:, None, :]) / N)
    col_tw = np.stack([t.real, t.imag])
    r8 = np.arange(OCT)
    big = np.kron(np.eye(16), np.exp(-2j * math.pi * np.outer(r8, r8) / 8))
    block = np.block([[big.real, big.imag], [-big.imag, big.real]])
    t = np.exp(-2j * math.pi * np.outer(np.arange(OCT), rho) / SHORT)
    col_tw = np.concatenate([col_tw.reshape(2, 4 * LANES, LANES), np.stack([t.real, t.imag])], axis=1)
    return dict(left=_split(left), inner=_split(inner), block=_split(block), row_tw=row_tw, col_tw=col_tw.astype(np.float32))


def split(x):
    high = x.astype(jnp.bfloat16)
    return high, (x - high.astype(jnp.float32)).astype(jnp.bfloat16)


def dot3(a, b, dims):
    dot = functools.partial(
        lax.dot_general, dimension_numbers=(dims, ((), ())), preferred_element_type=jnp.float32
    )
    return dot(a[0], b[0]) + (dot(a[0], b[1]) + dot(a[1], b[0]))


NN = ((1,), (0,))
NT = ((1,), (1,))
TN = ((0,), (0,))


def cmul(a, b):
    return a[0] * b[0] - a[1] * b[1], a[0] * b[1] + a[1] * b[0]


def cadd(a, b):
    return a[0] + b[0], a[1] + b[1]


def csub(a, b):
    return a[0] - b[0], a[1] - b[1]


def times_i(a, sign):
    return (-a[1], a[0]) if sign > 0 else (a[1], -a[0])


def rotate(a, turns, length, sign):
    turns = turns % length
    if turns == 0:
        return a
    eighths = turns * 8 % (length * 8) / length
    if eighths == 4:
        return -a[0], -a[1]
    if eighths == 2:
        return times_i(a, sign)
    if eighths == 6:
        return times_i(a, -sign)
    angle = sign * 2 * math.pi * turns / length
    c, s = float(np.float32(math.cos(angle))), float(np.float32(math.sin(angle)))
    if eighths in (1, 3, 5, 7):
        h = float(np.float32(math.sqrt(0.5)))
        cs, ss = (1 if c > 0 else -1), (1 if s > 0 else -1)
        re = (a[0] if cs > 0 else -a[0]) - (a[1] if ss > 0 else -a[1])
        im = (a[1] if cs > 0 else -a[1]) + (a[0] if ss > 0 else -a[0])
        return re * h, im * h
    return a[0] * c - a[1] * s, a[0] * s + a[1] * c


def fft4(x, sign):
    a, b = cadd(x[0], x[2]), csub(x[0], x[2])
    c, d = cadd(x[1], x[3]), times_i(csub(x[1], x[3]), sign)
    return [cadd(a, c), cadd(b, d), csub(a, c), csub(b, d)]


def fft8(x, sign):
    even, odd = fft4(x[0::2], sign), fft4(x[1::2], sign)
    odd = [rotate(o, j, 8, sign) for j, o in enumerate(odd)]
    return [cadd(u, v) for u, v in zip(even, odd)] + [csub(u, v) for u, v in zip(even, odd)]


def fft32(load, store, mid, sign):
    for p0 in range(8):
        y = fft4([load(8 * p1 + p0) for p1 in range(4)], sign)
        for k0 in range(4):
            v = rotate(y[k0], p0 * k0, 32, sign)
            mid[0, k0 * 8 + p0] = v[0]
            mid[1, k0 * 8 + p0] = v[1]
    for k0 in range(4):
        y = fft8([(mid[0, k0 * 8 + p0], mid[1, k0 * 8 + p0]) for p0 in range(8)], sign)
        for k1 in range(8):
            store(k0 + 4 * k1, y[k1])


def code_times(code, z):
    odd = (code & 1) == 1
    a = jnp.where(odd, z[1], z[0])
    b = jnp.where(odd, z[0], z[1])
    return jnp.where((code == 1) | (code == 2), -a, a), jnp.where(code >= 2, -b, b)


def conj_code_times(code, z):
    odd = (code & 1) == 1
    a = jnp.where(odd, z[1], z[0])
    b = jnp.where(odd, z[0], z[1])
    return jnp.where(code >= 2, -a, a), jnp.where((code == 1) | (code == 2), -b, b)


def rows_forward(index, obj, code, left, tw, out, c2, c1, c3, mid, xs):
    m = pl.program_id(0)
    shift = lax.rem(m + MASKS - index[0], MASKS)
    for s, c in enumerate((c1, c2, c3)):

        @pl.when(shift == s + 1)
        def _():
            c[...] = code[0]

    def load(p):
        cols = slice(LANES * p, LANES * p + LANES)
        return code_times(code[0, :, cols], (obj[0, :, cols], obj[1, :, cols]))

    def store(k, v):
        v = cmul(v, (tw[0, k : k + 1], tw[1, k : k + 1]))
        xs[OCT * k : OCT * k + OCT, :LANES] = v[0]
        xs[OCT * k : OCT * k + OCT, LANES:] = v[1]

    fft32(load, store, mid, -1)
    y = dot3((left[0], left[1]), split(xs[...]), NT)
    for ri in range(2):
        for h in range(2):
            out[pl.ds(ri * 8 + 2 * m + h, LANES, stride=16), :] = y[
                LANES * ri : LANES * ri + LANES, LANES * h : LANES * h + LANES
            ]


def columns(rec, inten, inner, block, tw, out, s):
    def turned(e, sign):
        row = slice(4 * LANES + e, 4 * LANES + e + 1)
        return tw[0, row, :], sign * tw[1, row, :]

    for m in range(MASKS):
        x = jnp.concatenate(
            [
                jnp.concatenate(
                    [rec[pl.ds(ri * 8 + 2 * m + h, LANES, stride=16), :] for h in range(2)], axis=1
                )
                for ri in range(2)
            ],
            axis=0,
        )
        y = dot3((inner[0], inner[1]), split(x), NN)
        rows = slice(LANES * m, LANES * m + LANES)
        t = (tw[0, rows], tw[1, rows])
        for h in range(2):
            cols = slice(LANES * h, LANES * h + LANES)
            v = cmul((y[:LANES, cols], y[LANES:, cols]), t)
            s[m, 0, h] = v[0]
            s[m, 1, h] = v[1]

    for h in range(2):
        def turn(i, _):
            rows = pl.ds(pl.multiple_of(i * OCT, OCT), OCT)
            y = fft4([(s[m, 0, h, rows, :], s[m, 1, h, rows, :]) for m in range(4)], -1)
            for e in range(4):
                v = cmul(y[e], turned(e, 1)) if e else y[e]
                s[e, 0, h, rows, :] = v[0]
                s[e, 1, h, rows, :] = v[1]
            return 0

        lax.fori_loop(0, LANES // OCT, turn, 0, unroll=True)

    for e in range(4):
        x = jnp.concatenate(
            [jnp.concatenate([s[e, 0, h], s[e, 1, h]], axis=1) for h in range(2)], axis=0
        )
        y = dot3(split(x), (block[0], block[1]), NN)
        wr, wi = y[:, :LANES], y[:, LANES:]
        weight = wr * wr + wi * wi - inten[e]
        v = jnp.concatenate([wr * weight, wi * weight], axis=1)
        y = dot3(split(v), (block[0], block[1]), NT)
        for h in range(2):
            rows = slice(LANES * h, LANES * h + LANES)
            s[e, 0, h] = y[rows, :LANES]
            s[e, 1, h] = y[rows, LANES:]

    for h in range(2):
        def turn_back(i, _):
            rows = pl.ds(pl.multiple_of(i * OCT, OCT), OCT)
            x = [(s[e, 0, h, rows, :], s[e, 1, h, rows, :]) for e in range(4)]
            y = fft4([cmul(v, turned(e, -1)) if e else v for e, v in enumerate(x)], 1)
            for m in range(4):
                near = pl.ds(pl.multiple_of(LANES * m + i * OCT, OCT), OCT)
                v = cmul(y[m], (tw[0, near, :], -tw[1, near, :]))
                s[m, 0, h, rows, :] = v[0]
                s[m, 1, h, rows, :] = v[1]
            return 0

        lax.fori_loop(0, LANES // OCT, turn_back, 0, unroll=True)

    for m in range(MASKS):
        x = jnp.concatenate(
            [jnp.concatenate([s[m, ri, 0], s[m, ri, 1]], axis=1) for ri in range(2)], axis=0
        )
        y = dot3((inner[0], inner[1]), split(x), TN)
        for ri in range(2):
            for h in range(2):
                out[pl.ds(m * 4 + ri * 2 + h, LANES, stride=16), :] = y[
                    LANES * ri : LANES * ri + LANES, LANES * h : LANES * h + LANES
                ]


def rows_back(index, rec, c0, c1, c2, c3, left, tw, out, out_re, out_im, mid, ys):
    for s, code in enumerate((c0, c1, c2, c3)):
        l = lax.rem(index[0] + MASKS - s, MASKS)
        x = jnp.concatenate(
            [
                jnp.concatenate(
                    [
                        rec[pl.ds(l * 4 + ri * 2 + h, LANES, stride=16), :].T
                        for ri in range(2)
                    ],
                    axis=1,
                )
                for h in range(2)
            ],
            axis=0,
        )
        ys[...] = dot3(split(x), (left[0], left[1]), NN)

        def load(k):
            rows = slice(OCT * k, OCT * k + OCT)
            return cmul((ys[rows, :LANES], ys[rows, LANES:]), (tw[0, k : k + 1], -tw[1, k : k + 1]))

        def store(p, v):
            cols = slice(LANES * p, LANES * p + LANES)
            v = conj_code_times(code[:, cols], v)
            for ri in range(2):
                if s == 0:
                    out[ri, :, cols] = v[ri]
                elif s < MASKS - 1:
                    out[ri, :, cols] += v[ri]
                else:
                    total = (out[ri, :, cols] + v[ri]) * (1.0 / MASKS)
                    out[ri, :, cols] = total
                    (out_re, out_im)[ri][:, cols] = total

        fft32(load, store, mid, 1)


def write_rows(masks, parts, obj, updated, direction, bufs, sems):
    copies = []
    for i, (mask, part) in enumerate(zip(masks, parts)):
        rows = pl.ds(pl.multiple_of(mask * OCT, OCT), OCT)
        for ri in range(2):
            value = part[ri][...]
            bufs[i, 0, ri] = obj[ri, rows, :] - step_size * value
            bufs[i, 1, ri] = value
        for j, out in enumerate((updated, direction)):
            copy = pltpu.make_async_copy(bufs.at[i, j], out.at[:, rows, :], sems.at[i, j])
            copy.start()
            copies.append(copy)
    for copy in copies:
        copy.wait()


def side_of(core):
    return 2 * lax.rem(core[0], 2) - 1


def finish_first(index, core, own_re, own_im, near_re, near_im, obj, updated, direction, bufs, sems):
    masks = [lax.rem(index[0] + MASKS + shift, MASKS) for shift in (0, side_of(core))]
    parts = ((own_re, own_im), (near_re, near_im))
    write_rows(masks, parts, obj, updated, direction, bufs, sems)


def finish_last(index, core, far_re, far_im, other, obj, _u, _d, updated, direction, bufs, sems):
    masks = [lax.rem(index[0] + MASKS + shift, MASKS) for shift in (-side_of(core), 2)]
    parts = ((other.at[0], other.at[1]), (far_re, far_im))
    write_rows(masks, parts, obj, updated, direction, bufs, sems)


VM = pl.BlockSpec(memory_space=pltpu.VMEM)
F32 = jnp.float32


def call(kernel, name, out_shape, n_in, scratch, flops, vmem=24, smem=()):
    specs = [VM] * n_in
    for i in smem:
        specs[i] = pl.BlockSpec(memory_space=pltpu.SMEM)
    outs = jax.tree.map(lambda _: VM, out_shape)
    return pl.pallas_call(
        kernel,
        name=name,
        out_shape=out_shape,
        in_specs=specs,
        out_specs=outs,
        scratch_shapes=scratch,
        compiler_params=pltpu.CompilerParams(vmem_limit_bytes=vmem << 20),
        cost_estimate=pl.CostEstimate(flops=flops, bytes_accessed=3 << 20, transcendentals=0),
    )


def body(object_field, phases, intensity):
    t = {k: jnp.asarray(v) for k, v in tables().items()}
    sds = jax.ShapeDtypeStruct
    index = lax.axis_index("mask").astype(jnp.int32).reshape(1)
    octet = lambda m: (0, m, 0)
    flat = lambda m: (0, 0)
    rows8 = sds((OCT, N), jnp.int32)
    sent, c2, c1, c3 = pl.pallas_call(
        rows_forward,
        name="rows_forward",
        out_shape=(sds((2048, LANES), F32),) + (rows8,) * 3,
        grid=(MASKS,),
        in_specs=[
            pl.BlockSpec(memory_space=pltpu.SMEM),
            pl.BlockSpec((2, OCT, N), octet),
            pl.BlockSpec((1, OCT, N), octet),
            pl.BlockSpec((2, 256, 256), lambda m: (0, 0, 0)),
            pl.BlockSpec((2, SHORT, LANES), lambda m: (0, 0, 0)),
        ],
        out_specs=(pl.BlockSpec((2048, LANES), flat),) + (pl.BlockSpec((OCT, N), flat),) * 3,
        scratch_shapes=[
            pltpu.VMEM((2, SHORT, OCT, LANES), F32),
            pltpu.VMEM((256, 256), F32),
        ],
        compiler_params=pltpu.CompilerParams(vmem_limit_bytes=60 << 20),
        cost_estimate=pl.CostEstimate(flops=1 << 29, bytes_accessed=3 << 20, transcendentals=0),
    )(index, object_field, phases, t["left"], t["row_tw"])
    inten = intensity.reshape(2, 16, 8, 4, LANES).transpose(3, 0, 4, 1, 2).reshape(4, 256, LANES)
    up = [(i, (i + 1) % MASKS) for i in range(MASKS)]
    down = [((i + 1) % MASKS, i) for i in range(MASKS)]
    ring = [
        (m * LANES + r, (m + 1 - 2 * (r % 2)) % MASKS * LANES + r)
        for m in range(MASKS)
        for r in range(LANES)
    ]
    both = ("mask", "rows")
    order = [int(i) for i in exchange_order()]
    every = [m * LANES + i for i in order for m in range(MASKS)]
    exchange = functools.partial(lax.all_to_all, split_axis=0, concat_axis=0, tiled=True)
    rec = exchange(sent.reshape(LANES, 16, LANES), "rows", axis_index_groups=[order])
    g1 = lax.ppermute(c1, "mask", up)
    g2 = lax.ppermute(lax.ppermute(c2, both, ring), both, ring)
    g3 = lax.ppermute(c3, "mask", down)
    c0 = lax.dynamic_slice_in_dim(phases[0], index[0] * OCT, OCT)
    back = call(
        columns, "columns", sds((2048, LANES), F32), 5,
        [pltpu.VMEM((4, 2, 2, LANES, LANES), F32)], 3 << 29,
    )(rec.reshape(2048, LANES), inten, t["inner"], t["block"], t["col_tw"])
    back, g2, g1, g3, c0 = lax.optimization_barrier((back, g2, g1, g3, c0))
    rec = exchange(back.reshape(512, 4, LANES), ("mask", "rows"), axis_index_groups=[every])
    half = sds((OCT, N), F32)
    part, own_re, own_im = call(
        rows_back, "rows_back", (sds((2, OCT, N), F32), half, half), 8,
        [pltpu.VMEM((2, SHORT, OCT, LANES), F32), pltpu.VMEM((256, 256), F32)], 1 << 29, smem=(0,),
    )(index, rec.reshape(2048, LANES), c0, g1, g2, g3, t["left"], t["row_tw"])
    near_re = lax.ppermute(own_re, both, ring)
    near_im = lax.ppermute(own_im, both, ring)
    other = lax.ppermute(part, both, [(b, a) for a, b in ring])
    far_re = lax.ppermute(near_re, both, ring)
    far_im = lax.ppermute(near_im, both, ring)
    core = lax.axis_index("rows").astype(jnp.int32).reshape(1)
    whole = sds((2, SHORT, N), F32)
    scalars = [pl.BlockSpec(memory_space=pltpu.SMEM)] * 2
    anywhere = [pl.BlockSpec(memory_space=pl.ANY)] * 2
    scratch = [pltpu.VMEM((2, 2, 2, OCT, N), F32), pltpu.SemaphoreType.DMA((2, 2))]
    cost = pl.CostEstimate(flops=1 << 19, bytes_accessed=2 << 20, transcendentals=0)
    options = dict(
        out_shape=(whole, whole),
        out_specs=anywhere,
        scratch_shapes=scratch,
        compiler_params=pltpu.CompilerParams(vmem_limit_bytes=24 << 20),
        cost_estimate=cost,
    )
    first = pl.pallas_call(
        finish_first, name="finish_first", in_specs=scalars + [VM] * 5, **options
    )(index, core, own_re, own_im, near_re, near_im, object_field)
    return pl.pallas_call(
        finish_last,
        name="finish_last",
        in_specs=scalars + [VM] * 4 + anywhere,
        input_output_aliases={6: 0, 7: 1},
        **options,
    )(index, core, far_re, far_im, other, object_field, *first)


def solution(mesh):
    return jax.shard_map(
        body,
        mesh=mesh,
        in_specs=(P(None, "rows", None), P("mask", "rows", None), P("mask", "rows", None)),
        out_specs=(P(None, "rows", None), P(None, "rows", None)),
        check_vma=False,
    )
```
